32 devices in a mesh: row: 4 (over z), col: 8 (over y, x, core).
Axes of the slice: x: 2, y: 2, z: 4, core: 2. Of those that a mesh axis runs over, the one named last changes fastest.
Arguments:
- a_trail: float32 [16384, 16384], P('row', 'col'), may hold values from -60 to 60, as said below
- a_panel: float32 [16384, 256], P(('row', 'col')), may hold values from -6 to 6
- l_panel: float32 [16384, 256], P(('row', 'col')), may hold values from -0.5 to 0.5
- a_diag: float32 [256, 256], replicated, may hold values from -60 to 60, as said below
- l_inverse: float32 [256, 256], replicated, may hold values from -4 to 4, as said below
Outputs:
- trail_out: float32 [16384, 16384], P('row', 'col')
- panel_out: float32 [16384, 256], P(('row', 'col'))
The draws below stay inside these ranges and needn't reach their ends.
Inputs may be any that keep to these rules, and one draw needn't show every extreme that they name: `a_trail`: symmetric. `a_diag`: symmetric. `l_inverse`: lower triangular with a positive diagonal.
All inputs are finite; a program needn't handle non-finite values.
Results may differ from the reference program's by a relative error of at most 0.0003.
Values sent between devices are 32-bit elements; how exact they have to be, the bound alone decides.
A program may use at most 192 MiB of HBM per device.

```python
import jax
import jax.numpy as jnp
from jax import lax

M = 16384
NB = 256
NS_STEPS = 8


def draw_a_trail(key, part):
    base = jax.random.normal(jax.random.fold_in(key, 11), (M, M), jnp.float32)
    sym = (base + base.T) * 0.7071067811865476
    return jnp.clip(sym, -60.0, 60.0)


def draw_a_diag(key, part):
    base = jax.random.normal(jax.random.fold_in(key, 21), (NB, NB), jnp.float32)
    sym = (base + base.T) * 0.7071067811865476
    return jnp.clip(sym, -60.0, 60.0)


def draw_l_inverse(key, part):
    lower = jnp.tril(jnp.ones((NB, NB), jnp.float32), -1)
    spread = 0.5 * jnp.clip(jax.random.normal(jax.random.fold_in(key, 31), (NB, NB), jnp.float32), -6.0, 6.0)
    diag_vals = jax.random.uniform(jax.random.fold_in(key, 32), (NB,), jnp.float32, 0.8, 1.2)
    off_part = spread * lower / jnp.sqrt(jnp.float32(NB))
    return off_part + jnp.diag(diag_vals)


def block_levels(rng, extent, split, least, high):
    level = 1.0
    for axis_at, shards_of in split:
        heights = jax.random.uniform(jax.random.fold_in(jax.random.fold_in(rng, 6), axis_at), (shards_of,), jnp.float32, least / len(split), high / len(split))
        level = level * jnp.repeat(jnp.exp(heights), extent[axis_at] // shards_of).reshape((-1,) + (1,) * (len(extent) - 1 - axis_at))
    return level


def gaussian(rng, extent, width, most, pieces=(), kind=jnp.bfloat16):
    factor_of = block_levels(rng, extent, pieces, -0.22, 0.18) if pieces else 1.0
    result = jax.random.normal(rng, extent, jnp.float32) * width * factor_of
    return jnp.minimum(jnp.maximum(result, -most), most).astype(kind)


def setup_inputs(seed: int = 0) -> dict:
    splits = jax.random.split(jax.random.key(seed), 6)
    a_trail = draw_a_trail(jax.random.fold_in(splits[5], 71), 0)
    a_panel = gaussian(splits[1], (M, NB), 1.0, 6.0, ((0, 32),), jnp.float32)
    l_panel = gaussian(splits[2], (M, NB), 0.0625, 0.5, ((0, 32),), jnp.float32)
    a_diag = draw_a_diag(jax.random.fold_in(splits[5], 71), 0)
    l_inverse = draw_l_inverse(jax.random.fold_in(splits[5], 71), 0)
    return dict(a_trail=a_trail, a_panel=a_panel, l_panel=l_panel, a_diag=a_diag, l_inverse=l_inverse)


def product(left, right):
    return jnp.dot(left.astype(jnp.float32), right.astype(jnp.float32), precision=lax.Precision.HIGHEST, preferred_element_type=jnp.float32)

def newton_inverse(matrix):
    identity = jnp.eye(matrix.shape[0], dtype=jnp.float32)
    approx = identity
    for repeat in range(NS_STEPS):
        approx = product(approx, 2.0 * identity - product(matrix, approx))
    return approx

def right_solve(factor, values):
    return lax.linalg.triangular_solve(factor, values, left_side=False, lower=True, transpose_a=True)

def reference(a_trail, a_panel, l_panel, a_diag, l_inverse):
    a11_new = product(product(l_inverse, a_diag), l_inverse.T)
    solved = product(a_panel, l_inverse.T)
    half_term = 0.5 * product(l_panel, a11_new)
    first_y = solved - half_term
    panel_out = first_y - half_term
    updated = a_trail - (product(first_y, l_panel.T) + product(l_panel, first_y.T))
    all_rows = jnp.arange(M, dtype=jnp.int32)
    keep_mask = (all_rows >= NB)[:, None]
    next_panel = jnp.where(keep_mask, updated[:, :NB], 0.0)
    picker = (all_rows[:, None] - NB == jnp.arange(NB, dtype=jnp.int32)[None, :]).astype(jnp.float32)
    gram = product(next_panel.T, next_panel)
    top_block = next_panel[NB:2 * NB]
    factor = jnp.linalg.cholesky(gram)
    q_rows = right_solve(factor, next_panel)
    q_top = right_solve(factor, top_block)
    identity = jnp.eye(NB, dtype=jnp.float32)
    g_inverse = newton_inverse(identity + q_top).T
    y_full = q_rows + picker
    x_mat = product(product(updated, y_full), g_inverse)
    m_core = product(g_inverse.T, product(y_full.T, x_mat))
    z_mat = x_mat - 0.5 * product(y_full, m_core)
    trail_out = updated - (product(z_mat, y_full.T) + product(y_full, z_mat.T))
    return (trail_out, panel_out)
```

```python
import functools

import jax
import jax.numpy as jnp
from jax import lax
from jax.experimental import pallas as pl
from jax.experimental.layout import Layout, with_layout_constraint
from jax.experimental.pallas import tpu as pltpu
from jax.sharding import PartitionSpec as P

NS_STEPS = 8
BOTH = ("row", "col")
MESH_ID = pl.DeviceIdType.MESH


def product(left, right):
    return jnp.dot(left, right, precision=lax.Precision.HIGHEST, preferred_element_type=jnp.float32)


def large_product(left, right):
    return jnp.dot(left, right, precision=lax.Precision.HIGH, preferred_element_type=jnp.float32)


def exact(left, right, dims=(((1,), (0,)), ((), ()))):
    return lax.dot_general(left, right, dims, precision=lax.Precision.HIGHEST, preferred_element_type=jnp.float32)


def three(x):
    high = x.astype(jnp.bfloat16).astype(jnp.float32)
    rest = x - high
    mid = rest.astype(jnp.bfloat16).astype(jnp.float32)
    return high, mid, rest - mid


def sub_block(V, lanes_at, n, W):
    row = lax.broadcasted_iota(jnp.int32, (8, 128), 0)
    shifted = pltpu.roll(V[:, :n], n - lanes_at, 1)[:, :128]
    cols = [jnp.broadcast_to(shifted[:, j:j+1], (8, 128)) for j in range(8)]
    vs = [V[:, 128*t:128*(t+1)] for t in range(W//128)]
    for j in range(8):
        r = lax.rsqrt(cols[j][j:j+1, :])
        r = r * (1.5 - 0.5 * cols[j][j:j+1, :] * r * r)
        lj = jnp.where(row > j, cols[j] * r, 0.0)
        sc = jnp.where(row == j, jnp.broadcast_to(r, (8,128)), 1.0)
        for k in range(j+1, 8):
            cols[k] = cols[k] - lj * lj[k:k+1, :]
        for t in range(len(vs)):
            top = vs[t][j:j+1, :] * r
            vs[t] = jnp.where(row == j, jnp.broadcast_to(top, (8,128)), vs[t] - lj * top)
    return jnp.concatenate(vs, axis=1)


def inverse_factor(S, n):
    W = 2*n
    lane = lax.broadcasted_iota(jnp.int32, (8, n), 1)

    def body(b, carry):
        k0 = pl.multiple_of(b*8, 8)
        V = sub_block(S[pl.ds(k0, 8), :], k0, n, W)
        S[pl.ds(k0, 8), :] = V
        U = jnp.where(lane >= k0 + 8, V[:, :n], 0.0)
        h, m, l = three(U)
        hr, mr, lr = three(V)
        lhs = jnp.concatenate([h, h, m, h, m, l], axis=0).astype(jnp.bfloat16)
        rhs = jnp.concatenate([hr, mr, hr, lr, mr, hr], axis=0).astype(jnp.bfloat16)
        S[...] -= lax.dot_general(lhs, rhs, (((0,), (0,)), ((), ())), preferred_element_type=jnp.float32)
        return carry

    lax.fori_loop(0, n//8, body, 0)


def unit(n):
    return (
        lax.broadcasted_iota(jnp.int32, (n, n), 0) == lax.broadcasted_iota(jnp.int32, (n, n), 1)
    ).astype(jnp.float32)


def newton_product(q_top):
    rem = -q_top
    approx = unit(q_top.shape[0]) + rem
    for _ in range(NS_STEPS - 1):
        rem = exact(rem, rem)
        approx = approx + exact(approx, rem)
    return approx


def factor_kernel(g_ref, top_ref, x_ref, inv_ref, work):
    n = g_ref.shape[0]
    work[:, :n] = g_ref[...]
    work[:, n:] = unit(n)
    inverse_factor(work, n)
    inverse = work[:, n:]
    x_ref[...] = inverse
    inv_ref[...] = newton_product(exact(top_ref[...], inverse, (((1,), (1,)), ((), ()))))


def factor_call(gram, top):
    n = gram.shape[0]
    shape = jax.ShapeDtypeStruct((n, n), jnp.float32)
    return pl.pallas_call(
        factor_kernel, out_shape=(shape, shape), scratch_shapes=[pltpu.VMEM((n, 2 * n), jnp.float32)]
    )(gram, top)


def greet_all(rows, cols):
    count = rows * cols
    me = lax.axis_index("row") * cols + lax.axis_index("col")
    barrier = pltpu.get_barrier_semaphore()

    def greet(step, carry):
        at = lax.rem(me + step, count)
        pl.semaphore_signal(
            barrier, inc=1, device_id=(at // cols, lax.rem(at, cols)), device_id_type=MESH_ID
        )
        return carry

    lax.fori_loop(1, count, greet, 0)
    pl.semaphore_wait(barrier, count - 1)


def sum_steps(rows, cols, x_ref, o_ref, recv, red, send_a, recv_a, send_b, recv_b, held):
    count = rows * cols
    me = lax.axis_index("row") * cols + lax.axis_index("col")

    def peer(step):
        at = lax.rem(me + step, count)
        return at, (at // cols, lax.rem(at, cols))

    def owner(at):
        return (at * x_ref.shape[1]) // held

    def scatter(step):
        at, device = peer(step)
        return pltpu.make_async_remote_copy(
            src_ref=x_ref.at[at], dst_ref=recv.at[step], send_sem=send_a.at[step],
            recv_sem=recv_a.at[step], device_id=device, device_id_type=MESH_ID,
        )

    def gather(step):
        device = peer(step)[1]
        return pltpu.make_async_remote_copy(
            src_ref=red, dst_ref=o_ref.at[me], send_sem=send_b.at[step],
            recv_sem=recv_b.at[step], device_id=device, device_id_type=MESH_ID,
        )

    def loop(action):
        def body(step, carry):
            action(step)
            return carry

        lax.fori_loop(1, count, body, 0)

    def sends(step, action):
        if held is None:
            action()
        else:
            pl.when(owner(peer(step)[0]) == me)(action)

    def first():
        loop(lambda step: sends(step, lambda: scatter(step).start()))

    def second():
        if held is None:
            def add(step, total):
                scatter(step).wait_recv()
                return total + recv[step]

            total = lax.fori_loop(1, count, add, x_ref[me])
            red[...] = total
            o_ref[me] = total
        else:
            source = owner(me)

            @pl.when(source == me)
            def _():
                red[...] = x_ref[me]
                o_ref[me] = x_ref[me]

            @pl.when(source != me)
            def _():
                step = lax.rem(me + count - source, count)
                scatter(step).wait_recv()
                red[...] = recv[step]
                o_ref[me] = recv[step]
        loop(lambda step: gather(step).start())

    def third():
        def finish(step):
            gather(step).wait_recv()
            sends(step, lambda: scatter(step).wait_send())
            gather(step).wait_send()

        loop(finish)

    return first, second, third


def sum_scratch(count, piece, width):
    return [
        pltpu.VMEM((count, piece, width), jnp.float32),
        pltpu.VMEM((piece, width), jnp.float32),
        pltpu.SemaphoreType.DMA((count,)),
        pltpu.SemaphoreType.DMA((count,)),
        pltpu.SemaphoreType.DMA((count,)),
        pltpu.SemaphoreType.DMA((count,)),
    ]


def sum_kernel(rows, cols, *refs):
    first, second, third = sum_steps(rows, cols, *refs, None)
    greet_all(rows, cols)
    first()
    second()
    third()


def first_kernel(rows, cols, held, x_ref, a_ref, o_ref, a_first, recv, red, send_a, recv_a,
                 send_b, recv_b, send_p, recv_p, own_sem):
    i = lax.axis_index("row")
    c = lax.axis_index("col")
    height, width = a_first.shape
    first, second, third = sum_steps(
        rows, cols, x_ref, o_ref, recv, red, send_a, recv_a, send_b, recv_b, held
    )

    def piece(to):
        return pltpu.make_async_remote_copy(
            src_ref=a_ref.at[pl.ds(to * height, height), pl.ds(0, width)], dst_ref=a_first,
            send_sem=send_p.at[to], recv_sem=recv_p.at[0], device_id=(i, to),
            device_id_type=MESH_ID,
        )

    own = pltpu.make_async_copy(
        a_ref.at[pl.ds(0, height), pl.ds(0, width)], a_first, own_sem.at[0]
    )
    greet_all(rows, cols)
    first()

    @pl.when(c == 0)
    def _():
        own.start()
        for to in range(1, cols):
            piece(to).start()

    second()
    third()

    @pl.when(c == 0)
    def _():
        own.wait()
        for to in range(1, cols):
            piece(to).wait_send()

    @pl.when(c != 0)
    def _():
        piece(1).wait_recv()


def sum_all(rows, cols, value, ident):
    count = rows * cols
    height, width = value.shape
    piece = height // count
    spec = pl.BlockSpec(memory_space=pltpu.VMEM)
    out = pl.pallas_call(
        functools.partial(sum_kernel, rows, cols),
        out_shape=jax.ShapeDtypeStruct((count, piece, width), jnp.float32),
        in_specs=[spec],
        out_specs=spec,
        scratch_shapes=sum_scratch(count, piece, width),
        compiler_params=pltpu.CompilerParams(collective_id=ident, has_side_effects=True),
    )(value.reshape(count, piece, width))
    return out.reshape(height, width)


def first_exchange(rows, cols, value, held, a_trail, height, block_width, ident):
    count = rows * cols
    tall, width = value.shape
    piece = tall // count
    spec = pl.BlockSpec(memory_space=pltpu.VMEM)
    anywhere = pl.BlockSpec(memory_space=pl.ANY)
    out, a_first = pl.pallas_call(
        functools.partial(first_kernel, rows, cols, held),
        out_shape=(
            jax.ShapeDtypeStruct((count, piece, width), jnp.float32),
            jax.ShapeDtypeStruct((height, block_width), jnp.float32),
        ),
        in_specs=[spec, anywhere],
        out_specs=(spec, spec),
        scratch_shapes=sum_scratch(count, piece, width) + [
            pltpu.SemaphoreType.DMA((cols,)),
            pltpu.SemaphoreType.DMA((1,)),
            pltpu.SemaphoreType.DMA((1,)),
        ],
        compiler_params=pltpu.CompilerParams(collective_id=ident, has_side_effects=True),
    )(value.reshape(count, piece, width), a_trail)
    return out.reshape(tall, width), a_first


def gather_kernel(rows, cols, p_ref, x_ref, v_ref, o_ref, x_rows, v_rows, x_cols, recv, red,
                  send_a, recv_a, send_b, recv_b, col_send, col_recv, row_send, row_recv,
                  twin_send, twin_recv, own_sem):
    chips = cols // 2
    i = lax.axis_index("row")
    c = lax.axis_index("col")
    me = i * cols + c
    core = lax.rem(c, 2)
    twin = c + 1 - 2 * core
    first, second, third = sum_steps(
        rows, cols, p_ref, o_ref, recv, red, send_a, recv_a, send_b, recv_b, None
    )
    greet_all(rows, cols)
    first()

    block = me // rows
    slot = lax.rem(me, rows)
    own = [
        pltpu.make_async_copy(x_ref, x_rows.at[c], own_sem.at[0]),
        pltpu.make_async_copy(v_ref, v_rows.at[c], own_sem.at[1]),
    ]
    own_col = pltpu.make_async_copy(x_ref, x_cols.at[slot], own_sem.at[2])

    def to_col(step):
        return pltpu.make_async_remote_copy(
            src_ref=x_ref, dst_ref=x_cols.at[slot], send_sem=col_send.at[step],
            recv_sem=col_recv.at[slot], device_id=(lax.rem(i + step, rows), block),
            device_id_type=MESH_ID,
        )

    def from_col(k):
        return pltpu.make_async_remote_copy(
            src_ref=x_ref, dst_ref=x_cols.at[k], send_sem=col_send.at[0],
            recv_sem=col_recv.at[k], device_id=(i, twin), device_id_type=MESH_ID,
        )

    pieces = ((x_ref, x_rows), (v_ref, v_rows))

    def to_row(which, step):
        src, dst = pieces[which]
        return pltpu.make_async_remote_copy(
            src_ref=src, dst_ref=dst.at[c], send_sem=row_send.at[which, step],
            recv_sem=row_recv.at[which, step],
            device_id=(i, lax.rem(c + 2 * step, cols)), device_id_type=MESH_ID,
        )

    def to_twin(which, step):
        src, dst = pieces[which]
        at = lax.rem(c + cols - 2 * step, cols)
        return pltpu.make_async_remote_copy(
            src_ref=dst.at[at] if step else src, dst_ref=dst.at[at],
            send_sem=twin_send.at[which, step], recv_sem=twin_recv.at[which, step],
            device_id=(i, twin), device_id_type=MESH_ID,
        )

    is_own = block == c
    for step in range(1, rows):
        to_col(step).start()

    @pl.when(is_own)
    def _():
        own_col.start()

    @pl.when(jnp.logical_not(is_own))
    def _():
        to_col(0).start()

    for which in range(2):
        for step in range(1, chips):
            to_row(which, step).start()
    for which in range(2):
        own[which].start()
        to_twin(which, 0).start()
    second()
    for which in range(2):
        for step in range(1, chips):
            to_row(which, step).wait_recv()
            to_twin(which, step).start()
    for which in range(2):
        for step in range(chips):
            to_twin(which, step).wait_recv()
    for k in range(rows):
        source_is_me = c * rows + k == me

        @pl.when(source_is_me)
        def _():
            own_col.wait()

        @pl.when(jnp.logical_not(source_is_me))
        def _(k=k):
            from_col(k).wait_recv()

    for which in range(2):
        own[which].wait()
        for step in range(chips):
            to_twin(which, step).wait_send()
            if step:
                to_row(which, step).wait_send()
    third()
    for step in range(1, rows):
        to_col(step).wait_send()

    @pl.when(jnp.logical_not(is_own))
    def _():
        to_col(0).wait_send()


def gather_both(rows, cols, part, x, v, ident):
    height, width = x.shape
    chips = cols // 2
    count = rows * cols
    piece = width // count
    near = pl.BlockSpec(memory_space=pltpu.VMEM)
    spec = pl.BlockSpec(memory_space=pl.ANY)
    tall = jax.ShapeDtypeStruct((cols, height, width), jnp.float32)
    total, x_rows, v_rows, x_cols = pl.pallas_call(
        functools.partial(gather_kernel, rows, cols),
        out_shape=(
            jax.ShapeDtypeStruct((count, piece, width), jnp.float32), tall, tall,
            jax.ShapeDtypeStruct((rows, height, width), jnp.float32),
        ),
        in_specs=[near, spec, spec],
        out_specs=(near, spec, spec, spec),
        scratch_shapes=sum_scratch(count, piece, width) + [
            pltpu.SemaphoreType.DMA((rows,)),
            pltpu.SemaphoreType.DMA((rows,)),
            pltpu.SemaphoreType.DMA((2, chips)),
            pltpu.SemaphoreType.DMA((2, chips)),
            pltpu.SemaphoreType.DMA((2, chips)),
            pltpu.SemaphoreType.DMA((2, chips)),
            pltpu.SemaphoreType.DMA((3,)),
        ],
        compiler_params=pltpu.CompilerParams(collective_id=ident, has_side_effects=True),
    )(part.reshape(count, piece, width), x, v)
    return (
        total.reshape(width, width), x_rows.reshape(-1, width), v_rows.reshape(-1, width), x_cols.reshape(-1, width)
    )


def shards(rows, cols, a_trail, a_panel, l_panel, a_diag, l_inverse):
    chips = cols // 2
    height = a_panel.shape[0]
    block_width = a_diag.shape[0]
    row_index = lax.axis_index("row")
    col_index = lax.axis_index("col")
    chip = col_index // 2
    core = col_index % 2
    me = row_index * cols + col_index
    sibling = [(c, c ^ 1) for c in range(cols)]

    def chip_shift(step):
        return [(c, (c + 2 * step) % cols) for c in range(cols)]

    def rows_from(shard):
        out = jnp.zeros((cols,) + shard.shape, jnp.float32)
        for step in range(chips):
            part = lax.ppermute(shard, "col", chip_shift(step)) if step else shard
            twin = lax.ppermute(part, "col", sibling)
            at = (col_index + cols - 2 * step) % cols
            out = lax.dynamic_update_index_in_dim(out, part, at, 0)
            out = lax.dynamic_update_index_in_dim(out, twin, at ^ 1, 0)
        return out.reshape(cols * shard.shape[0], shard.shape[1])

    def cols_from(shard):
        out = jnp.zeros((rows,) + shard.shape, jnp.float32)
        for step in range(rows):
            pairs = [
                (c * rows + (i + step) % rows, i * cols + c)
                for i in range(rows) for c in range(cols)
            ]
            part = lax.ppermute(shard, BOTH, pairs)
            out = lax.dynamic_update_index_in_dim(out, part, (row_index + step) % rows, 0)
        return out.reshape(rows * shard.shape[0], shard.shape[1])

    def sum_to_shard(values):
        parts = values.reshape(chips, 2, height, values.shape[1])

        def pick(to_chip, to_core):
            return lax.dynamic_slice(
                parts, (to_chip, to_core, 0, 0), (1, 1) + parts.shape[2:]
            ).reshape(parts.shape[2:])

        total = None
        for step in range(chips):
            to_chip = (chip + step) % chips
            both = pick(to_chip, core) + lax.ppermute(pick(to_chip, 1 - core), "col", sibling)
            if step:
                both = lax.ppermute(both, "col", chip_shift(step))
            total = both if total is None else total + both
        return total

    a11_new = product(product(l_inverse, a_diag), l_inverse.T)
    solved = product(a_panel, l_inverse.T)
    half_term = 0.5 * product(l_panel, a11_new)
    first_y = solved - half_term
    panel_out = first_y - half_term
    pair = jnp.concatenate((first_y, l_panel), axis=1)
    tall = min(height, block_width)
    first_pair, a_first = first_exchange(
        rows, cols, jnp.concatenate([pair[:tall]] * (block_width // tall), axis=0), tall,
        a_trail, height, block_width, 0,
    )
    first_swap = jnp.concatenate(
        (first_pair[:, block_width:], first_pair[:, :block_width]), axis=1
    )
    panel = a_first - product(pair, first_swap.T)
    global_rows = me * height + lax.iota(jnp.int32, height)
    next_panel = jnp.where((global_rows >= block_width)[:, None], panel, 0.0)
    picker = (
        global_rows[:, None] - block_width == lax.iota(jnp.int32, block_width)[None, :]
    ).astype(jnp.float32)
    stats = sum_all(
        rows, cols,
        jnp.concatenate(
            (product(next_panel.T, next_panel), product(picker.T, next_panel)), axis=1
        ),
        1,
    )
    late_pair, stats = lax.optimization_barrier((pair, stats))
    late_pair = with_layout_constraint(late_pair, Layout(major_to_minor=(0, 1)))
    inverse, newton = factor_call(stats[:, :block_width], stats[:, block_width:])
    g_inverse = newton.T
    refl = product(next_panel, inverse.T) + picker

    pair_rows = rows_from(late_pair)
    pair_cols = cols_from(late_pair)
    swap_cols = jnp.concatenate((pair_cols[:, block_width:], pair_cols[:, :block_width]), axis=1)
    updated = a_trail - large_product(pair_rows, swap_cols.T)

    refl_cols = cols_from(refl)
    x_shard = product(sum_to_shard(large_product(updated, refl_cols)), g_inverse)
    core_sum, x_rows, refl_rows, x_cols = gather_both(
        rows, cols, product(refl.T, x_shard), x_shard, refl, 3
    )
    half_core = 0.5 * product(g_inverse.T, core_sum)
    z_cols = x_cols - product(refl_cols, half_core + half_core.T)
    trail_out = updated - large_product(
        jnp.concatenate((x_rows, refl_rows), axis=1),
        jnp.concatenate((refl_cols, z_cols), axis=1).T,
    )
    return (trail_out, panel_out)


def layer(rows, cols, *args):
    return shards(rows, cols, *args)


def solution(mesh):
    rows, cols = mesh.shape["row"], mesh.shape["col"]
    return jax.shard_map(
        functools.partial(layer, rows, cols),
        mesh=mesh,
        in_specs=(P("row", "col"), P(BOTH, None), P(BOTH, None), P(), P()),
        out_specs=(P("row", "col"), P(BOTH, None)),
        check_vma=False,
    )
```

```python
import functools

import jax
import jax.numpy as jnp
from jax import lax
from jax.experimental import pallas as pl
from jax.experimental.pallas import tpu as pltpu
from jax.sharding import PartitionSpec as P

NS_STEPS = 8
BOTH = ("row", "col")
MESH_ID = pl.DeviceIdType.MESH


def product(left, right):
    return jnp.dot(left, right, precision=lax.Precision.HIGHEST, preferred_element_type=jnp.float32)


def large_product(left, right):
    return jnp.dot(left, right, precision=lax.Precision.HIGH, preferred_element_type=jnp.float32)


def exact(left, right, dims=(((1,), (0,)), ((), ()))):
    return lax.dot_general(left, right, dims, precision=lax.Precision.HIGHEST, preferred_element_type=jnp.float32)


def three(x):
    high = x.astype(jnp.bfloat16).astype(jnp.float32)
    rest = x - high
    mid = rest.astype(jnp.bfloat16).astype(jnp.float32)
    return high, mid, rest - mid


def sub_block(V, lanes_at, n, W):
    row = lax.broadcasted_iota(jnp.int32, (8, 128), 0)
    shifted = pltpu.roll(V[:, :n], n - lanes_at, 1)[:, :128]
    cols = [jnp.broadcast_to(shifted[:, j:j+1], (8, 128)) for j in range(8)]
    vs = [V[:, 128*t:128*(t+1)] for t in range(W//128)]
    for j in range(8):
        r = lax.rsqrt(cols[j][j:j+1, :])
        r = r * (1.5 - 0.5 * cols[j][j:j+1, :] * r * r)
        lj = jnp.where(row > j, cols[j] * r, 0.0)
        sc = jnp.where(row == j, jnp.broadcast_to(r, (8,128)), 1.0)
        for k in range(j+1, 8):
            cols[k] = cols[k] - lj * lj[k:k+1, :]
        for t in range(len(vs)):
            top = vs[t][j:j+1, :] * r
            vs[t] = jnp.where(row == j, jnp.broadcast_to(top, (8,128)), vs[t] - lj * top)
    return jnp.concatenate(vs, axis=1)


def eliminate(work, n, begin, end):
    lane = lax.broadcasted_iota(jnp.int32, (8, n), 1)

    def body(b, carry):
        k0 = pl.multiple_of(b * 8, 8)
        V = sub_block(work[pl.ds(k0, 8), :], k0, n, 2 * n)
        work[pl.ds(k0, 8), :] = V
        h, m, l = three(jnp.where(lane >= k0 + 8, V[:, :n], 0.0))
        hr, mr, lr = three(V)
        lhs = jnp.concatenate([h, h, m, h, m, l], axis=0).astype(jnp.bfloat16)
        rhs = jnp.concatenate([hr, mr, hr, lr, mr, hr], axis=0).astype(jnp.bfloat16)
        work[...] -= lax.dot_general(
            lhs, rhs, (((0,), (0,)), ((), ())), preferred_element_type=jnp.float32
        )
        return carry

    lax.fori_loop(begin, end, body, 0)


def unit(n):
    return (
        lax.broadcasted_iota(jnp.int32, (n, n), 0) == lax.broadcasted_iota(jnp.int32, (n, n), 1)
    ).astype(jnp.float32)


def newton_product(q_top):
    rem = -q_top
    approx = unit(q_top.shape[0]) + rem
    for _ in range(NS_STEPS - 1):
        rem = exact(rem, rem)
        approx = approx + exact(approx, rem)
    return approx


def greet_all(rows, cols):
    count = rows * cols
    me = lax.axis_index("row") * cols + lax.axis_index("col")
    barrier = pltpu.get_barrier_semaphore()

    def greet(step, carry):
        at = lax.rem(me + step, count)
        pl.semaphore_signal(
            barrier, inc=1, device_id=(at // cols, lax.rem(at, cols)), device_id_type=MESH_ID
        )
        return carry

    lax.fori_loop(1, count, greet, 0)
    pl.semaphore_wait(barrier, count - 1)


def sum_steps(rows, cols, x_ref, o_ref, recv, red, send_a, recv_a, send_b, recv_b, held):
    count = rows * cols
    me = lax.axis_index("row") * cols + lax.axis_index("col")

    def peer(step):
        at = lax.rem(me + step, count)
        return at, (at // cols, lax.rem(at, cols))

    def owner(at):
        return (at * x_ref.shape[1]) // held

    def scatter(step):
        at, device = peer(step)
        return pltpu.make_async_remote_copy(
            src_ref=x_ref.at[at], dst_ref=recv.at[step], send_sem=send_a.at[step],
            recv_sem=recv_a.at[step], device_id=device, device_id_type=MESH_ID,
        )

    def gather(step):
        device = peer(step)[1]
        return pltpu.make_async_remote_copy(
            src_ref=red, dst_ref=o_ref.at[me], send_sem=send_b.at[step],
            recv_sem=recv_b.at[step], device_id=device, device_id_type=MESH_ID,
        )

    def loop(action):
        def body(step, carry):
            action(step)
            return carry

        lax.fori_loop(1, count, body, 0)

    def sends(step, action):
        if held is None:
            action()
        else:
            pl.when(owner(peer(step)[0]) == me)(action)

    def first():
        loop(lambda step: sends(step, lambda: scatter(step).start()))

    def second():
        if held is None:
            def add(step, total):
                scatter(step).wait_recv()
                return total + recv[step]

            total = lax.fori_loop(1, count, add, x_ref[me])
            red[...] = total
            o_ref[me] = total
        else:
            source = owner(me)

            @pl.when(source == me)
            def _():
                red[...] = x_ref[me]
                o_ref[me] = x_ref[me]

            @pl.when(source != me)
            def _():
                step = lax.rem(me + count - source, count)
                scatter(step).wait_recv()
                red[...] = recv[step]
                o_ref[me] = recv[step]
        loop(lambda step: gather(step).start())

    def third():
        def finish(step):
            gather(step).wait_recv()
            sends(step, lambda: scatter(step).wait_send())
            gather(step).wait_send()

        loop(finish)

    return first, second, third


def sum_scratch(count, piece, width):
    return [
        pltpu.VMEM((count, piece, width), jnp.float32),
        pltpu.VMEM((piece, width), jnp.float32),
        pltpu.SemaphoreType.DMA((count,)),
        pltpu.SemaphoreType.DMA((count,)),
        pltpu.SemaphoreType.DMA((count,)),
        pltpu.SemaphoreType.DMA((count,)),
    ]


def first_kernel(rows, cols, held, x_ref, a_ref, o_ref, a_first, recv, red, send_a, recv_a,
                 send_b, recv_b, send_p, recv_p, own_sem):
    i = lax.axis_index("row")
    c = lax.axis_index("col")
    height, width = a_first.shape
    first, second, third = sum_steps(
        rows, cols, x_ref, o_ref, recv, red, send_a, recv_a, send_b, recv_b, held
    )

    def piece(to):
        return pltpu.make_async_remote_copy(
            src_ref=a_ref.at[pl.ds(to * height, height), pl.ds(0, width)], dst_ref=a_first,
            send_sem=send_p.at[to], recv_sem=recv_p.at[0], device_id=(i, to),
            device_id_type=MESH_ID,
        )

    own = pltpu.make_async_copy(
        a_ref.at[pl.ds(0, height), pl.ds(0, width)], a_first, own_sem.at[0]
    )
    greet_all(rows, cols)
    first()

    @pl.when(c == 0)
    def _():
        own.start()
        for to in range(1, cols):
            piece(to).start()

    second()
    third()

    @pl.when(c == 0)
    def _():
        own.wait()
        for to in range(1, cols):
            piece(to).wait_send()

    @pl.when(c != 0)
    def _():
        piece(1).wait_recv()


def first_exchange(rows, cols, value, held, a_trail, height, block_width, ident):
    count = rows * cols
    tall, width = value.shape
    piece = tall // count
    spec = pl.BlockSpec(memory_space=pltpu.VMEM)
    anywhere = pl.BlockSpec(memory_space=pl.ANY)
    out, a_first = pl.pallas_call(
        functools.partial(first_kernel, rows, cols, held),
        out_shape=(
            jax.ShapeDtypeStruct((count, piece, width), jnp.float32),
            jax.ShapeDtypeStruct((height, block_width), jnp.float32),
        ),
        in_specs=[spec, anywhere],
        out_specs=(spec, spec),
        scratch_shapes=sum_scratch(count, piece, width) + [
            pltpu.SemaphoreType.DMA((cols,)),
            pltpu.SemaphoreType.DMA((1,)),
            pltpu.SemaphoreType.DMA((1,)),
        ],
        compiler_params=pltpu.CompilerParams(collective_id=ident, has_side_effects=True),
    )(value.reshape(count, piece, width), a_trail)
    return out.reshape(tall, width), a_first


def remote(src, dst, send, recv, device):
    return pltpu.make_async_remote_copy(
        src_ref=src, dst_ref=dst, send_sem=send, recv_sem=recv, device_id=device,
        device_id_type=MESH_ID,
    )


def two(x):
    high = x.astype(jnp.bfloat16)
    return high, (x - high.astype(jnp.float32)).astype(jnp.bfloat16)


class Place:
    def __init__(self, rows, cols):
        self.rows, self.cols, self.chips = rows, cols, cols // 2
        self.i, self.c = lax.axis_index("row"), lax.axis_index("col")
        self.core = lax.rem(self.c, 2)
        self.chip = self.c // 2
        self.twin = self.c + 1 - 2 * self.core
        self.bits = self.chips.bit_length() - 1

    def stride(self, step, core):
        return (1 - core) * (1 << step) + core * (1 << (self.bits - 1 - step))

    def flip(self, chip, step, core):
        size = self.stride(step, core)
        return chip + (1 - 2 * lax.rem(chip // size, 2)) * size

    def relative(self, mask, core):
        chip = self.chip
        for step in range(self.bits):
            if mask >> step & 1:
                chip = self.flip(chip, step, core)
        return chip


class PlaneSum:
    def __init__(self, place, x, out, recv, part, red, sems):
        self.p, self.x, self.out, self.recv, self.part, self.red = place, x, out, recv, part, red
        self.sems = sems

    @staticmethod
    def scratch(rows, cols, piece, width):
        return [
            pltpu.VMEM((cols, piece, width), jnp.float32),
            pltpu.VMEM((rows, piece, width), jnp.float32),
            pltpu.VMEM((piece, width), jnp.float32),
        ] + [pltpu.SemaphoreType.DMA((cols,))] * 2 + [pltpu.SemaphoreType.DMA((rows,))] * 2 + [
            pltpu.SemaphoreType.DMA((cols,))
        ] * 2

    def scatter(self, step):
        p = self.p
        to = lax.rem(p.c + step, p.cols)
        return remote(
            self.x.at[to], self.recv.at[step], self.sems[0].at[step], self.sems[1].at[step], (p.i, to)
        )

    def across(self, step):
        p = self.p
        to = lax.rem(p.i + step, p.rows)
        return remote(
            self.part.at[0], self.part.at[step], self.sems[2].at[step], self.sems[3].at[step],
            (to, p.c),
        )

    def gather(self, step):
        p = self.p
        to = lax.rem(p.c + step, p.cols)
        return remote(
            self.red, self.out.at[p.c], self.sems[4].at[step], self.sems[5].at[step], (p.i, to)
        )

    def loop(self, count, action):
        def body(step, carry):
            action(step)
            return carry

        lax.fori_loop(1, count, body, 0)

    def begin(self):
        self.loop(self.p.cols, lambda step: self.scatter(step).start())

    def middle(self):
        def add(step, total):
            self.scatter(step).wait_recv()
            return total + self.recv[step]

        self.part[0] = lax.fori_loop(1, self.p.cols, add, self.x[self.p.c])
        self.loop(self.p.rows, lambda step: self.across(step).start())

    def late(self):
        def add(step, total):
            self.across(step).wait_recv()
            return total + self.part[step]

        total = lax.fori_loop(1, self.p.rows, add, self.part[0])
        self.red[...] = total
        self.out[self.p.c] = total
        self.loop(self.p.cols, lambda step: self.gather(step).start())

    def arrive(self):
        self.loop(self.p.cols, lambda step: self.gather(step).wait_recv())

    def finish(self):
        self.loop(self.p.cols, lambda step: self.scatter(step).wait_send())
        self.loop(self.p.cols, lambda step: self.gather(step).wait_send())
        self.loop(self.p.rows, lambda step: self.across(step).wait_send())


class RowGather:
    def __init__(self, place, x, out, sems):
        self.p, self.x, self.out, self.sems = place, x, out, sems
        p = place
        self.own = pltpu.make_async_copy(x, out.at[p.c], sems[4].at[0])

    @staticmethod
    def scratch(cols):
        chips = cols // 2
        return [pltpu.SemaphoreType.DMA((chips,))] * 4 + [pltpu.SemaphoreType.DMA((1,))]

    def hop(self, step, mask):
        p = self.p
        at = p.relative(mask, p.core) * 2 + p.core
        index = (1 << step) - 1 + mask
        to = p.flip(p.chip, step, p.core) * 2 + p.core
        return remote(
            self.out.at[at] if mask else self.x, self.out.at[at], self.sems[0].at[index],
            self.sems[1].at[index], (p.i, to),
        )

    def to_twin(self, mask):
        p = self.p
        at = p.relative(mask, p.core) * 2 + p.core
        return remote(
            self.out.at[at] if mask else self.x, self.out.at[at], self.sems[2].at[mask],
            self.sems[3].at[mask], (p.i, p.twin),
        )

    def begin(self):
        for step in range(self.p.bits):
            self.hop(step, 0).start()
        self.own.start()
        self.to_twin(0).start()

    def arrivals(self):
        return [(step, mask) for step in range(self.p.bits) for mask in range(1 << step)]

    def forward(self, step, mask):
        self.hop(step, mask).wait_recv()
        here = mask + (1 << step)
        for later in range(step + 1, self.p.bits):
            self.hop(later, here).start()
        self.to_twin(here).start()

    def finish(self):
        self.own.wait()
        for mask in range(self.p.chips):
            self.to_twin(mask).wait_recv()
        for mask in range(self.p.chips):
            self.to_twin(mask).wait_send()
        for step, mask in self.arrivals():
            self.hop(step, mask).wait_send()


class LineGather:
    def __init__(self, place, x, out, sems):
        self.p, self.x, self.out, self.sems = place, x, out, sems
        self.own = pltpu.make_async_copy(x, out.at[place.i], sems[4].at[0])

    @staticmethod
    def scratch(rows):
        return [pltpu.SemaphoreType.DMA((rows,))] * 4 + [pltpu.SemaphoreType.DMA((1,))]

    def up(self, step):
        p = self.p
        at = p.i - step
        return remote(
            self.out.at[at] if step else self.x, self.out.at[at], self.sems[0].at[step],
            self.sems[1].at[step], (p.i + 1, p.c),
        )

    def up_recv(self, step):
        p = self.p
        return remote(
            self.x, self.out.at[p.i - step], self.sems[0].at[step], self.sems[1].at[step - 1],
            (p.i - 1, p.c),
        )

    def down(self, step):
        p = self.p
        at = p.i + step
        return remote(
            self.out.at[at] if step else self.x, self.out.at[at], self.sems[2].at[step],
            self.sems[3].at[step], (p.i - 1, p.c),
        )

    def down_recv(self, step):
        p = self.p
        return remote(
            self.x, self.out.at[p.i + step], self.sems[2].at[step], self.sems[3].at[step - 1],
            (p.i + 1, p.c),
        )

    def begin(self):
        p = self.p
        pl.when(p.i + 1 < p.rows)(lambda: self.up(0).start())
        pl.when(p.i >= 1)(lambda: self.down(0).start())
        self.own.start()

    def forward(self, step):
        p = self.p

        @pl.when(p.i >= step)
        def _():
            self.up_recv(step).wait_recv()
            pl.when(p.i + 1 < p.rows)(lambda: self.up(step).start())

        @pl.when(p.i + step < p.rows)
        def _():
            self.down_recv(step).wait_recv()
            pl.when(p.i >= 1)(lambda: self.down(step).start())

    def finish(self):
        p = self.p
        for step in range(p.rows):
            pl.when((p.i >= step) & (p.i + 1 < p.rows))(lambda step=step: self.up(step).wait_send())
            pl.when((p.i + step < p.rows) & (p.i >= 1))(lambda step=step: self.down(step).wait_send())
        self.own.wait()


class Spread:
    def __init__(self, place, x, out, sems):
        self.p, self.x, self.out, self.sems = place, x, out, sems
        self.per = place.cols // place.rows
        self.slot = lax.rem(place.c, place.rows)

    @staticmethod
    def scratch(rows):
        return [pltpu.SemaphoreType.DMA((rows,))] * 3

    def target(self, plane):
        return plane * self.per + self.p.c // self.p.rows

    def copy(self, plane):
        return remote(
            self.x.at[plane], self.out.at[self.slot], self.sems[0].at[plane],
            self.sems[1].at[self.slot], (self.p.i, self.target(plane)),
        )

    def local(self, plane):
        return pltpu.make_async_copy(self.x.at[plane], self.out.at[self.slot], self.sems[2].at[plane])

    def begin(self, plane):
        here = self.target(plane) == self.p.c
        pl.when(here)(lambda: self.local(plane).start())
        pl.when(jnp.logical_not(here))(lambda: self.copy(plane).start())

    def finish(self):
        p = self.p
        for slot in range(p.rows):
            source = lax.rem(p.c, self.per) * p.rows + slot

            @pl.when(source != p.c)
            def _(slot=slot):
                remote(
                    self.x.at[0], self.out.at[slot], self.sems[0].at[0], self.sems[1].at[slot],
                    (p.i, p.twin),
                ).wait_recv()

        for plane in range(p.rows):
            here = self.target(plane) == p.c
            pl.when(here)(lambda plane=plane: self.local(plane).wait())
            pl.when(jnp.logical_not(here))(lambda plane=plane: self.copy(plane).wait_send())


def take(refs, *counts):
    out, at = [], 0
    for count in counts:
        out.append(refs[at:at + count])
        at += count
    return out


ANY = pl.BlockSpec(memory_space=pl.ANY)
NEAR = pl.BlockSpec(memory_space=pltpu.VMEM)


def middle_kernel(rows, cols, stats_ref, panel_ref, pair_ref, inv_ref, newton_ref, panel_cols,
                  panel_line, pair_rows, pair_line, *refs):
    p = Place(rows, cols)
    total, work, *refs = refs
    s_sum, s_line, s_spread, s_row, s_pair = take(refs, 9, 5, 3, 5, 5)
    n = inv_ref.shape[0]
    sums = PlaneSum(p, stats_ref, total, *s_sum[:3], s_sum[3:])
    line = LineGather(p, panel_ref, panel_line, s_line)
    spread = Spread(p, panel_line, panel_cols, s_spread)
    row = RowGather(p, pair_ref, pair_rows, s_row)
    pline = LineGather(p, pair_ref, pair_line, s_pair)
    greet_all(rows, cols)
    sums.begin()
    line.begin()
    sums.middle()
    sums.late()
    row.begin()
    for step in range(1, rows):
        line.forward(step)
        if step == 1:
            sums.arrive()
    pline.begin()
    line.own.wait()
    for plane in range(rows):
        spread.begin(plane)
    stats = total[...].reshape(n, 2 * n)
    work[:, :n] = stats[:, :n]
    work[:, n:] = unit(n)
    todo = [lambda a=a: row.forward(*a) for a in row.arrivals()]
    todo[:0] = [lambda: pline.forward(1)]
    pieces = 4
    panels = n // 8 // pieces
    for part in range(pieces):
        eliminate(work, n, part * panels, (part + 1) * panels)
        for at, act in enumerate(todo):
            if at * pieces // len(todo) == part:
                act()
    inverse = work[:, n:]
    inv_ref[...] = inverse
    newton_ref[...] = newton_product(exact(stats[:, n:], inverse, (((1,), (1,)), ((), ()))))
    for step in range(2, rows):
        pline.forward(step)
    spread.finish()
    row.finish()
    sums.finish()
    line_finish(line)
    pline.finish()


def line_finish(line):
    p = line.p
    for step in range(p.rows):
        pl.when((p.i >= step) & (p.i + 1 < p.rows))(lambda step=step: line.up(step).wait_send())
        pl.when((p.i + step < p.rows) & (p.i >= 1))(lambda step=step: line.down(step).wait_send())


def middle(rows, cols, stats, panel, pair, ident):
    n = panel.shape[1]
    height = panel.shape[0]
    width = pair.shape[1]
    piece = n // cols
    square = jax.ShapeDtypeStruct((n, n), jnp.float32)
    outs = [
        square, square, jax.ShapeDtypeStruct((rows, height, n), jnp.float32),
        jax.ShapeDtypeStruct((rows, height, n), jnp.float32),
        jax.ShapeDtypeStruct((cols, height, width), jnp.float32),
        jax.ShapeDtypeStruct((rows, height, width), jnp.float32),
    ]
    scratch = [pltpu.VMEM((cols, piece, 2 * n), jnp.float32), pltpu.VMEM((n, 2 * n), jnp.float32)]
    scratch += PlaneSum.scratch(rows, cols, piece, 2 * n) + LineGather.scratch(rows)
    scratch += Spread.scratch(rows) + RowGather.scratch(cols) + LineGather.scratch(rows)
    inverse, newton, panel_cols, _, pair_rows, pair_line = pl.pallas_call(
        functools.partial(middle_kernel, rows, cols),
        out_shape=outs,
        in_specs=[NEAR, ANY, ANY],
        out_specs=[NEAR, NEAR, ANY, ANY, ANY, ANY],
        scratch_shapes=scratch,
        compiler_params=pltpu.CompilerParams(collective_id=ident, has_side_effects=True),
    )(stats.reshape(cols, piece, 2 * n), panel, pair)
    return inverse, newton, panel_cols.reshape(-1, n), pair_rows, pair_line


def image_kernel(rows, cols, cross_ref, a_ref, refl_ref, pair_line, image_ref, total_ref, pair_cols,
                 tiles, high, low, mine, twin_in, hop_in, *refs):
    p = Place(rows, cols)
    tile_sem, twin_send, twin_recv, hop_send, hop_recv, *refs = refs
    s_sum, s_spread = take(refs, 9, 3)
    height, _ = image_ref.shape
    chips = p.chips
    sums = PlaneSum(p, cross_ref, total_ref, *s_sum[:3], s_sum[3:])
    spread = Spread(p, pair_line, pair_cols, s_spread)
    masks = sorted(range(1, chips), key=lambda m: (m & -m, m)) + [0]
    other = 1 - p.core

    def piece_col(step):
        index = step // 2
        if step % 2:
            return p.relative(masks[index], p.core) * 2 + p.core
        return p.relative(masks[index], other) * 2 + other

    def load(step):
        at = pl.multiple_of(piece_col(step) * height, 8)
        return pltpu.make_async_copy(
            a_ref.at[pl.ds(at, height), :], tiles.at[step % 2], tile_sem.at[step % 2]
        )

    def to_twin(index):
        return remote(
            mine.at[2 * index], twin_in.at[index], twin_send.at[index], twin_recv.at[index],
            (p.i, p.twin),
        )

    hops = [(step, m) for step in range(p.bits) for m in range(chips) if m % (2 << step) == 0]
    number = {key: at for at, key in enumerate(hops)}

    def hop(step, mask):
        index = number[(step, mask)]
        to = p.flip(p.chip, step, p.core) * 2 + p.core
        return remote(
            mine.at[2 * masks.index(mask + (1 << step)) + 1], hop_in.at[index], hop_send.at[index],
            hop_recv.at[index], (p.i, to),
        )

    greet_all(rows, cols)
    sums.begin()
    load(0).start()
    high[...], low[...] = two(refl_ref[...])
    for plane in range(rows):
        spread.begin(plane)
    depth = high.shape[0]
    chunk = min(depth, 512)

    def multiply(slot, at):
        total = None
        for k in range(depth // chunk):
            a_high, a_low = two(tiles[slot, :, k * chunk:(k + 1) * chunk])
            y_high, y_low = high[k * chunk:(k + 1) * chunk, :], low[k * chunk:(k + 1) * chunk, :]
            dot = functools.partial(jnp.dot, preferred_element_type=jnp.float32)
            now = dot(a_high, y_high) + (dot(a_high, y_low) + dot(a_low, y_high))
            total = now if total is None else total + now
        mine[at] = total

    for step in range(2 * chips):
        if step + 1 < 2 * chips:
            load(step + 1).start()
        load(step).wait()
        multiply(step % 2, step)
        index = step // 2
        if step % 2 == 0:
            to_twin(index).start()
        else:
            mask = masks[index]
            low_bit = p.bits if mask == 0 else (mask & -mask).bit_length() - 1
            to_twin(index).wait_recv()
            value = mine[step] + twin_in[index]
            for t in range(low_bit):
                hop(t, mask).wait_recv()
                value = value + hop_in[number[(t, mask)]]
            if mask:
                mine[step] = value
                hop(low_bit, mask - (1 << low_bit)).start()
            else:
                image_ref[...] = value
        if step == 2:
            sums.middle()
        if step == 4:
            sums.late()
    sums.arrive()
    sums.finish()
    for index in range(chips):
        to_twin(index).wait_send()
    for step, mask in hops:
        hop(step, mask).wait_send()
    spread.finish()


def image(rows, cols, cross, a_trail, refl_cols, pair_line, height, ident):
    width, n = cross.shape
    piece = width // cols
    _, wide = a_trail.shape
    chips = cols // 2
    outs = [
        jax.ShapeDtypeStruct((height, n), jnp.float32),
        jax.ShapeDtypeStruct((cols, piece, n), jnp.float32),
        jax.ShapeDtypeStruct(pair_line.shape, jnp.float32),
    ]
    dma = pltpu.SemaphoreType.DMA
    scratch = [
        pltpu.VMEM((2, height, wide), jnp.float32), pltpu.VMEM((wide, n), jnp.bfloat16),
        pltpu.VMEM((wide, n), jnp.bfloat16), pltpu.VMEM((cols, height, n), jnp.float32),
        pltpu.VMEM((chips, height, n), jnp.float32), pltpu.VMEM((chips, height, n), jnp.float32),
        dma((2,)), dma((chips,)), dma((chips,)), dma((chips,)), dma((chips,)),
    ] + PlaneSum.scratch(rows, cols, piece, n) + Spread.scratch(rows)
    result, total, pair_cols = pl.pallas_call(
        functools.partial(image_kernel, rows, cols),
        out_shape=outs,
        in_specs=[NEAR, ANY, NEAR, ANY],
        out_specs=[NEAR, NEAR, ANY],
        scratch_shapes=scratch,
        compiler_params=pltpu.CompilerParams(collective_id=ident, has_side_effects=True),
    )(cross.reshape(cols, piece, n), a_trail, refl_cols, pair_line)
    return result, total.reshape(width, n), pair_cols.reshape(-1, pair_cols.shape[2])


def update_kernel(rows, cols, core_ref, a_ref, swap_ref, pair_rows, x_ref, y_ref, out_ref, total_ref,
                  x_cols, x_line, x_rows, y_rows, tiles, sides, results, high, low, *refs):
    p = Place(rows, cols)
    tile_sem, side_sem, out_sem, *refs = refs
    s_sum, s_line, s_spread, s_x, s_y = take(refs, 9, 5, 3, 5, 5)
    sums = PlaneSum(p, core_ref, total_ref, *s_sum[:3], s_sum[3:])
    line = LineGather(p, x_ref, x_line, s_line)
    spread = Spread(p, x_line, x_cols, s_spread)
    gather_x = RowGather(p, x_ref, x_rows, s_x)
    gather_y = RowGather(p, y_ref, y_rows, s_y)
    height = pair_rows.shape[1]

    def load(step):
        slot = lax.rem(step, 2)
        return (
            pltpu.make_async_copy(
                a_ref.at[pl.ds(pl.multiple_of(step * height, 8), height), :], tiles.at[slot],
                tile_sem.at[slot],
            ),
            pltpu.make_async_copy(pair_rows.at[step], sides.at[slot], side_sem.at[slot]),
        )

    def store(step):
        slot = lax.rem(step, 2)
        return pltpu.make_async_copy(
            results.at[slot], out_ref.at[pl.ds(pl.multiple_of(step * height, 8), height), :],
            out_sem.at[slot],
        )

    greet_all(rows, cols)
    sums.begin()
    line.begin()
    gather_x.begin()
    gather_y.begin()
    for copy in load(0):
        copy.start()
    high[...], low[...] = two(swap_ref[...])
    last = cols - 1
    chunk = min(high.shape[0], 512)

    def body(step, carry):
        @pl.when(step < last)
        def _():
            for copy in load(step + 1):
                copy.start()

        for copy in load(step):
            copy.wait()

        @pl.when(step >= 2)
        def _():
            store(step - 2).wait()

        slot = lax.rem(step, 2)
        l_high, l_low = two(sides[slot])

        def dot(left, right):
            return lax.dot_general(
                left, right, (((1,), (1,)), ((), ())), preferred_element_type=jnp.float32
            )

        for k in range(high.shape[0] // chunk):
            at = slice(k * chunk, (k + 1) * chunk)
            r_high, r_low = high[at, :], low[at, :]
            results[slot, :, at] = tiles[slot, :, at] - (
                dot(l_high, r_high) + (dot(l_high, r_low) + dot(l_low, r_high))
            )
        store(step).start()

        def begin_spread():
            line.own.wait()
            for plane in range(rows):
                spread.begin(plane)

        actions = {0: [sums.middle], 1: [sums.late]}
        for index, arrival in enumerate(gather_x.arrivals()):
            actions.setdefault(min(1 + index, last), []).append(
                lambda arrival=arrival: gather_x.forward(*arrival)
            )
        for index, arrival in enumerate(gather_y.arrivals()):
            actions.setdefault(min(2 + index, last), []).append(
                lambda arrival=arrival: gather_y.forward(*arrival)
            )
        for hop in range(1, rows):
            actions.setdefault(min(hop, last), []).append(lambda hop=hop: line.forward(hop))
        actions.setdefault(min(rows - 1, last), []).append(begin_spread)
        for when, todo in actions.items():
            @pl.when(step == when)
            def _(todo=todo):
                for action in todo:
                    action()
        return carry

    lax.fori_loop(0, cols, body, 0)
    sums.arrive()
    sums.finish()
    gather_x.finish()
    gather_y.finish()
    spread.finish()
    line_finish(line)
    for step in range(max(cols - 2, 0), cols):
        store(step).wait()


def update(rows, cols, core, a_trail, swap_cols, pair_rows, x, y, ident):
    n = core.shape[0]
    piece = n // cols
    height = x.shape[0]
    _, wide = a_trail.shape
    width = swap_cols.shape[1]
    outs = [
        jax.ShapeDtypeStruct(a_trail.shape, jnp.float32),
        jax.ShapeDtypeStruct((cols, piece, n), jnp.float32),
        jax.ShapeDtypeStruct((rows, height, n), jnp.float32),
        jax.ShapeDtypeStruct((rows, height, n), jnp.float32),
        jax.ShapeDtypeStruct((cols, height, n), jnp.float32),
        jax.ShapeDtypeStruct((cols, height, n), jnp.float32),
    ]
    dma = pltpu.SemaphoreType.DMA
    scratch = [
        pltpu.VMEM((2, height, wide), jnp.float32), pltpu.VMEM((2, height, width), jnp.float32),
        pltpu.VMEM((2, height, wide), jnp.float32), pltpu.VMEM((wide, width), jnp.bfloat16),
        pltpu.VMEM((wide, width), jnp.bfloat16), dma((2,)), dma((2,)), dma((2,)),
    ] + PlaneSum.scratch(rows, cols, piece, n) + LineGather.scratch(rows)
    scratch += Spread.scratch(rows) + RowGather.scratch(cols) + RowGather.scratch(cols)
    updated, total, x_cols, _, x_rows, y_rows = pl.pallas_call(
        functools.partial(update_kernel, rows, cols),
        out_shape=outs,
        in_specs=[NEAR, ANY, NEAR, ANY, ANY, ANY],
        out_specs=[ANY, NEAR, ANY, ANY, ANY, ANY],
        scratch_shapes=scratch,
        compiler_params=pltpu.CompilerParams(collective_id=ident, has_side_effects=True),
    )(core.reshape(cols, piece, n), a_trail, swap_cols, pair_rows, x, y)
    return (
        updated, total.reshape(n, n), x_cols.reshape(-1, n), x_rows.reshape(-1, n),
        y_rows.reshape(-1, n),
    )


def swapped(pair):
    half = pair.shape[1] // 2
    return jnp.concatenate((pair[:, half:], pair[:, :half]), axis=1)


def shards(rows, cols, a_trail, a_panel, l_panel, a_diag, l_inverse):
    height = a_panel.shape[0]
    block_width = a_diag.shape[0]
    me = lax.axis_index("row") * cols + lax.axis_index("col")
    a11_new = product(product(l_inverse, a_diag), l_inverse.T)
    solved = product(a_panel, l_inverse.T)
    half_term = 0.5 * product(l_panel, a11_new)
    first_y = solved - half_term
    panel_out = first_y - half_term
    pair = jnp.concatenate((first_y, l_panel), axis=1)
    tall = min(height, block_width)
    first_pair, a_first = first_exchange(
        rows, cols, jnp.concatenate([pair[:tall]] * (block_width // tall), axis=0), tall,
        a_trail, height, block_width, 0,
    )
    panel = a_first - product(pair, swapped(first_pair).T)
    lanes = lax.iota(jnp.int32, block_width)
    global_rows = me * height + lax.iota(jnp.int32, height)
    next_panel = jnp.where((global_rows >= block_width)[:, None], panel, 0.0)

    def picker(at):
        return (at[:, None] - block_width == lanes[None, :]).astype(jnp.float32)

    own_pick = picker(global_rows)
    stats = jnp.concatenate(
        (product(next_panel.T, next_panel), product(own_pick.T, next_panel)), axis=1
    )
    inverse, newton, panel_cols, pair_rows, pair_line = middle(
        rows, cols, stats, next_panel, pair, 1
    )
    g_inverse = newton.T
    wide = a_trail.shape[1]
    col_rows = lax.axis_index("col") * wide + lax.iota(jnp.int32, wide)
    refl = product(next_panel, inverse.T) + own_pick
    refl_cols = product(panel_cols, inverse.T) + picker(col_rows)
    image_shard, cross, pair_cols = image(
        rows, cols, product(pair.T, refl), a_trail, refl_cols, pair_line, height, 2
    )
    cross_swap = jnp.concatenate((cross[block_width:], cross[:block_width]), axis=0)
    x_shard = product(image_shard - product(pair, cross_swap), g_inverse)
    updated, core_sum, x_cols, x_rows, refl_rows = update(
        rows, cols, product(refl.T, x_shard), a_trail, swapped(pair_cols), pair_rows, x_shard, refl, 3
    )
    half_core = 0.5 * product(g_inverse.T, core_sum)
    z_cols = x_cols - product(refl_cols, half_core + half_core.T)
    trail_out = updated - large_product(
        jnp.concatenate((x_rows, refl_rows), axis=1),
        jnp.concatenate((refl_cols, z_cols), axis=1).T,
    )
    return (trail_out, panel_out)


def layer(rows, cols, *args):
    return shards(rows, cols, *args)


def solution(mesh):
    rows, cols = mesh.shape["row"], mesh.shape["col"]
    return jax.shard_map(
        functools.partial(layer, rows, cols),
        mesh=mesh,
        in_specs=(P("row", "col"), P(BOTH, None), P(BOTH, None), P(), P()),
        out_specs=(P("row", "col"), P(BOTH, None)),
        check_vma=False,
    )
```

```python
import functools

import jax
import jax.numpy as jnp
from jax import lax
from jax.experimental import pallas as pl
from jax.experimental.pallas import tpu as pltpu
from jax.sharding import PartitionSpec as P

NS_STEPS = 8
BOTH = ("row", "col")
MESH_ID = pl.DeviceIdType.MESH


def product(left, right):
    return jnp.dot(left, right, precision=lax.Precision.HIGHEST, preferred_element_type=jnp.float32)


def large_product(left, right):
    return jnp.dot(left, right, precision=lax.Precision.HIGH, preferred_element_type=jnp.float32)


def exact(left, right, dims=(((1,), (0,)), ((), ()))):
    return lax.dot_general(left, right, dims, precision=lax.Precision.HIGHEST, preferred_element_type=jnp.float32)


def three(x):
    high = x.astype(jnp.bfloat16).astype(jnp.float32)
    rest = x - high
    mid = rest.astype(jnp.bfloat16).astype(jnp.float32)
    return high, mid, rest - mid


def sub_block(V, lanes_at, n, W):
    row = lax.broadcasted_iota(jnp.int32, (8, 128), 0)
    shifted = pltpu.roll(V[:, :n], n - lanes_at, 1)[:, :128]
    cols = [jnp.broadcast_to(shifted[:, j:j+1], (8, 128)) for j in range(8)]
    vs = [V[:, 128*t:128*(t+1)] for t in range(W//128)]
    for j in range(8):
        r = lax.rsqrt(cols[j][j:j+1, :])
        r = r * (1.5 - 0.5 * cols[j][j:j+1, :] * r * r)
        lj = jnp.where(row > j, cols[j] * r, 0.0)
        sc = jnp.where(row == j, jnp.broadcast_to(r, (8,128)), 1.0)
        for k in range(j+1, 8):
            cols[k] = cols[k] - lj * lj[k:k+1, :]
        for t in range(len(vs)):
            top = vs[t][j:j+1, :] * r
            vs[t] = jnp.where(row == j, jnp.broadcast_to(top, (8,128)), vs[t] - lj * top)
    return jnp.concatenate(vs, axis=1)


def eliminate(work, n, begin, end):
    lane = lax.broadcasted_iota(jnp.int32, (8, n), 1)

    def body(b, carry):
        k0 = pl.multiple_of(b * 8, 8)
        V = sub_block(work[pl.ds(k0, 8), :], k0, n, 2 * n)
        work[pl.ds(k0, 8), :] = V
        h, m, l = three(jnp.where(lane >= k0 + 8, V[:, :n], 0.0))
        hr, mr, lr = three(V)
        lhs = jnp.concatenate([h, h, m, h, m, l], axis=0).astype(jnp.bfloat16)
        rhs = jnp.concatenate([hr, mr, hr, lr, mr, hr], axis=0).astype(jnp.bfloat16)
        work[...] -= lax.dot_general(
            lhs, rhs, (((0,), (0,)), ((), ())), preferred_element_type=jnp.float32
        )
        return carry

    lax.fori_loop(begin, end, body, 0)


def unit(n):
    return (
        lax.broadcasted_iota(jnp.int32, (n, n), 0) == lax.broadcasted_iota(jnp.int32, (n, n), 1)
    ).astype(jnp.float32)


def newton_product(q_top):
    rem = -q_top
    approx = unit(q_top.shape[0]) + rem
    for _ in range(NS_STEPS - 1):
        rem = exact(rem, rem)
        approx = approx + exact(approx, rem)
    return approx


def greet_all(rows, cols):
    count = rows * cols
    me = lax.axis_index("row") * cols + lax.axis_index("col")
    barrier = pltpu.get_barrier_semaphore()

    def greet(step, carry):
        at = lax.rem(me + step, count)
        pl.semaphore_signal(
            barrier, inc=1, device_id=(at // cols, lax.rem(at, cols)), device_id_type=MESH_ID
        )
        return carry

    lax.fori_loop(1, count, greet, 0)
    pl.semaphore_wait(barrier, count - 1)


def sum_steps(rows, cols, x_ref, o_ref, recv, red, send_a, recv_a, send_b, recv_b, held):
    count = rows * cols
    me = lax.axis_index("row") * cols + lax.axis_index("col")

    def peer(step):
        at = lax.rem(me + step, count)
        return at, (at // cols, lax.rem(at, cols))

    def owner(at):
        return (at * x_ref.shape[1]) // held

    def scatter(step):
        at, device = peer(step)
        return pltpu.make_async_remote_copy(
            src_ref=x_ref.at[at], dst_ref=recv.at[step], send_sem=send_a.at[step],
            recv_sem=recv_a.at[step], device_id=device, device_id_type=MESH_ID,
        )

    def gather(step):
        device = peer(step)[1]
        return pltpu.make_async_remote_copy(
            src_ref=red, dst_ref=o_ref.at[me], send_sem=send_b.at[step],
            recv_sem=recv_b.at[step], device_id=device, device_id_type=MESH_ID,
        )

    def loop(action):
        def body(step, carry):
            action(step)
            return carry

        lax.fori_loop(1, count, body, 0)

    def sends(step, action):
        if held is None:
            action()
        else:
            pl.when(owner(peer(step)[0]) == me)(action)

    def first():
        loop(lambda step: sends(step, lambda: scatter(step).start()))

    def second():
        if held is None:
            def add(step, total):
                scatter(step).wait_recv()
                return total + recv[step]

            total = lax.fori_loop(1, count, add, x_ref[me])
            red[...] = total
            o_ref[me] = total
        else:
            source = owner(me)

            @pl.when(source == me)
            def _():
                red[...] = x_ref[me]
                o_ref[me] = x_ref[me]

            @pl.when(source != me)
            def _():
                step = lax.rem(me + count - source, count)
                scatter(step).wait_recv()
                red[...] = recv[step]
                o_ref[me] = recv[step]
        loop(lambda step: gather(step).start())

    def third():
        def finish(step):
            gather(step).wait_recv()
            sends(step, lambda: scatter(step).wait_send())
            gather(step).wait_send()

        loop(finish)

    return first, second, third


def sum_scratch(count, piece, width):
    return [
        pltpu.VMEM((count, piece, width), jnp.float32),
        pltpu.VMEM((piece, width), jnp.float32),
        pltpu.SemaphoreType.DMA((count,)),
        pltpu.SemaphoreType.DMA((count,)),
        pltpu.SemaphoreType.DMA((count,)),
        pltpu.SemaphoreType.DMA((count,)),
    ]


def remote(src, dst, send, recv, device):
    return pltpu.make_async_remote_copy(
        src_ref=src, dst_ref=dst, send_sem=send, recv_sem=recv, device_id=device,
        device_id_type=MESH_ID,
    )


def two(x):
    high = x.astype(jnp.bfloat16)
    return high, (x - high.astype(jnp.float32)).astype(jnp.bfloat16)


class Place:
    def __init__(self, rows, cols):
        self.rows, self.cols, self.chips = rows, cols, cols // 2
        self.i, self.c = lax.axis_index("row"), lax.axis_index("col")
        self.core = lax.rem(self.c, 2)
        self.chip = self.c // 2
        self.twin = self.c + 1 - 2 * self.core
        self.bits = self.chips.bit_length() - 1

    def stride(self, step, core):
        return (1 - core) * (1 << step) + core * (1 << (self.bits - 1 - step))

    def flip(self, chip, step, core):
        size = self.stride(step, core)
        return chip + (1 - 2 * lax.rem(chip // size, 2)) * size

    def relative(self, mask, core):
        chip = self.chip
        for step in range(self.bits):
            if mask >> step & 1:
                chip = self.flip(chip, step, core)
        return chip


class PlaneSum:
    def __init__(self, place, x, out, recv, part, red, sems):
        self.p, self.x, self.out, self.recv, self.part, self.red = place, x, out, recv, part, red
        self.sems = sems

    @staticmethod
    def scratch(rows, cols, piece, width):
        return [
            pltpu.VMEM((cols, piece, width), jnp.float32),
            pltpu.VMEM((rows, piece, width), jnp.float32),
            pltpu.VMEM((piece, width), jnp.float32),
        ] + [pltpu.SemaphoreType.DMA((cols,))] * 2 + [pltpu.SemaphoreType.DMA((rows,))] * 2 + [
            pltpu.SemaphoreType.DMA((cols,))
        ] * 2

    def scatter(self, step):
        p = self.p
        to = lax.rem(p.c + step, p.cols)
        return remote(
            self.x.at[to], self.recv.at[step], self.sems[0].at[step], self.sems[1].at[step], (p.i, to)
        )

    def across(self, step):
        p = self.p
        to = lax.rem(p.i + step, p.rows)
        return remote(
            self.part.at[0], self.part.at[step], self.sems[2].at[step], self.sems[3].at[step],
            (to, p.c),
        )

    def gather(self, step):
        p = self.p
        to = lax.rem(p.c + step, p.cols)
        return remote(
            self.red, self.out.at[p.c], self.sems[4].at[step], self.sems[5].at[step], (p.i, to)
        )

    def loop(self, count, action):
        def body(step, carry):
            action(step)
            return carry

        lax.fori_loop(1, count, body, 0)

    def begin(self):
        self.loop(self.p.cols, lambda step: self.scatter(step).start())

    def middle(self):
        def add(step, total):
            self.scatter(step).wait_recv()
            return total + self.recv[step]

        self.part[0] = lax.fori_loop(1, self.p.cols, add, self.x[self.p.c])
        self.loop(self.p.rows, lambda step: self.across(step).start())

    def late(self):
        def add(step, total):
            self.across(step).wait_recv()
            return total + self.part[step]

        total = lax.fori_loop(1, self.p.rows, add, self.part[0])
        self.red[...] = total
        self.out[self.p.c] = total
        self.loop(self.p.cols, lambda step: self.gather(step).start())

    def arrive(self):
        self.loop(self.p.cols, lambda step: self.gather(step).wait_recv())

    def finish(self):
        self.loop(self.p.cols, lambda step: self.scatter(step).wait_send())
        self.loop(self.p.cols, lambda step: self.gather(step).wait_send())
        self.loop(self.p.rows, lambda step: self.across(step).wait_send())


class RowGather:
    def __init__(self, place, x, out, sems):
        self.p, self.x, self.out, self.sems = place, x, out, sems
        p = place
        self.own = pltpu.make_async_copy(x, out.at[p.c], sems[4].at[0])

    @staticmethod
    def scratch(cols):
        chips = cols // 2
        return [pltpu.SemaphoreType.DMA((chips,))] * 4 + [pltpu.SemaphoreType.DMA((1,))]

    def hop(self, step, mask):
        p = self.p
        at = p.relative(mask, p.core) * 2 + p.core
        index = (1 << step) - 1 + mask
        to = p.flip(p.chip, step, p.core) * 2 + p.core
        return remote(
            self.out.at[at] if mask else self.x, self.out.at[at], self.sems[0].at[index],
            self.sems[1].at[index], (p.i, to),
        )

    def to_twin(self, mask):
        p = self.p
        at = p.relative(mask, p.core) * 2 + p.core
        return remote(
            self.out.at[at] if mask else self.x, self.out.at[at], self.sems[2].at[mask],
            self.sems[3].at[mask], (p.i, p.twin),
        )

    def begin(self):
        for step in range(self.p.bits):
            self.hop(step, 0).start()
        self.own.start()
        self.to_twin(0).start()

    def arrivals(self):
        return [(step, mask) for step in range(self.p.bits) for mask in range(1 << step)]

    def forward(self, step, mask):
        self.hop(step, mask).wait_recv()
        here = mask + (1 << step)
        for later in range(step + 1, self.p.bits):
            self.hop(later, here).start()
        self.to_twin(here).start()

    def finish(self):
        self.own.wait()
        for mask in range(self.p.chips):
            self.to_twin(mask).wait_recv()
        for mask in range(self.p.chips):
            self.to_twin(mask).wait_send()
        for step, mask in self.arrivals():
            self.hop(step, mask).wait_send()


class LineGather:
    def __init__(self, place, x, out, sems):
        self.p, self.x, self.out, self.sems = place, x, out, sems
        self.own = pltpu.make_async_copy(x, out.at[place.i], sems[4].at[0])

    @staticmethod
    def scratch(rows):
        return [pltpu.SemaphoreType.DMA((rows,))] * 4 + [pltpu.SemaphoreType.DMA((1,))]

    def up(self, step):
        p = self.p
        at = p.i - step
        return remote(
            self.out.at[at] if step else self.x, self.out.at[at], self.sems[0].at[step],
            self.sems[1].at[step], (p.i + 1, p.c),
        )

    def up_recv(self, step):
        p = self.p
        return remote(
            self.x, self.out.at[p.i - step], self.sems[0].at[step], self.sems[1].at[step - 1],
            (p.i - 1, p.c),
        )

    def down(self, step):
        p = self.p
        at = p.i + step
        return remote(
            self.out.at[at] if step else self.x, self.out.at[at], self.sems[2].at[step],
            self.sems[3].at[step], (p.i - 1, p.c),
        )

    def down_recv(self, step):
        p = self.p
        return remote(
            self.x, self.out.at[p.i + step], self.sems[2].at[step], self.sems[3].at[step - 1],
            (p.i + 1, p.c),
        )

    def begin(self):
        p = self.p
        pl.when(p.i + 1 < p.rows)(lambda: self.up(0).start())
        pl.when(p.i >= 1)(lambda: self.down(0).start())
        self.own.start()

    def forward(self, step):
        p = self.p

        @pl.when(p.i >= step)
        def _():
            self.up_recv(step).wait_recv()
            pl.when(p.i + 1 < p.rows)(lambda: self.up(step).start())

        @pl.when(p.i + step < p.rows)
        def _():
            self.down_recv(step).wait_recv()
            pl.when(p.i >= 1)(lambda: self.down(step).start())

    def finish(self):
        p = self.p
        for step in range(p.rows):
            pl.when((p.i >= step) & (p.i + 1 < p.rows))(lambda step=step: self.up(step).wait_send())
            pl.when((p.i + step < p.rows) & (p.i >= 1))(lambda step=step: self.down(step).wait_send())
        self.own.wait()


class Spread:
    def __init__(self, place, x, out, sems):
        self.p, self.x, self.out, self.sems = place, x, out, sems
        self.per = place.cols // place.rows
        self.slot = lax.rem(place.c, place.rows)

    @staticmethod
    def scratch(rows):
        return [pltpu.SemaphoreType.DMA((rows,))] * 3

    def target(self, plane):
        return plane * self.per + self.p.c // self.p.rows

    def copy(self, plane):
        return remote(
            self.x.at[plane], self.out.at[self.slot], self.sems[0].at[plane],
            self.sems[1].at[self.slot], (self.p.i, self.target(plane)),
        )

    def local(self, plane):
        return pltpu.make_async_copy(self.x.at[plane], self.out.at[self.slot], self.sems[2].at[plane])

    def begin(self, plane):
        here = self.target(plane) == self.p.c
        pl.when(here)(lambda: self.local(plane).start())
        pl.when(jnp.logical_not(here))(lambda: self.copy(plane).start())

    def finish(self):
        p = self.p
        for slot in range(p.rows):
            source = lax.rem(p.c, self.per) * p.rows + slot

            @pl.when(source != p.c)
            def _(slot=slot):
                remote(
                    self.x.at[0], self.out.at[slot], self.sems[0].at[0], self.sems[1].at[slot],
                    (p.i, p.twin),
                ).wait_recv()

        for plane in range(p.rows):
            here = self.target(plane) == p.c
            pl.when(here)(lambda plane=plane: self.local(plane).wait())
            pl.when(jnp.logical_not(here))(lambda plane=plane: self.copy(plane).wait_send())


def take(refs, *counts):
    out, at = [], 0
    for count in counts:
        out.append(refs[at:at + count])
        at += count
    return out


ANY = pl.BlockSpec(memory_space=pl.ANY)
NEAR = pl.BlockSpec(memory_space=pltpu.VMEM)


def front_kernel(rows, cols, held, top_ref, panel_ref, l_ref, diag_ref, linv_ref, a_ref,
                 out_ref, f_ref, next_ref, inv_ref, newton_ref, panel_cols, panel_line, l_rows,
                 l_line, f_rows, f_line, l_cols, *refs):
    p = Place(rows, cols)
    top_all, a_first, stats, total, work, *refs = refs
    send_p, recv_p, own_sem, *refs = refs
    (s_top, s_sum, s_line, s_spread, s_lrow, s_lline, s_lspread, s_frow, s_fline) = take(
        refs, 6, 9, 5, 3, 5, 5, 3, 5, 5
    )
    n = inv_ref.shape[0]
    height = f_ref.shape[0]
    tops = sum_steps(rows, cols, top_ref, top_all, *s_top, held)
    sums = PlaneSum(p, stats, total, *s_sum[:3], s_sum[3:])
    line = LineGather(p, next_ref, panel_line, s_line)
    spread = Spread(p, panel_line, panel_cols, s_spread)
    l_row = RowGather(p, l_ref, l_rows, s_lrow)
    l_pass = LineGather(p, l_ref, l_line, s_lline)
    l_spread = Spread(p, l_line, l_cols, s_lspread)
    f_row = RowGather(p, f_ref, f_rows, s_frow)
    f_pass = LineGather(p, f_ref, f_line, s_fline)

    def piece(to):
        return remote(
            a_ref.at[pl.ds(to * height, height), pl.ds(0, n)], a_first, send_p.at[to],
            recv_p.at[0], (p.i, to),
        )

    own = pltpu.make_async_copy(a_ref.at[pl.ds(0, height), pl.ds(0, n)], a_first, own_sem.at[0])
    greet_all(rows, cols)
    tops[0]()

    @pl.when(p.c == 0)
    def _():
        own.start()
        for to in range(1, cols):
            piece(to).start()

    l_pass.begin()
    pl.when(p.chip != 0)(l_row.begin)
    across = (((1,), (1,)), ((), ()))
    along = (((0,), (0,)), ((), ()))
    linv = linv_ref[...]
    a11 = exact(exact(linv, diag_ref[...]), linv, across)
    half = 0.5 * exact(l_ref[...], a11)
    f_ref[...] = exact(panel_ref[...], linv, across) - half
    out_ref[...] = f_ref[...] - half
    tops[1]()
    tops[2]()
    top = top_all[...].reshape(n, 2 * n)
    l_top = top[:, n:]
    f_top = exact(top[:, :n], linv, across) - 0.5 * exact(l_top, a11)

    @pl.when(p.c == 0)
    def _():
        own.wait()
        for to in range(1, cols):
            piece(to).wait_send()

    @pl.when(p.c != 0)
    def _():
        piece(1).wait_recv()

    pl.when(p.chip == 0)(l_row.begin)
    me = p.i * cols + p.c
    at = me * height + lax.broadcasted_iota(jnp.int32, (height, n), 0)
    panel = a_first[...] - exact(f_ref[...], l_top, across) - exact(l_ref[...], f_top, across)
    panel = jnp.where(at >= n, panel, 0.0)
    next_ref[...] = panel
    picker = (at - n == lax.broadcasted_iota(jnp.int32, (height, n), 1)).astype(jnp.float32)
    gram = exact(panel, panel, along)
    pick = exact(picker, panel, along)
    deep = n // cols
    for at in range(cols):
        rows_at = slice(at * deep, (at + 1) * deep)
        stats[at, :, :n] = gram[rows_at]
        stats[at, :, n:] = pick[rows_at]
    sums.begin()
    l_pass.forward(1)
    line.begin()
    sums.middle()
    l_pass.forward(2)
    sums.late()
    line.own.wait()
    spread.begin(p.i)
    f_row.begin()
    for step in range(3, rows):
        l_pass.forward(step)
    sums.arrive()
    line.forward(1)
    whole = total[...].reshape(n, 2 * n)
    work[:, :n] = whole[:, :n]
    work[:, n:] = unit(n)

    def spread_next(step):
        pl.when(p.i >= step)(lambda: spread.begin(p.i - step))
        pl.when(p.i + step < rows)(lambda: spread.begin(p.i + step))

    def spread_l():
        l_pass.own.wait()
        for plane in range(rows):
            l_spread.begin(plane)

    todo = [lambda: spread_next(1)]
    todo += [lambda a=a: l_row.forward(*a) for a in l_row.arrivals()]
    for step in range(2, rows):
        todo += [lambda step=step: line.forward(step), lambda step=step: spread_next(step)]
    todo += [f_pass.begin]
    todo += [lambda a=a: f_row.forward(*a) for a in f_row.arrivals()]
    todo += [spread_l] + [lambda step=step: f_pass.forward(step) for step in range(1, 2)]
    pieces = 8
    panels = n // 8 // pieces
    for part in range(pieces):
        eliminate(work, n, part * panels, (part + 1) * panels)
        for at, act in enumerate(todo):
            if at * pieces // len(todo) == part:
                act()
    inverse = work[:, n:]
    inv_ref[...] = inverse
    newton_ref[...] = newton_product(exact(whole[:, n:], inverse, across))
    for step in range(2, rows):
        f_pass.forward(step)
    spread.finish()
    l_spread.finish()
    l_row.finish()
    f_row.finish()
    sums.finish()
    line_finish(line)
    line_finish(l_pass)
    f_pass.finish()


def line_finish(line):
    p = line.p
    for step in range(p.rows):
        pl.when((p.i >= step) & (p.i + 1 < p.rows))(lambda step=step: line.up(step).wait_send())
        pl.when((p.i + step < p.rows) & (p.i >= 1))(lambda step=step: line.down(step).wait_send())


def front(rows, cols, top, held, a_panel, l_panel, a_diag, l_inverse, a_trail, ident):
    height, n = a_panel.shape
    count = rows * cols
    small, deep = n // count, n // cols

    def f32(*shape):
        return jax.ShapeDtypeStruct(shape, jnp.float32)

    outs = [
        f32(height, n), f32(height, n), f32(height, n), f32(n, n), f32(n, n),
        f32(rows, height, n), f32(rows, height, n), f32(cols, height, n), f32(rows, height, n),
        f32(cols, height, n), f32(rows, height, n), f32(rows, height, n),
    ]
    dma = pltpu.SemaphoreType.DMA
    scratch = [
        pltpu.VMEM((count, small, 2 * n), jnp.float32), pltpu.VMEM((height, n), jnp.float32),
        pltpu.VMEM((cols, deep, 2 * n), jnp.float32), pltpu.VMEM((cols, deep, 2 * n), jnp.float32),
        pltpu.VMEM((n, 2 * n), jnp.float32), dma((cols,)), dma((1,)), dma((1,)),
    ] + sum_scratch(count, small, 2 * n) + PlaneSum.scratch(rows, cols, deep, 2 * n)
    scratch += LineGather.scratch(rows) + Spread.scratch(rows)
    scratch += RowGather.scratch(cols) + LineGather.scratch(rows) + Spread.scratch(rows)
    scratch += RowGather.scratch(cols) + LineGather.scratch(rows)
    return pl.pallas_call(
        functools.partial(front_kernel, rows, cols, held),
        out_shape=outs,
        in_specs=[NEAR, NEAR, NEAR, NEAR, NEAR, ANY],
        out_specs=[NEAR] * 5 + [ANY] * 7,
        scratch_shapes=scratch,
        compiler_params=pltpu.CompilerParams(collective_id=ident, has_side_effects=True),
    )(top.reshape(count, small, 2 * n), a_panel, l_panel, a_diag, l_inverse, a_trail)


def image_kernel(rows, cols, cross_ref, a_ref, refl_ref, f_line, y_ref, image_ref, total_ref, f_cols,
                 y_rows, tiles, high, low, mine, twin_in, hop_in, *refs):
    p = Place(rows, cols)
    tile_sem, twin_send, twin_recv, hop_send, hop_recv, *refs = refs
    s_sum, s_spread, s_y = take(refs, 9, 3, 5)
    gather_y = RowGather(p, y_ref, y_rows, s_y)
    height, _ = image_ref.shape
    chips = p.chips
    sums = PlaneSum(p, cross_ref, total_ref, *s_sum[:3], s_sum[3:])
    spread = Spread(p, f_line, f_cols, s_spread)
    masks = sorted(range(1, chips), key=lambda m: (m & -m, m)) + [0]
    other = 1 - p.core

    def piece_col(step):
        index = step // 2
        if step % 2:
            return p.relative(masks[index], p.core) * 2 + p.core
        return p.relative(masks[index], other) * 2 + other

    def load(step):
        at = pl.multiple_of(piece_col(step) * height, 8)
        return pltpu.make_async_copy(
            a_ref.at[pl.ds(at, height), :], tiles.at[step % 2], tile_sem.at[step % 2]
        )

    def to_twin(index):
        return remote(
            mine.at[2 * index], twin_in.at[index], twin_send.at[index], twin_recv.at[index],
            (p.i, p.twin),
        )

    hops = [(step, m) for step in range(p.bits) for m in range(chips) if m % (2 << step) == 0]
    number = {key: at for at, key in enumerate(hops)}

    def hop(step, mask):
        index = number[(step, mask)]
        to = p.flip(p.chip, step, p.core) * 2 + p.core
        return remote(
            mine.at[2 * masks.index(mask + (1 << step)) + 1], hop_in.at[index], hop_send.at[index],
            hop_recv.at[index], (p.i, to),
        )

    greet_all(rows, cols)
    sums.begin()
    load(0).start()
    high[...], low[...] = two(refl_ref[...])
    for plane in range(rows):
        spread.begin(plane)
    depth = high.shape[0]
    chunk = min(depth, 512)

    def multiply(slot, at):
        total = None
        for k in range(depth // chunk):
            a_high, a_low = two(tiles[slot, :, k * chunk:(k + 1) * chunk])
            y_high, y_low = high[k * chunk:(k + 1) * chunk, :], low[k * chunk:(k + 1) * chunk, :]
            dot = functools.partial(jnp.dot, preferred_element_type=jnp.float32)
            now = dot(a_high, y_high) + (dot(a_high, y_low) + dot(a_low, y_high))
            total = now if total is None else total + now
        mine[at] = total

    for step in range(2 * chips):
        if step + 1 < 2 * chips:
            load(step + 1).start()
        load(step).wait()
        multiply(step % 2, step)
        index = step // 2
        if step % 2 == 0:
            to_twin(index).start()
        else:
            mask = masks[index]
            low_bit = p.bits if mask == 0 else (mask & -mask).bit_length() - 1
            to_twin(index).wait_recv()
            value = mine[step] + twin_in[index]
            for t in range(low_bit):
                hop(t, mask).wait_recv()
                value = value + hop_in[number[(t, mask)]]
            if mask:
                mine[step] = value
                hop(low_bit, mask - (1 << low_bit)).start()
            else:
                image_ref[...] = value
        if step == 2:
            sums.middle()
            gather_y.begin()
        if step == 4:
            sums.late()
    for arrival in gather_y.arrivals():
        gather_y.forward(*arrival)
    sums.arrive()
    sums.finish()
    gather_y.finish()
    for index in range(chips):
        to_twin(index).wait_send()
    for step, mask in hops:
        hop(step, mask).wait_send()
    spread.finish()


def image(rows, cols, cross, a_trail, refl_cols, f_line, refl, ident):
    width, n = cross.shape
    piece = width // cols
    wide = a_trail.shape[1]
    height = refl.shape[0]
    chips = cols // 2
    outs = [
        jax.ShapeDtypeStruct((height, n), jnp.float32),
        jax.ShapeDtypeStruct((cols, piece, n), jnp.float32),
        jax.ShapeDtypeStruct(f_line.shape, jnp.float32),
        jax.ShapeDtypeStruct((cols, height, n), jnp.float32),
    ]
    dma = pltpu.SemaphoreType.DMA
    scratch = [
        pltpu.VMEM((2, height, wide), jnp.float32), pltpu.VMEM((wide, n), jnp.bfloat16),
        pltpu.VMEM((wide, n), jnp.bfloat16), pltpu.VMEM((cols, height, n), jnp.float32),
        pltpu.VMEM((chips, height, n), jnp.float32), pltpu.VMEM((chips, height, n), jnp.float32),
        dma((2,)), dma((chips,)), dma((chips,)), dma((chips,)), dma((chips,)),
    ] + PlaneSum.scratch(rows, cols, piece, n) + Spread.scratch(rows) + RowGather.scratch(cols)
    result, total, f_cols, y_rows = pl.pallas_call(
        functools.partial(image_kernel, rows, cols),
        out_shape=outs,
        in_specs=[NEAR, ANY, NEAR, ANY, ANY],
        out_specs=[NEAR, NEAR, ANY, ANY],
        scratch_shapes=scratch,
        compiler_params=pltpu.CompilerParams(collective_id=ident, has_side_effects=True),
    )(cross.reshape(cols, piece, n), a_trail, refl_cols, f_line, refl)
    return result, total.reshape(width, n), f_cols.reshape(-1, n), y_rows.reshape(-1, n)


def update_kernel(rows, cols, core_ref, a_ref, l_cols, f_cols, f_rows, l_rows, x_ref, out_ref,
                  total_ref, x_cols, x_line, x_rows, tiles, sides, results, high, low, *refs):
    p = Place(rows, cols)
    tile_sem, side_sem, out_sem, *refs = refs
    s_sum, s_line, s_spread, s_x = take(refs, 9, 5, 3, 5)
    sums = PlaneSum(p, core_ref, total_ref, *s_sum[:3], s_sum[3:])
    line = LineGather(p, x_ref, x_line, s_line)
    spread = Spread(p, x_line, x_cols, s_spread)
    gather_x = RowGather(p, x_ref, x_rows, s_x)
    height, n = f_rows.shape[1:]

    def load(step):
        slot = lax.rem(step, 2)
        return (
            pltpu.make_async_copy(
                a_ref.at[pl.ds(pl.multiple_of(step * height, 8), height), :], tiles.at[slot],
                tile_sem.at[slot],
            ),
            pltpu.make_async_copy(f_rows.at[step], sides.at[slot, 0], side_sem.at[0, slot]),
            pltpu.make_async_copy(l_rows.at[step], sides.at[slot, 1], side_sem.at[1, slot]),
        )

    def store(step):
        slot = lax.rem(step, 2)
        return pltpu.make_async_copy(
            results.at[slot], out_ref.at[pl.ds(pl.multiple_of(step * height, 8), height), :],
            out_sem.at[slot],
        )

    greet_all(rows, cols)
    sums.begin()
    line.begin()
    gather_x.begin()
    for copy in load(0):
        copy.start()
    high[:, :n], low[:, :n] = two(l_cols[...])
    high[:, n:], low[:, n:] = two(f_cols[...])
    last = cols - 1
    chunk = min(high.shape[0], 512)

    def body(step, carry):
        @pl.when(step < last)
        def _():
            for copy in load(step + 1):
                copy.start()

        for copy in load(step):
            copy.wait()

        @pl.when(step >= 2)
        def _():
            store(step - 2).wait()

        slot = lax.rem(step, 2)
        f_high, f_low = two(sides[slot, 0])
        l_high, l_low = two(sides[slot, 1])

        def dot(left, right):
            return lax.dot_general(
                left, right, (((1,), (1,)), ((), ())), preferred_element_type=jnp.float32
            )

        for k in range(high.shape[0] // chunk):
            at = slice(k * chunk, (k + 1) * chunk)
            with_l, with_f = high[at, :n], high[at, n:]
            results[slot, :, at] = tiles[slot, :, at] - (
                (dot(f_high, with_l) + dot(l_high, with_f))
                + (dot(f_high, low[at, :n]) + dot(f_low, with_l))
                + (dot(l_high, low[at, n:]) + dot(l_low, with_f))
            )
        store(step).start()

        def begin_spread():
            line.own.wait()
            for plane in range(rows):
                spread.begin(plane)

        actions = {0: [sums.middle], 1: [sums.late]}
        for index, arrival in enumerate(gather_x.arrivals()):
            actions.setdefault(min(1 + index, last), []).append(
                lambda arrival=arrival: gather_x.forward(*arrival)
            )
        for hop in range(1, rows):
            actions.setdefault(min(hop, last), []).append(lambda hop=hop: line.forward(hop))
        actions.setdefault(min(rows - 1, last), []).append(begin_spread)
        for when, todo in actions.items():
            @pl.when(step == when)
            def _(todo=todo):
                for action in todo:
                    action()
        return carry

    lax.fori_loop(0, cols, body, 0)
    sums.arrive()
    sums.finish()
    gather_x.finish()
    spread.finish()
    line_finish(line)
    for step in range(max(cols - 2, 0), cols):
        store(step).wait()


def update(rows, cols, core, a_trail, l_cols, f_cols, f_rows, l_rows, x, ident):
    n = core.shape[0]
    piece = n // cols
    height = x.shape[0]
    wide = a_trail.shape[1]
    outs = [
        jax.ShapeDtypeStruct(a_trail.shape, jnp.float32),
        jax.ShapeDtypeStruct((cols, piece, n), jnp.float32),
        jax.ShapeDtypeStruct((rows, height, n), jnp.float32),
        jax.ShapeDtypeStruct((rows, height, n), jnp.float32),
        jax.ShapeDtypeStruct((cols, height, n), jnp.float32),
    ]
    dma = pltpu.SemaphoreType.DMA
    scratch = [
        pltpu.VMEM((2, height, wide), jnp.float32), pltpu.VMEM((2, 2, height, n), jnp.float32),
        pltpu.VMEM((2, height, wide), jnp.float32), pltpu.VMEM((wide, 2 * n), jnp.bfloat16),
        pltpu.VMEM((wide, 2 * n), jnp.bfloat16), dma((2,)), dma((2, 2)), dma((2,)),
    ] + PlaneSum.scratch(rows, cols, piece, n) + LineGather.scratch(rows)
    scratch += Spread.scratch(rows) + RowGather.scratch(cols)
    updated, total, x_cols, _, x_rows = pl.pallas_call(
        functools.partial(update_kernel, rows, cols),
        out_shape=outs,
        in_specs=[NEAR, ANY, NEAR, NEAR, ANY, ANY, ANY],
        out_specs=[ANY, NEAR, ANY, ANY, ANY],
        scratch_shapes=scratch,
        compiler_params=pltpu.CompilerParams(collective_id=ident, has_side_effects=True),
    )(core.reshape(cols, piece, n), a_trail, l_cols, f_cols, f_rows, l_rows, x)
    return updated, total.reshape(n, n), x_cols.reshape(-1, n), x_rows.reshape(-1, n)


def shards(rows, cols, a_trail, a_panel, l_panel, a_diag, l_inverse):
    height, block_width = a_panel.shape
    me = lax.axis_index("row") * cols + lax.axis_index("col")
    tall = min(height, block_width)
    top = jnp.concatenate((a_panel[:tall], l_panel[:tall]), axis=1)
    (panel_out, first_y, next_panel, inverse, newton, panel_cols, _, l_rows, _, f_rows, f_line,
     l_cols) = front(
        rows, cols, jnp.concatenate([top] * (block_width // tall), axis=0), tall, a_panel, l_panel,
        a_diag, l_inverse, a_trail, 0,
    )
    panel_cols, l_cols = panel_cols.reshape(-1, block_width), l_cols.reshape(-1, block_width)

    def picker(at):
        return (at[:, None] - block_width == lax.iota(jnp.int32, block_width)[None, :]).astype(
            jnp.float32
        )

    wide = a_trail.shape[1]
    refl = large_product(next_panel, inverse.T) + picker(me * height + lax.iota(jnp.int32, height))
    refl_cols = large_product(panel_cols, inverse.T) + picker(
        lax.axis_index("col") * wide + lax.iota(jnp.int32, wide)
    )
    image_shard, cross, f_cols, refl_rows = image(
        rows, cols,
        jnp.concatenate((large_product(first_y.T, refl), large_product(l_panel.T, refl)), axis=0),
        a_trail, refl_cols, f_line, refl, 2,
    )
    x_shard = product(
        image_shard - large_product(first_y, cross[block_width:])
        - large_product(l_panel, cross[:block_width]),
        newton.T,
    )
    updated, core_sum, x_cols, x_rows = update(
        rows, cols, large_product(refl.T, x_shard), a_trail, l_cols, f_cols, f_rows, l_rows, x_shard, 3
    )
    half_core = 0.5 * product(newton, core_sum)
    z_cols = x_cols - large_product(refl_cols, half_core + half_core.T)
    trail_out = updated - large_product(
        jnp.concatenate((x_rows, refl_rows), axis=1),
        jnp.concatenate((refl_cols, z_cols), axis=1).T,
    )
    return (trail_out, panel_out)


def layer(rows, cols, *args):
    return shards(rows, cols, *args)


def solution(mesh):
    rows, cols = mesh.shape["row"], mesh.shape["col"]
    return jax.shard_map(
        functools.partial(layer, rows, cols),
        mesh=mesh,
        in_specs=(P("row", "col"), P(BOTH, None), P(BOTH, None), P(), P()),
        out_specs=(P("row", "col"), P(BOTH, None)),
        check_vma=False,
    )
```

```python
import functools

import jax
import jax.numpy as jnp
from jax import lax
from jax.experimental import pallas as pl
from jax.experimental.pallas import tpu as pltpu
from jax.sharding import PartitionSpec as P

NS_STEPS = 8
BOTH = ("row", "col")
MESH_ID = pl.DeviceIdType.MESH


def product(left, right):
    return jnp.dot(left, right, precision=lax.Precision.HIGHEST, preferred_element_type=jnp.float32)


def large_product(left, right):
    return jnp.dot(left, right, precision=lax.Precision.HIGH, preferred_element_type=jnp.float32)


def exact(left, right, dims=(((1,), (0,)), ((), ()))):
    return lax.dot_general(left, right, dims, precision=lax.Precision.HIGHEST, preferred_element_type=jnp.float32)


def three(x):
    high = x.astype(jnp.bfloat16).astype(jnp.float32)
    rest = x - high
    mid = rest.astype(jnp.bfloat16).astype(jnp.float32)
    return high, mid, rest - mid


def sub_block(V, lanes_at, n, W):
    row = lax.broadcasted_iota(jnp.int32, (8, 128), 0)
    shifted = pltpu.roll(V[:, :n], n - lanes_at, 1)[:, :128]
    cols = [jnp.broadcast_to(shifted[:, j:j+1], (8, 128)) for j in range(8)]
    vs = [V[:, 128*t:128*(t+1)] for t in range(W//128)]
    for j in range(8):
        r = lax.rsqrt(cols[j][j:j+1, :])
        r = r * (1.5 - 0.5 * cols[j][j:j+1, :] * r * r)
        lj = jnp.where(row > j, cols[j] * r, 0.0)
        sc = jnp.where(row == j, jnp.broadcast_to(r, (8,128)), 1.0)
        for k in range(j+1, 8):
            cols[k] = cols[k] - lj * lj[k:k+1, :]
        for t in range(len(vs)):
            top = vs[t][j:j+1, :] * r
            vs[t] = jnp.where(row == j, jnp.broadcast_to(top, (8,128)), vs[t] - lj * top)
    return jnp.concatenate(vs, axis=1)


def eliminate(work, n, begin, end):
    lane = lax.broadcasted_iota(jnp.int32, (8, n), 1)

    def body(b, carry):
        k0 = pl.multiple_of(b * 8, 8)
        V = sub_block(work[pl.ds(k0, 8), :], k0, n, 2 * n)
        work[pl.ds(k0, 8), :] = V
        h, m, l = three(jnp.where(lane >= k0 + 8, V[:, :n], 0.0))
        hr, mr, lr = three(V)
        lhs = jnp.concatenate([h, h, m, h, m, l], axis=0).astype(jnp.bfloat16)
        rhs = jnp.concatenate([hr, mr, hr, lr, mr, hr], axis=0).astype(jnp.bfloat16)
        work[...] -= lax.dot_general(
            lhs, rhs, (((0,), (0,)), ((), ())), preferred_element_type=jnp.float32
        )
        return carry

    lax.fori_loop(begin, end, body, 0)


def unit(n):
    return (
        lax.broadcasted_iota(jnp.int32, (n, n), 0) == lax.broadcasted_iota(jnp.int32, (n, n), 1)
    ).astype(jnp.float32)


def newton_product(q_top):
    rem = -q_top
    approx = unit(q_top.shape[0]) + rem
    for _ in range(NS_STEPS - 1):
        rem = exact(rem, rem)
        approx = approx + exact(approx, rem)
    return approx


def greet_all(rows, cols):
    count = rows * cols
    me = lax.axis_index("row") * cols + lax.axis_index("col")
    barrier = pltpu.get_barrier_semaphore()

    def greet(step, carry):
        at = lax.rem(me + step, count)
        pl.semaphore_signal(
            barrier, inc=1, device_id=(at // cols, lax.rem(at, cols)), device_id_type=MESH_ID
        )
        return carry

    lax.fori_loop(1, count, greet, 0)
    pl.semaphore_wait(barrier, count - 1)


def greet_near(rows, cols):
    i, c = lax.axis_index("row"), lax.axis_index("col")
    barrier = pltpu.get_barrier_semaphore()

    def greet_plane(step, carry):
        pl.semaphore_signal(
            barrier, inc=1, device_id=(i, lax.rem(c + step, cols)), device_id_type=MESH_ID
        )
        return carry

    def greet_line(step, carry):
        pl.semaphore_signal(
            barrier, inc=1, device_id=(lax.rem(i + step, rows), c), device_id_type=MESH_ID
        )
        return carry

    lax.fori_loop(1, cols, greet_plane, 0)
    lax.fori_loop(1, rows, greet_line, 0)
    pl.semaphore_wait(barrier, rows + cols - 2)


def sum_steps(rows, cols, x_ref, o_ref, recv, red, send_a, recv_a, send_b, recv_b, held):
    count = rows * cols
    me = lax.axis_index("row") * cols + lax.axis_index("col")

    def peer(step):
        at = lax.rem(me + step, count)
        return at, (at // cols, lax.rem(at, cols))

    def owner(at):
        return (at * x_ref.shape[1]) // held

    def scatter(step):
        at, device = peer(step)
        return pltpu.make_async_remote_copy(
            src_ref=x_ref.at[at], dst_ref=recv.at[step], send_sem=send_a.at[step],
            recv_sem=recv_a.at[step], device_id=device, device_id_type=MESH_ID,
        )

    def gather(step):
        device = peer(step)[1]
        return pltpu.make_async_remote_copy(
            src_ref=red, dst_ref=o_ref.at[me], send_sem=send_b.at[step],
            recv_sem=recv_b.at[step], device_id=device, device_id_type=MESH_ID,
        )

    def loop(action):
        def body(step, carry):
            action(step)
            return carry

        lax.fori_loop(1, count, body, 0)

    def sends(step, action):
        if held is None:
            action()
        else:
            pl.when(owner(peer(step)[0]) == me)(action)

    def first():
        loop(lambda step: sends(step, lambda: scatter(step).start()))

    def second():
        if held is None:
            def add(step, total):
                scatter(step).wait_recv()
                return total + recv[step]

            total = lax.fori_loop(1, count, add, x_ref[me])
            red[...] = total
            o_ref[me] = total
        else:
            source = owner(me)

            @pl.when(source == me)
            def _():
                red[...] = x_ref[me]
                o_ref[me] = x_ref[me]

            @pl.when(source != me)
            def _():
                step = lax.rem(me + count - source, count)
                scatter(step).wait_recv()
                red[...] = recv[step]
                o_ref[me] = recv[step]
        loop(lambda step: gather(step).start())

    def third():
        def finish(step):
            gather(step).wait_recv()
            sends(step, lambda: scatter(step).wait_send())
            gather(step).wait_send()

        loop(finish)

    return first, second, third


def sum_scratch(count, piece, width):
    return [
        pltpu.VMEM((count, piece, width), jnp.float32),
        pltpu.VMEM((piece, width), jnp.float32),
        pltpu.SemaphoreType.DMA((count,)),
        pltpu.SemaphoreType.DMA((count,)),
        pltpu.SemaphoreType.DMA((count,)),
        pltpu.SemaphoreType.DMA((count,)),
    ]


def remote(src, dst, send, recv, device):
    return pltpu.make_async_remote_copy(
        src_ref=src, dst_ref=dst, send_sem=send, recv_sem=recv, device_id=device,
        device_id_type=MESH_ID,
    )


def two(x):
    high = x.astype(jnp.bfloat16)
    return high, (x - high.astype(jnp.float32)).astype(jnp.bfloat16)


class Place:
    def __init__(self, rows, cols):
        self.rows, self.cols, self.chips = rows, cols, cols // 2
        self.i, self.c = lax.axis_index("row"), lax.axis_index("col")
        self.core = lax.rem(self.c, 2)
        self.chip = self.c // 2
        self.twin = self.c + 1 - 2 * self.core
        self.bits = self.chips.bit_length() - 1

    def stride(self, step, core):
        return (1 - core) * (1 << step) + core * (1 << (self.bits - 1 - step))

    def flip(self, chip, step, core):
        size = self.stride(step, core)
        return chip + (1 - 2 * lax.rem(chip // size, 2)) * size

    def relative(self, mask, core):
        chip = self.chip
        for step in range(self.bits):
            if mask >> step & 1:
                chip = self.flip(chip, step, core)
        return chip


class PlaneSum:
    def __init__(self, place, x, out, recv, part, red, sems):
        self.p, self.x, self.out, self.recv, self.part, self.red = place, x, out, recv, part, red
        self.sems = sems

    @staticmethod
    def scratch(rows, cols, piece, width):
        return [
            pltpu.VMEM((cols, piece, width), jnp.float32),
            pltpu.VMEM((rows, piece, width), jnp.float32),
            pltpu.VMEM((piece, width), jnp.float32),
        ] + [pltpu.SemaphoreType.DMA((cols,))] * 2 + [pltpu.SemaphoreType.DMA((rows,))] * 2 + [
            pltpu.SemaphoreType.DMA((cols,))
        ] * 2

    def scatter(self, step):
        p = self.p
        to = lax.rem(p.c + step, p.cols)
        return remote(
            self.x.at[to], self.recv.at[step], self.sems[0].at[step], self.sems[1].at[step], (p.i, to)
        )

    def across(self, step):
        p = self.p
        to = lax.rem(p.i + step, p.rows)
        return remote(
            self.part.at[0], self.part.at[step], self.sems[2].at[step], self.sems[3].at[step],
            (to, p.c),
        )

    def gather(self, step):
        p = self.p
        to = lax.rem(p.c + step, p.cols)
        return remote(
            self.red, self.out.at[p.c], self.sems[4].at[step], self.sems[5].at[step], (p.i, to)
        )

    def loop(self, count, action):
        def body(step, carry):
            action(step)
            return carry

        lax.fori_loop(1, count, body, 0)

    def begin(self):
        self.loop(self.p.cols, lambda step: self.scatter(step).start())

    def middle(self):
        def add(step, total):
            self.scatter(step).wait_recv()
            return total + self.recv[step]

        self.part[0] = lax.fori_loop(1, self.p.cols, add, self.x[self.p.c])
        self.loop(self.p.rows, lambda step: self.across(step).start())

    def late(self):
        def add(step, total):
            self.across(step).wait_recv()
            return total + self.part[step]

        total = lax.fori_loop(1, self.p.rows, add, self.part[0])
        self.red[...] = total
        self.out[self.p.c] = total
        self.loop(self.p.cols, lambda step: self.gather(step).start())

    def arrive(self):
        self.loop(self.p.cols, lambda step: self.gather(step).wait_recv())

    def finish(self):
        self.loop(self.p.cols, lambda step: self.scatter(step).wait_send())
        self.loop(self.p.cols, lambda step: self.gather(step).wait_send())
        self.loop(self.p.rows, lambda step: self.across(step).wait_send())


class RowGather:
    def __init__(self, place, x, out, sems):
        self.p, self.x, self.out, self.sems = place, x, out, sems
        p = place
        self.own = pltpu.make_async_copy(x, out.at[p.c], sems[4].at[0])

    @staticmethod
    def scratch(cols):
        chips = cols // 2
        return [pltpu.SemaphoreType.DMA((chips,))] * 4 + [pltpu.SemaphoreType.DMA((1,))]

    def hop(self, step, mask):
        p = self.p
        at = p.relative(mask, p.core) * 2 + p.core
        index = (1 << step) - 1 + mask
        to = p.flip(p.chip, step, p.core) * 2 + p.core
        return remote(
            self.out.at[at] if mask else self.x, self.out.at[at], self.sems[0].at[index],
            self.sems[1].at[index], (p.i, to),
        )

    def to_twin(self, mask):
        p = self.p
        at = p.relative(mask, p.core) * 2 + p.core
        return remote(
            self.out.at[at] if mask else self.x, self.out.at[at], self.sems[2].at[mask],
            self.sems[3].at[mask], (p.i, p.twin),
        )

    def begin(self):
        for step in range(self.p.bits):
            self.hop(step, 0).start()
        self.own.start()
        self.to_twin(0).start()

    def arrivals(self):
        return [(step, mask) for step in range(self.p.bits) for mask in range(1 << step)]

    def forward(self, step, mask):
        self.hop(step, mask).wait_recv()
        here = mask + (1 << step)
        for later in range(step + 1, self.p.bits):
            self.hop(later, here).start()
        self.to_twin(here).start()

    def finish(self):
        self.own.wait()
        for mask in range(self.p.chips):
            self.to_twin(mask).wait_recv()
        for mask in range(self.p.chips):
            self.to_twin(mask).wait_send()
        for step, mask in self.arrivals():
            self.hop(step, mask).wait_send()


class LineGather:
    def __init__(self, place, x, out, sems):
        self.p, self.x, self.out, self.sems = place, x, out, sems
        self.own = pltpu.make_async_copy(x, out.at[place.i], sems[4].at[0])

    @staticmethod
    def scratch(rows):
        return [pltpu.SemaphoreType.DMA((rows,))] * 4 + [pltpu.SemaphoreType.DMA((1,))]

    def up(self, step):
        p = self.p
        at = p.i - step
        return remote(
            self.out.at[at] if step else self.x, self.out.at[at], self.sems[0].at[step],
            self.sems[1].at[step], (p.i + 1, p.c),
        )

    def up_recv(self, step):
        p = self.p
        return remote(
            self.x, self.out.at[p.i - step], self.sems[0].at[step], self.sems[1].at[step - 1],
            (p.i - 1, p.c),
        )

    def down(self, step):
        p = self.p
        at = p.i + step
        return remote(
            self.out.at[at] if step else self.x, self.out.at[at], self.sems[2].at[step],
            self.sems[3].at[step], (p.i - 1, p.c),
        )

    def down_recv(self, step):
        p = self.p
        return remote(
            self.x, self.out.at[p.i + step], self.sems[2].at[step], self.sems[3].at[step - 1],
            (p.i + 1, p.c),
        )

    def begin(self):
        p = self.p
        pl.when(p.i + 1 < p.rows)(lambda: self.up(0).start())
        pl.when(p.i >= 1)(lambda: self.down(0).start())
        self.own.start()

    def forward(self, step):
        p = self.p

        @pl.when(p.i >= step)
        def _():
            self.up_recv(step).wait_recv()
            pl.when(p.i + 1 < p.rows)(lambda: self.up(step).start())

        @pl.when(p.i + step < p.rows)
        def _():
            self.down_recv(step).wait_recv()
            pl.when(p.i >= 1)(lambda: self.down(step).start())

    def finish(self):
        p = self.p
        for step in range(p.rows):
            pl.when((p.i >= step) & (p.i + 1 < p.rows))(lambda step=step: self.up(step).wait_send())
            pl.when((p.i + step < p.rows) & (p.i >= 1))(lambda step=step: self.down(step).wait_send())


class Spread:
    def __init__(self, place, x, out, sems):
        self.p, self.x, self.out, self.sems = place, x, out, sems
        self.per = place.cols // place.rows
        self.slot = lax.rem(place.c, place.rows)

    @staticmethod
    def scratch(rows):
        return [pltpu.SemaphoreType.DMA((rows,))] * 3

    def target(self, plane):
        return plane * self.per + self.p.c // self.p.rows

    def copy(self, plane):
        return remote(
            self.x.at[plane], self.out.at[self.slot], self.sems[0].at[plane],
            self.sems[1].at[self.slot], (self.p.i, self.target(plane)),
        )

    def local(self, plane):
        return pltpu.make_async_copy(self.x.at[plane], self.out.at[self.slot], self.sems[2].at[plane])

    def begin(self, plane):
        here = self.target(plane) == self.p.c
        pl.when(here)(lambda: self.local(plane).start())
        pl.when(jnp.logical_not(here))(lambda: self.copy(plane).start())

    def begin_next(self, step):
        p = self.p
        pl.when(p.i >= step)(lambda: self.begin(p.i - step))
        pl.when(p.i + step < p.rows)(lambda: self.begin(p.i + step))

    def finish(self):
        p = self.p
        for slot in range(p.rows):
            source = lax.rem(p.c, self.per) * p.rows + slot

            @pl.when(source != p.c)
            def _(slot=slot):
                remote(
                    self.x.at[0], self.out.at[slot], self.sems[0].at[0], self.sems[1].at[slot],
                    (p.i, p.twin),
                ).wait_recv()

        for plane in range(p.rows):
            here = self.target(plane) == p.c
            pl.when(here)(lambda plane=plane: self.local(plane).wait())
            pl.when(jnp.logical_not(here))(lambda plane=plane: self.copy(plane).wait_send())


def take(refs, *counts):
    out, at = [], 0
    for count in counts:
        out.append(refs[at:at + count])
        at += count
    return out


ANY = pl.BlockSpec(memory_space=pl.ANY)
NEAR = pl.BlockSpec(memory_space=pltpu.VMEM)


def front_kernel(rows, cols, held, top_ref, panel_ref, l_ref, diag_ref, linv_ref, a_ref,
                 out_ref, f_ref, next_ref, inv_ref, newton_ref, panel_cols, l_rows, f_rows, l_cols,
                 panel_line, l_line, *refs):
    p = Place(rows, cols)
    top_all, a_first, gram_in, gram_all, pick_in, pick_all, work, *refs = refs
    send_p, recv_p, own_sem, *refs = refs
    s_top, s_gram, s_pick, s_line, s_spread, s_lrow, s_lline, s_lspread, s_frow = take(
        refs, 6, 9, 9, 5, 3, 5, 5, 3, 5
    )
    n = inv_ref.shape[0]
    height = f_ref.shape[0]
    tops = sum_steps(rows, cols, top_ref, top_all, *s_top, held)
    grams = PlaneSum(p, gram_in, gram_all, *s_gram[:3], s_gram[3:])
    picks = PlaneSum(p, pick_in, pick_all, *s_pick[:3], s_pick[3:])
    line = LineGather(p, next_ref, panel_line, s_line)
    spread = Spread(p, panel_line, panel_cols, s_spread)
    l_row = RowGather(p, l_ref, l_rows, s_lrow)
    l_pass = LineGather(p, l_ref, l_line, s_lline)
    l_spread = Spread(p, l_line, l_cols, s_lspread)
    f_row = RowGather(p, f_ref, f_rows, s_frow)

    def piece(to):
        return remote(
            a_ref.at[pl.ds(to * height, height), pl.ds(0, n)], a_first, send_p.at[to],
            recv_p.at[0], (p.i, to),
        )

    own = pltpu.make_async_copy(a_ref.at[pl.ds(0, height), pl.ds(0, n)], a_first, own_sem.at[0])
    greet_all(rows, cols)
    tops[0]()
    across = (((1,), (1,)), ((), ()))
    along = (((0,), (0,)), ((), ()))
    linv = linv_ref[...]
    a11 = exact(exact(linv, diag_ref[...]), linv, across)
    tops[1]()

    @pl.when(p.c == 0)
    def _():
        own.start()
        for to in range(1, cols):
            piece(to).start()

    l_pass.begin()
    l_row.begin()
    half = 0.5 * exact(l_ref[...], a11)
    f_ref[...] = exact(panel_ref[...], linv, across) - half
    out_ref[...] = f_ref[...] - half
    tops[2]()
    top = top_all[...].reshape(n, 2 * n)
    l_top = top[:, n:]
    f_top = exact(top[:, :n], linv, across) - 0.5 * exact(l_top, a11)
    l_pass.forward(1)

    @pl.when(p.c == 0)
    def _():
        own.wait()
        for to in range(1, cols):
            piece(to).wait_send()

    @pl.when(p.c != 0)
    def _():
        piece(1).wait_recv()

    if rows > 2:
        l_pass.forward(2)
    me = p.i * cols + p.c
    at = me * height + lax.broadcasted_iota(jnp.int32, (height, n), 0)
    panel = a_first[...] - exact(f_ref[...], l_top, across) - exact(l_ref[...], f_top, across)
    panel = jnp.where(at >= n, panel, 0.0)
    next_ref[...] = panel
    picker = (at - n == lax.broadcasted_iota(jnp.int32, (height, n), 1)).astype(jnp.float32)
    gram = exact(panel, panel, along)
    pick = exact(picker, panel, along)
    deep = n // cols
    for at in range(cols):
        rows_at = slice(at * deep, (at + 1) * deep)
        gram_in[at] = gram[rows_at]
        pick_in[at] = pick[rows_at]
    grams.begin()
    picks.begin()
    arrivals = l_row.arrivals()
    l_row.forward(*arrivals[0])
    grams.middle()
    picks.middle()
    line.begin()
    for step in range(3, rows):
        l_pass.forward(step)
    grams.late()
    picks.late()
    l_pass.own.wait()
    for plane in range(rows):
        l_spread.begin(plane)
    line.own.wait()
    spread.begin(p.i)
    grams.arrive()
    work[:, :n] = gram_all[...].reshape(n, n)
    work[:, n:] = unit(n)
    todo = [lambda: line.forward(1), lambda: spread.begin_next(1)]
    todo += [lambda a=a: l_row.forward(*a) for a in arrivals[1:]]
    todo += [f_row.begin]
    for step in range(2, rows):
        todo += [lambda step=step: line.forward(step), lambda step=step: spread.begin_next(step)]
    todo += [lambda: f_row.forward(*arrivals[0])]
    pieces = 8
    panels = n // 8 // pieces
    for part in range(pieces):
        eliminate(work, n, part * panels, (part + 1) * panels)
        for at, act in enumerate(todo):
            if at * pieces // len(todo) == part:
                act()
    inverse = work[:, n:]
    inv_ref[...] = inverse
    picks.arrive()
    top_panel = pick_all[...].reshape(n, n)
    newton_ref[...] = newton_product(exact(top_panel, inverse, across))
    for arrival in arrivals[1:]:
        f_row.forward(*arrival)
    l_row.finish()
    l_spread.finish()
    spread.finish()
    f_row.finish()
    line.finish()
    l_pass.finish()
    grams.finish()
    picks.finish()


def front(rows, cols, top, held, a_panel, l_panel, a_diag, l_inverse, a_trail, ident):
    height, n = a_panel.shape
    count = rows * cols
    small, deep = n // count, n // cols

    def f32(*shape):
        return jax.ShapeDtypeStruct(shape, jnp.float32)

    outs = [
        f32(height, n), f32(height, n), f32(height, n), f32(n, n), f32(n, n),
        f32(rows, height, n), f32(cols, height, n), f32(cols, height, n), f32(rows, height, n),
        f32(rows, height, n), f32(rows, height, n),
    ]
    dma = pltpu.SemaphoreType.DMA
    scratch = [
        pltpu.VMEM((count, small, 2 * n), jnp.float32), pltpu.VMEM((height, n), jnp.float32),
    ] + [pltpu.VMEM((cols, deep, n), jnp.float32)] * 4 + [
        pltpu.VMEM((n, 2 * n), jnp.float32), dma((cols,)), dma((1,)), dma((1,)),
    ] + sum_scratch(count, small, 2 * n) + PlaneSum.scratch(rows, cols, deep, n) * 2
    scratch += LineGather.scratch(rows) + Spread.scratch(rows) + RowGather.scratch(cols)
    scratch += LineGather.scratch(rows) + Spread.scratch(rows) + RowGather.scratch(cols)
    return pl.pallas_call(
        functools.partial(front_kernel, rows, cols, held),
        out_shape=outs,
        in_specs=[NEAR, NEAR, NEAR, NEAR, NEAR, ANY],
        out_specs=[NEAR] * 5 + [ANY] * 6,
        scratch_shapes=scratch,
        compiler_params=pltpu.CompilerParams(collective_id=ident, has_side_effects=True),
    )(top.reshape(count, small, 2 * n), a_panel, l_panel, a_diag, l_inverse, a_trail)


def image_kernel(rows, cols, cross_ref, a_ref, refl_ref, f_ref, y_ref, image_ref, total_ref, f_cols,
                 y_rows, f_line, tiles, high, low, mine, twin_in, hop_in, *refs):
    p = Place(rows, cols)
    tile_sem, twin_send, twin_recv, hop_send, hop_recv, *refs = refs
    s_sum, s_fline, s_fspread, s_y = take(refs, 9, 5, 3, 5)
    gather_y = RowGather(p, y_ref, y_rows, s_y)
    height, _ = image_ref.shape
    chips = p.chips
    sums = PlaneSum(p, cross_ref, total_ref, *s_sum[:3], s_sum[3:])
    f_pass = LineGather(p, f_ref, f_line, s_fline)
    f_spread = Spread(p, f_line, f_cols, s_fspread)
    masks = sorted(range(1, chips), key=lambda m: (m & -m, m)) + [0]
    other = 1 - p.core

    def piece_col(step):
        index = step // 2
        if step % 2:
            return p.relative(masks[index], p.core) * 2 + p.core
        return p.relative(masks[index], other) * 2 + other

    def load(step):
        at = pl.multiple_of(piece_col(step) * height, 8)
        return pltpu.make_async_copy(
            a_ref.at[pl.ds(at, height), :], tiles.at[step % 2], tile_sem.at[step % 2]
        )

    def to_twin(index):
        return remote(
            mine.at[2 * index], twin_in.at[index], twin_send.at[index], twin_recv.at[index],
            (p.i, p.twin),
        )

    hops = [(step, m) for step in range(p.bits) for m in range(chips) if m % (2 << step) == 0]
    number = {key: at for at, key in enumerate(hops)}

    def hop(step, mask):
        index = number[(step, mask)]
        to = p.flip(p.chip, step, p.core) * 2 + p.core
        return remote(
            mine.at[2 * masks.index(mask + (1 << step)) + 1], hop_in.at[index], hop_send.at[index],
            hop_recv.at[index], (p.i, to),
        )

    greet_near(rows, cols)
    load(0).start()
    sums.begin()
    high[...], low[...] = two(refl_ref[...])
    depth = high.shape[0]
    chunk = min(depth, 512)

    def multiply(slot, at):
        total = None
        for k in range(depth // chunk):
            a_high, a_low = two(tiles[slot, :, k * chunk:(k + 1) * chunk])
            y_high, y_low = high[k * chunk:(k + 1) * chunk, :], low[k * chunk:(k + 1) * chunk, :]
            dot = functools.partial(jnp.dot, preferred_element_type=jnp.float32)
            now = dot(a_high, y_high) + (dot(a_high, y_low) + dot(a_low, y_high))
            total = now if total is None else total + now
        mine[at] = total

    for step in range(2 * chips):
        if step + 1 < 2 * chips:
            load(step + 1).start()
        load(step).wait()
        multiply(step % 2, step)
        index = step // 2
        if step % 2 == 0:
            to_twin(index).start()
        else:
            mask = masks[index]
            low_bit = p.bits if mask == 0 else (mask & -mask).bit_length() - 1
            to_twin(index).wait_recv()
            value = mine[step] + twin_in[index]
            for t in range(low_bit):
                hop(t, mask).wait_recv()
                value = value + hop_in[number[(t, mask)]]
            if mask:
                mine[step] = value
                hop(low_bit, mask - (1 << low_bit)).start()
            else:
                image_ref[...] = value
        if step == 1:
            sums.middle()
            f_pass.begin()
        if step == 3:
            sums.late()
        if step == 2 * chips - 2:
            f_pass.own.wait()
            f_spread.begin(p.i)
            f_pass.forward(1)
            f_spread.begin_next(1)
        if step == 2 * chips - 3:
            gather_y.begin()
    for at, arrival in enumerate(gather_y.arrivals()):
        gather_y.forward(*arrival)
        if at == 0 and rows > 2:
            f_pass.forward(2)
            f_spread.begin_next(2)
    for later in range(3, rows):
        f_pass.forward(later)
        f_spread.begin_next(later)
    sums.arrive()
    sums.finish()
    gather_y.finish()
    for index in range(chips):
        to_twin(index).wait_send()
    for step, mask in hops:
        hop(step, mask).wait_send()
    f_pass.finish()
    f_spread.finish()


def image(rows, cols, cross, a_trail, refl_cols, first_y, refl, ident):
    width, n = cross.shape
    piece = width // cols
    wide = a_trail.shape[1]
    height = refl.shape[0]
    chips = cols // 2
    outs = [
        jax.ShapeDtypeStruct((height, n), jnp.float32),
        jax.ShapeDtypeStruct((cols, piece, n), jnp.float32),
        jax.ShapeDtypeStruct((rows, height, n), jnp.float32),
        jax.ShapeDtypeStruct((cols, height, n), jnp.float32),
        jax.ShapeDtypeStruct((rows, height, n), jnp.float32),
    ]
    dma = pltpu.SemaphoreType.DMA
    scratch = [
        pltpu.VMEM((2, height, wide), jnp.float32), pltpu.VMEM((wide, n), jnp.bfloat16),
        pltpu.VMEM((wide, n), jnp.bfloat16), pltpu.VMEM((cols, height, n), jnp.float32),
        pltpu.VMEM((chips, height, n), jnp.float32), pltpu.VMEM((chips, height, n), jnp.float32),
        dma((2,)), dma((chips,)), dma((chips,)), dma((chips,)), dma((chips,)),
    ] + PlaneSum.scratch(rows, cols, piece, n) + LineGather.scratch(rows)
    scratch += Spread.scratch(rows) + RowGather.scratch(cols)
    result, total, f_cols, y_rows, _ = pl.pallas_call(
        functools.partial(image_kernel, rows, cols),
        out_shape=outs,
        in_specs=[NEAR, ANY, NEAR, ANY, ANY],
        out_specs=[NEAR, NEAR, ANY, ANY, ANY],
        scratch_shapes=scratch,
        compiler_params=pltpu.CompilerParams(collective_id=ident, has_side_effects=True),
    )(cross.reshape(cols, piece, n), a_trail, refl_cols, first_y, refl)
    return result, total.reshape(width, n), f_cols.reshape(-1, n), y_rows.reshape(-1, n)


def update_kernel(rows, cols, core_ref, a_ref, l_cols, f_cols, f_rows, l_rows, x_ref, out_ref,
                  total_ref, x_cols, x_rows, x_line, tiles, sides, results, high, low, *refs):
    p = Place(rows, cols)
    tile_sem, side_sem, out_sem, *refs = refs
    s_sum, s_line, s_spread, s_x = take(refs, 9, 5, 3, 5)
    sums = PlaneSum(p, core_ref, total_ref, *s_sum[:3], s_sum[3:])
    line = LineGather(p, x_ref, x_line, s_line)
    spread = Spread(p, x_line, x_cols, s_spread)
    gather_x = RowGather(p, x_ref, x_rows, s_x)
    height, n = f_rows.shape[1:]

    def load(step):
        slot = lax.rem(step, 2)
        return (
            pltpu.make_async_copy(
                a_ref.at[pl.ds(pl.multiple_of(step * height, 8), height), :], tiles.at[slot],
                tile_sem.at[slot],
            ),
            pltpu.make_async_copy(f_rows.at[step], sides.at[slot, 0], side_sem.at[0, slot]),
            pltpu.make_async_copy(l_rows.at[step], sides.at[slot, 1], side_sem.at[1, slot]),
        )

    def store(step):
        slot = lax.rem(step, 2)
        return pltpu.make_async_copy(
            results.at[slot], out_ref.at[pl.ds(pl.multiple_of(step * height, 8), height), :],
            out_sem.at[slot],
        )

    greet_near(rows, cols)
    for copy in load(0):
        copy.start()
    sums.begin()
    line.begin()
    gather_x.begin()
    high[:, :n], low[:, :n] = two(l_cols[...])
    high[:, n:], low[:, n:] = two(f_cols[...])
    last = cols - 1
    chunk = min(high.shape[0], 512)

    def body(step, carry):
        @pl.when(step < last)
        def _():
            for copy in load(step + 1):
                copy.start()

        for copy in load(step):
            copy.wait()

        @pl.when(step >= 2)
        def _():
            store(step - 2).wait()

        slot = lax.rem(step, 2)
        f_high, f_low = two(sides[slot, 0])
        l_high, l_low = two(sides[slot, 1])

        def dot(left, right):
            return lax.dot_general(
                left, right, (((1,), (1,)), ((), ())), preferred_element_type=jnp.float32
            )

        for k in range(high.shape[0] // chunk):
            at = slice(k * chunk, (k + 1) * chunk)
            with_l, with_f = high[at, :n], high[at, n:]
            results[slot, :, at] = tiles[slot, :, at] - (
                (dot(f_high, with_l) + dot(l_high, with_f))
                + (dot(f_high, low[at, :n]) + dot(f_low, with_l))
                + (dot(l_high, low[at, n:]) + dot(l_low, with_f))
            )
        store(step).start()

        actions = {}

        def put(when, action):
            actions.setdefault(min(when, last), []).append(action)

        def spread_own():
            line.own.wait()
            spread.begin(p.i)

        put(0, spread_own)
        put(1, sums.middle)
        for hop in range(1, rows):
            put(2 * hop + hop // 3, lambda hop=hop: line.forward(hop))
            put(2 * hop + hop // 3, lambda hop=hop: spread.begin_next(hop))
        for index, arrival in enumerate(gather_x.arrivals()):
            put(2 + 2 * index, lambda arrival=arrival: gather_x.forward(*arrival))
        put(4, sums.late)
        for when, todo in actions.items():
            @pl.when(step == when)
            def _(todo=todo):
                for action in todo:
                    action()
        return carry

    lax.fori_loop(0, cols, body, 0)
    sums.arrive()
    sums.finish()
    gather_x.finish()
    spread.finish()
    line.finish()
    for step in range(max(cols - 2, 0), cols):
        store(step).wait()


def update(rows, cols, core, a_trail, l_cols, f_cols, f_rows, l_rows, x, ident):
    n = core.shape[0]
    piece = n // cols
    height = x.shape[0]
    wide = a_trail.shape[1]
    outs = [
        jax.ShapeDtypeStruct(a_trail.shape, jnp.float32),
        jax.ShapeDtypeStruct((cols, piece, n), jnp.float32),
        jax.ShapeDtypeStruct((rows, height, n), jnp.float32),
        jax.ShapeDtypeStruct((cols, height, n), jnp.float32),
        jax.ShapeDtypeStruct((rows, height, n), jnp.float32),
    ]
    dma = pltpu.SemaphoreType.DMA
    scratch = [
        pltpu.VMEM((2, height, wide), jnp.float32), pltpu.VMEM((2, 2, height, n), jnp.float32),
        pltpu.VMEM((2, height, wide), jnp.float32), pltpu.VMEM((wide, 2 * n), jnp.bfloat16),
        pltpu.VMEM((wide, 2 * n), jnp.bfloat16), dma((2,)), dma((2, 2)), dma((2,)),
    ] + PlaneSum.scratch(rows, cols, piece, n) + LineGather.scratch(rows)
    scratch += Spread.scratch(rows) + RowGather.scratch(cols)
    updated, total, x_cols, x_rows, _ = pl.pallas_call(
        functools.partial(update_kernel, rows, cols),
        out_shape=outs,
        in_specs=[NEAR, ANY, NEAR, NEAR, ANY, ANY, ANY],
        out_specs=[ANY, NEAR, ANY, ANY, ANY],
        scratch_shapes=scratch,
        compiler_params=pltpu.CompilerParams(collective_id=ident, has_side_effects=True),
    )(core.reshape(cols, piece, n), a_trail, l_cols, f_cols, f_rows, l_rows, x)
    return updated, total.reshape(n, n), x_cols.reshape(-1, n), x_rows.reshape(-1, n)


def shards(rows, cols, a_trail, a_panel, l_panel, a_diag, l_inverse):
    height, block_width = a_panel.shape
    me = lax.axis_index("row") * cols + lax.axis_index("col")
    tall = min(height, block_width)
    top = jnp.concatenate((a_panel[:tall], l_panel[:tall]), axis=1)
    (panel_out, first_y, next_panel, inverse, newton, panel_cols, l_rows, f_rows, l_cols, _,
     _) = front(
        rows, cols, jnp.concatenate([top] * (block_width // tall), axis=0), tall, a_panel, l_panel,
        a_diag, l_inverse, a_trail, 0,
    )
    panel_cols, l_cols = panel_cols.reshape(-1, block_width), l_cols.reshape(-1, block_width)

    def picker(at):
        return (at[:, None] - block_width == lax.iota(jnp.int32, block_width)[None, :]).astype(
            jnp.float32
        )

    wide = a_trail.shape[1]
    refl = large_product(next_panel, inverse.T) + picker(me * height + lax.iota(jnp.int32, height))
    refl_cols = large_product(panel_cols, inverse.T) + picker(
        lax.axis_index("col") * wide + lax.iota(jnp.int32, wide)
    )
    image_shard, cross, f_cols, refl_rows = image(
        rows, cols,
        jnp.concatenate((large_product(first_y.T, refl), large_product(l_panel.T, refl)), axis=0),
        a_trail, refl_cols, first_y, refl, 2,
    )
    x_shard = product(
        image_shard - large_product(first_y, cross[block_width:])
        - large_product(l_panel, cross[:block_width]),
        newton.T,
    )
    updated, core_sum, x_cols, x_rows = update(
        rows, cols, large_product(refl.T, x_shard), a_trail, l_cols, f_cols, f_rows, l_rows, x_shard, 3
    )
    half_core = 0.5 * product(newton, core_sum)
    z_cols = x_cols - large_product(refl_cols, half_core + half_core.T)
    trail_out = updated - large_product(
        jnp.concatenate((x_rows, refl_rows), axis=1),
        jnp.concatenate((refl_cols, z_cols), axis=1).T,
    )
    return (trail_out, panel_out)


def layer(rows, cols, *args):
    return shards(rows, cols, *args)


def solution(mesh):
    rows, cols = mesh.shape["row"], mesh.shape["col"]
    return jax.shard_map(
        functools.partial(layer, rows, cols),
        mesh=mesh,
        in_specs=(P("row", "col"), P(BOTH, None), P(BOTH, None), P(), P()),
        out_specs=(P("row", "col"), P(BOTH, None)),
        check_vma=False,
    )
```

```python
import functools

import jax
import jax.numpy as jnp
from jax import lax
from jax.experimental import pallas as pl
from jax.experimental.pallas import tpu as pltpu
from jax.sharding import PartitionSpec as P

NS_STEPS = 8
BOTH = ("row", "col")
MESH_ID = pl.DeviceIdType.MESH


def product(left, right):
    return jnp.dot(left, right, precision=lax.Precision.HIGHEST, preferred_element_type=jnp.float32)


def large_product(left, right):
    return jnp.dot(left, right, precision=lax.Precision.HIGH, preferred_element_type=jnp.float32)


def exact(left, right, dims=(((1,), (0,)), ((), ()))):
    return lax.dot_general(left, right, dims, precision=lax.Precision.HIGHEST, preferred_element_type=jnp.float32)


def three(x):
    high = x.astype(jnp.bfloat16).astype(jnp.float32)
    rest = x - high
    mid = rest.astype(jnp.bfloat16).astype(jnp.float32)
    return high, mid, rest - mid


def sub_block(V, lanes_at, n, W):
    row = lax.broadcasted_iota(jnp.int32, (8, 128), 0)
    shifted = pltpu.roll(V[:, :n], n - lanes_at, 1)[:, :128]
    cols = [jnp.broadcast_to(shifted[:, j:j+1], (8, 128)) for j in range(8)]
    vs = [V[:, 128*t:128*(t+1)] for t in range(W//128)]
    for j in range(8):
        r = lax.rsqrt(cols[j][j:j+1, :])
        r = r * (1.5 - 0.5 * cols[j][j:j+1, :] * r * r)
        lj = jnp.where(row > j, cols[j] * r, 0.0)
        sc = jnp.where(row == j, jnp.broadcast_to(r, (8,128)), 1.0)
        for k in range(j+1, 8):
            cols[k] = cols[k] - lj * lj[k:k+1, :]
        for t in range(len(vs)):
            top = vs[t][j:j+1, :] * r
            vs[t] = jnp.where(row == j, jnp.broadcast_to(top, (8,128)), vs[t] - lj * top)
    return jnp.concatenate(vs, axis=1)


def eliminate(work, n, begin, end):
    lane = lax.broadcasted_iota(jnp.int32, (8, n), 1)

    def body(b, carry):
        k0 = pl.multiple_of(b * 8, 8)
        V = sub_block(work[pl.ds(k0, 8), :], k0, n, 2 * n)
        work[pl.ds(k0, 8), :] = V
        h, m, l = three(jnp.where(lane >= k0 + 8, V[:, :n], 0.0))
        hr, mr, lr = three(V)
        lhs = jnp.concatenate([h, h, m, h, m, l], axis=0).astype(jnp.bfloat16)
        rhs = jnp.concatenate([hr, mr, hr, lr, mr, hr], axis=0).astype(jnp.bfloat16)
        work[...] -= lax.dot_general(
            lhs, rhs, (((0,), (0,)), ((), ())), preferred_element_type=jnp.float32
        )
        return carry

    lax.fori_loop(begin, end, body, 0)


def unit(n):
    return (
        lax.broadcasted_iota(jnp.int32, (n, n), 0) == lax.broadcasted_iota(jnp.int32, (n, n), 1)
    ).astype(jnp.float32)


def newton_product(q_top):
    rem = -q_top
    approx = unit(q_top.shape[0]) + rem
    for _ in range(NS_STEPS - 1):
        rem = exact(rem, rem)
        approx = approx + exact(approx, rem)
    return approx


def greet_all(rows, cols):
    count = rows * cols
    me = lax.axis_index("row") * cols + lax.axis_index("col")
    barrier = pltpu.get_barrier_semaphore()

    def greet(step, carry):
        at = lax.rem(me + step, count)
        pl.semaphore_signal(
            barrier, inc=1, device_id=(at // cols, lax.rem(at, cols)), device_id_type=MESH_ID
        )
        return carry

    lax.fori_loop(1, count, greet, 0)
    pl.semaphore_wait(barrier, count - 1)


def greet_near(rows, cols):
    i, c = lax.axis_index("row"), lax.axis_index("col")
    barrier = pltpu.get_barrier_semaphore()

    def greet_plane(step, carry):
        pl.semaphore_signal(
            barrier, inc=1, device_id=(i, lax.rem(c + step, cols)), device_id_type=MESH_ID
        )
        return carry

    def greet_line(step, carry):
        pl.semaphore_signal(
            barrier, inc=1, device_id=(lax.rem(i + step, rows), c), device_id_type=MESH_ID
        )
        return carry

    lax.fori_loop(1, cols, greet_plane, 0)
    lax.fori_loop(1, rows, greet_line, 0)
    pl.semaphore_wait(barrier, rows + cols - 2)


def sum_steps(rows, cols, x_ref, o_ref, recv, red, send_a, recv_a, send_b, recv_b, held):
    count = rows * cols
    me = lax.axis_index("row") * cols + lax.axis_index("col")

    def peer(step):
        at = lax.rem(me + step, count)
        return at, (at // cols, lax.rem(at, cols))

    def owner(at):
        return (at * x_ref.shape[1]) // held

    def scatter(step):
        at, device = peer(step)
        return pltpu.make_async_remote_copy(
            src_ref=x_ref.at[at], dst_ref=recv.at[step], send_sem=send_a.at[step],
            recv_sem=recv_a.at[step], device_id=device, device_id_type=MESH_ID,
        )

    def gather(step):
        device = peer(step)[1]
        return pltpu.make_async_remote_copy(
            src_ref=red, dst_ref=o_ref.at[me], send_sem=send_b.at[step],
            recv_sem=recv_b.at[step], device_id=device, device_id_type=MESH_ID,
        )

    def loop(action):
        def body(step, carry):
            action(step)
            return carry

        lax.fori_loop(1, count, body, 0)

    def sends(step, action):
        if held is None:
            action()
        else:
            pl.when(owner(peer(step)[0]) == me)(action)

    def first():
        loop(lambda step: sends(step, lambda: scatter(step).start()))

    def second():
        if held is None:
            def add(step, total):
                scatter(step).wait_recv()
                return total + recv[step]

            total = lax.fori_loop(1, count, add, x_ref[me])
            red[...] = total
            o_ref[me] = total
        else:
            source = owner(me)

            @pl.when(source == me)
            def _():
                red[...] = x_ref[me]
                o_ref[me] = x_ref[me]

            @pl.when(source != me)
            def _():
                step = lax.rem(me + count - source, count)
                scatter(step).wait_recv()
                red[...] = recv[step]
                o_ref[me] = recv[step]
        loop(lambda step: gather(step).start())

    def third():
        def finish(step):
            gather(step).wait_recv()
            sends(step, lambda: scatter(step).wait_send())
            gather(step).wait_send()

        loop(finish)

    return first, second, third


def sum_scratch(count, piece, width):
    return [
        pltpu.VMEM((count, piece, width), jnp.float32),
        pltpu.VMEM((piece, width), jnp.float32),
        pltpu.SemaphoreType.DMA((count,)),
        pltpu.SemaphoreType.DMA((count,)),
        pltpu.SemaphoreType.DMA((count,)),
        pltpu.SemaphoreType.DMA((count,)),
    ]


def remote(src, dst, send, recv, device):
    return pltpu.make_async_remote_copy(
        src_ref=src, dst_ref=dst, send_sem=send, recv_sem=recv, device_id=device,
        device_id_type=MESH_ID,
    )


def two(x):
    high = x.astype(jnp.bfloat16)
    return high, (x - high.astype(jnp.float32)).astype(jnp.bfloat16)


class Place:
    def __init__(self, rows, cols):
        self.rows, self.cols, self.chips = rows, cols, cols // 2
        self.i, self.c = lax.axis_index("row"), lax.axis_index("col")
        self.core = lax.rem(self.c, 2)
        self.chip = self.c // 2
        self.twin = self.c + 1 - 2 * self.core
        self.bits = self.chips.bit_length() - 1

    def stride(self, step, core):
        return (1 - core) * (1 << step) + core * (1 << (self.bits - 1 - step))

    def flip(self, chip, step, core):
        size = self.stride(step, core)
        return chip + (1 - 2 * lax.rem(chip // size, 2)) * size

    def relative(self, mask, core):
        chip = self.chip
        for step in range(self.bits):
            if mask >> step & 1:
                chip = self.flip(chip, step, core)
        return chip


class PlaneSum:
    def __init__(self, place, x, out, recv, part, red, sems):
        self.p, self.x, self.out, self.recv, self.part, self.red = place, x, out, recv, part, red
        self.sems = sems

    @staticmethod
    def scratch(rows, cols, piece, width):
        return [
            pltpu.VMEM((cols, piece, width), jnp.float32),
            pltpu.VMEM((rows, piece, width), jnp.float32),
            pltpu.VMEM((piece, width), jnp.float32),
        ] + [pltpu.SemaphoreType.DMA((cols,))] * 2 + [pltpu.SemaphoreType.DMA((rows,))] * 2 + [
            pltpu.SemaphoreType.DMA((cols,))
        ] * 2

    def scatter(self, step):
        p = self.p
        to = lax.rem(p.c + step, p.cols)
        return remote(
            self.x.at[to], self.recv.at[step], self.sems[0].at[step], self.sems[1].at[step], (p.i, to)
        )

    def across(self, step):
        p = self.p
        to = lax.rem(p.i + step, p.rows)
        return remote(
            self.part.at[0], self.part.at[step], self.sems[2].at[step], self.sems[3].at[step],
            (to, p.c),
        )

    def gather(self, step):
        p = self.p
        to = lax.rem(p.c + step, p.cols)
        return remote(
            self.red, self.out.at[p.c], self.sems[4].at[step], self.sems[5].at[step], (p.i, to)
        )

    def loop(self, count, action):
        def body(step, carry):
            action(step)
            return carry

        lax.fori_loop(1, count, body, 0)

    def begin(self):
        self.loop(self.p.cols, lambda step: self.scatter(step).start())

    def middle(self):
        def add(step, total):
            self.scatter(step).wait_recv()
            return total + self.recv[step]

        self.part[0] = lax.fori_loop(1, self.p.cols, add, self.x[self.p.c])
        self.loop(self.p.rows, lambda step: self.across(step).start())

    def late(self):
        def add(step, total):
            self.across(step).wait_recv()
            return total + self.part[step]

        total = lax.fori_loop(1, self.p.rows, add, self.part[0])
        self.red[...] = total
        self.out[self.p.c] = total
        self.loop(self.p.cols, lambda step: self.gather(step).start())

    def arrive(self):
        self.loop(self.p.cols, lambda step: self.gather(step).wait_recv())

    def finish(self):
        self.loop(self.p.cols, lambda step: self.scatter(step).wait_send())
        self.loop(self.p.cols, lambda step: self.gather(step).wait_send())
        self.loop(self.p.rows, lambda step: self.across(step).wait_send())


class RowGather:
    def __init__(self, place, x, out, sems):
        self.p, self.x, self.out, self.sems = place, x, out, sems
        p = place
        self.own = pltpu.make_async_copy(x, out.at[p.c], sems[4].at[0])

    @staticmethod
    def scratch(cols):
        chips = cols // 2
        return [pltpu.SemaphoreType.DMA((chips,))] * 4 + [pltpu.SemaphoreType.DMA((1,))]

    def hop(self, step, mask):
        p = self.p
        at = p.relative(mask, p.core) * 2 + p.core
        index = (1 << step) - 1 + mask
        to = p.flip(p.chip, step, p.core) * 2 + p.core
        return remote(
            self.out.at[at] if mask else self.x, self.out.at[at], self.sems[0].at[index],
            self.sems[1].at[index], (p.i, to),
        )

    def to_twin(self, mask):
        p = self.p
        at = p.relative(mask, p.core) * 2 + p.core
        return remote(
            self.out.at[at] if mask else self.x, self.out.at[at], self.sems[2].at[mask],
            self.sems[3].at[mask], (p.i, p.twin),
        )

    def begin(self):
        for step in range(self.p.bits):
            self.hop(step, 0).start()
        self.own.start()
        self.to_twin(0).start()

    def arrivals(self):
        return [(step, mask) for step in range(self.p.bits) for mask in range(1 << step)]

    def forward(self, step, mask):
        self.hop(step, mask).wait_recv()
        here = mask + (1 << step)
        for later in range(step + 1, self.p.bits):
            self.hop(later, here).start()
        self.to_twin(here).start()

    def finish(self):
        self.own.wait()
        for mask in range(self.p.chips):
            self.to_twin(mask).wait_recv()
        for mask in range(self.p.chips):
            self.to_twin(mask).wait_send()
        for step, mask in self.arrivals():
            self.hop(step, mask).wait_send()


class LineGather:
    def __init__(self, place, x, out, sems):
        self.p, self.x, self.out, self.sems = place, x, out, sems
        self.own = pltpu.make_async_copy(x, out.at[place.i], sems[4].at[0])

    @staticmethod
    def scratch(rows):
        return [pltpu.SemaphoreType.DMA((rows,))] * 4 + [pltpu.SemaphoreType.DMA((1,))]

    def up(self, step):
        p = self.p
        at = p.i - step
        return remote(
            self.out.at[at] if step else self.x, self.out.at[at], self.sems[0].at[step],
            self.sems[1].at[step], (p.i + 1, p.c),
        )

    def up_recv(self, step):
        p = self.p
        return remote(
            self.x, self.out.at[p.i - step], self.sems[0].at[step], self.sems[1].at[step - 1],
            (p.i - 1, p.c),
        )

    def down(self, step):
        p = self.p
        at = p.i + step
        return remote(
            self.out.at[at] if step else self.x, self.out.at[at], self.sems[2].at[step],
            self.sems[3].at[step], (p.i - 1, p.c),
        )

    def down_recv(self, step):
        p = self.p
        return remote(
            self.x, self.out.at[p.i + step], self.sems[2].at[step], self.sems[3].at[step - 1],
            (p.i + 1, p.c),
        )

    def begin(self):
        p = self.p
        pl.when(p.i + 1 < p.rows)(lambda: self.up(0).start())
        pl.when(p.i >= 1)(lambda: self.down(0).start())
        self.own.start()

    def forward(self, step):
        p = self.p

        @pl.when(p.i >= step)
        def _():
            self.up_recv(step).wait_recv()
            pl.when(p.i + 1 < p.rows)(lambda: self.up(step).start())

        @pl.when(p.i + step < p.rows)
        def _():
            self.down_recv(step).wait_recv()
            pl.when(p.i >= 1)(lambda: self.down(step).start())

    def finish(self):
        p = self.p
        for step in range(p.rows):
            pl.when((p.i >= step) & (p.i + 1 < p.rows))(lambda step=step: self.up(step).wait_send())
            pl.when((p.i + step < p.rows) & (p.i >= 1))(lambda step=step: self.down(step).wait_send())


class Spread:
    def __init__(self, place, x, out, sems):
        self.p, self.x, self.out, self.sems = place, x, out, sems
        self.per = place.cols // place.rows
        self.slot = lax.rem(place.c, place.rows)

    @staticmethod
    def scratch(rows):
        return [pltpu.SemaphoreType.DMA((rows,))] * 3

    def target(self, plane):
        return plane * self.per + self.p.c // self.p.rows

    def copy(self, plane):
        return remote(
            self.x.at[plane], self.out.at[self.slot], self.sems[0].at[plane],
            self.sems[1].at[self.slot], (self.p.i, self.target(plane)),
        )

    def local(self, plane):
        return pltpu.make_async_copy(self.x.at[plane], self.out.at[self.slot], self.sems[2].at[plane])

    def begin(self, plane):
        here = self.target(plane) == self.p.c
        pl.when(here)(lambda: self.local(plane).start())
        pl.when(jnp.logical_not(here))(lambda: self.copy(plane).start())

    def begin_next(self, step):
        p = self.p
        pl.when(p.i >= step)(lambda: self.begin(p.i - step))
        pl.when(p.i + step < p.rows)(lambda: self.begin(p.i + step))

    def finish(self):
        p = self.p
        for slot in range(p.rows):
            source = lax.rem(p.c, self.per) * p.rows + slot

            @pl.when(source != p.c)
            def _(slot=slot):
                remote(
                    self.x.at[0], self.out.at[slot], self.sems[0].at[0], self.sems[1].at[slot],
                    (p.i, p.twin),
                ).wait_recv()

        for plane in range(p.rows):
            here = self.target(plane) == p.c
            pl.when(here)(lambda plane=plane: self.local(plane).wait())
            pl.when(jnp.logical_not(here))(lambda plane=plane: self.copy(plane).wait_send())


def take(refs, *counts):
    out, at = [], 0
    for count in counts:
        out.append(refs[at:at + count])
        at += count
    return out


ANY = pl.BlockSpec(memory_space=pl.ANY)
NEAR = pl.BlockSpec(memory_space=pltpu.VMEM)


def front_kernel(rows, cols, held, top_ref, panel_ref, l_ref, diag_ref, linv_ref, a_ref,
                 out_ref, f_ref, next_ref, inv_ref, newton_ref, panel_cols, l_rows, f_rows, l_cols,
                 *refs):
    p = Place(rows, cols)
    panel_line, l_line, top_all, a_first, gram_in, gram_all, pick_in, pick_all, work, *refs = refs
    send_p, recv_p, own_sem, *refs = refs
    s_top, s_gram, s_pick, s_line, s_spread, s_lrow, s_lline, s_lspread, s_frow = take(
        refs, 6, 9, 9, 5, 3, 5, 5, 3, 5
    )
    n = inv_ref.shape[0]
    height = f_ref.shape[0]
    tops = sum_steps(rows, cols, top_ref, top_all, *s_top, held)
    grams = PlaneSum(p, gram_in, gram_all, *s_gram[:3], s_gram[3:])
    picks = PlaneSum(p, pick_in, pick_all, *s_pick[:3], s_pick[3:])
    line = LineGather(p, next_ref, panel_line, s_line)
    spread = Spread(p, panel_line, panel_cols, s_spread)
    l_row = RowGather(p, l_ref, l_rows, s_lrow)
    l_pass = LineGather(p, l_ref, l_line, s_lline)
    l_spread = Spread(p, l_line, l_cols, s_lspread)
    f_row = RowGather(p, f_ref, f_rows, s_frow)

    def piece(to):
        return remote(
            a_ref.at[pl.ds(to * height, height), pl.ds(0, n)], a_first, send_p.at[to],
            recv_p.at[0], (p.i, to),
        )

    own = pltpu.make_async_copy(a_ref.at[pl.ds(0, height), pl.ds(0, n)], a_first, own_sem.at[0])
    greet_all(rows, cols)
    tops[0]()
    across = (((1,), (1,)), ((), ()))
    along = (((0,), (0,)), ((), ()))
    linv = linv_ref[...]
    a11 = exact(exact(linv, diag_ref[...]), linv, across)
    tops[1]()

    @pl.when(p.c == 0)
    def _():
        own.start()
        for to in range(1, cols):
            piece(to).start()

    l_pass.begin()
    l_row.begin()
    half = 0.5 * exact(l_ref[...], a11)
    f_ref[...] = exact(panel_ref[...], linv, across) - half
    out_ref[...] = f_ref[...] - half
    tops[2]()
    top = top_all[...].reshape(n, 2 * n)
    l_top = top[:, n:]
    f_top = exact(top[:, :n], linv, across) - 0.5 * exact(l_top, a11)
    l_pass.forward(1)
    cut = exact(f_ref[...], l_top, across) + exact(l_ref[...], f_top, across)

    @pl.when(p.c == 0)
    def _():
        own.wait()
        for to in range(1, cols):
            piece(to).wait_send()

    @pl.when(p.c != 0)
    def _():
        piece(1).wait_recv()

    if rows > 2:
        l_pass.forward(2)
    me = p.i * cols + p.c
    at = me * height + lax.broadcasted_iota(jnp.int32, (height, n), 0)
    panel = a_first[...] - cut
    panel = jnp.where(at >= n, panel, 0.0)
    next_ref[...] = panel
    gram = exact(panel, panel, along)
    deep = n // cols
    for to in range(cols):
        gram_in[to] = gram[to * deep:(to + 1) * deep]
    grams.begin()
    picker = (at - n == lax.broadcasted_iota(jnp.int32, (height, n), 1)).astype(jnp.bfloat16)
    pick = None
    for part in three(panel):
        now = lax.dot_general(
            picker, part.astype(jnp.bfloat16), along, preferred_element_type=jnp.float32
        )
        pick = now if pick is None else pick + now
    for to in range(cols):
        pick_in[to] = pick[to * deep:(to + 1) * deep]
    picks.begin()
    arrivals = l_row.arrivals()
    l_row.forward(*arrivals[0])
    grams.middle()
    picks.middle()
    line.begin()
    for step in range(3, rows):
        l_pass.forward(step)
    grams.late()
    picks.late()
    l_pass.own.wait()
    for plane in range(rows):
        l_spread.begin(plane)
    line.own.wait()
    spread.begin(p.i)
    grams.arrive()
    work[:, :n] = gram_all[...].reshape(n, n)
    work[:, n:] = unit(n)
    todo = [lambda: line.forward(1), lambda: spread.begin_next(1)]
    todo += [lambda a=a: l_row.forward(*a) for a in arrivals[1:]]
    todo += [f_row.begin]
    for step in range(2, rows):
        todo += [lambda step=step: line.forward(step), lambda step=step: spread.begin_next(step)]
    todo += [lambda: f_row.forward(*arrivals[0])]
    pieces = 8
    panels = n // 8 // pieces
    for part in range(pieces):
        eliminate(work, n, part * panels, (part + 1) * panels)
        for at, act in enumerate(todo):
            if at * pieces // len(todo) == part:
                act()
    inverse = work[:, n:]
    inv_ref[...] = inverse
    picks.arrive()
    top_panel = pick_all[...].reshape(n, n)
    newton_ref[...] = newton_product(exact(top_panel, inverse, across))
    for arrival in arrivals[1:]:
        f_row.forward(*arrival)
    l_row.finish()
    l_spread.finish()
    spread.finish()
    f_row.finish()
    line.finish()
    l_pass.finish()
    grams.finish()
    picks.finish()


def front(rows, cols, top, held, a_panel, l_panel, a_diag, l_inverse, a_trail, ident):
    height, n = a_panel.shape
    count = rows * cols
    small, deep = n // count, n // cols

    def f32(*shape):
        return jax.ShapeDtypeStruct(shape, jnp.float32)

    outs = [
        f32(height, n), f32(height, n), f32(height, n), f32(n, n), f32(n, n),
        f32(rows, height, n), f32(cols, height, n), f32(cols, height, n), f32(rows, height, n),
    ]
    dma = pltpu.SemaphoreType.DMA
    scratch = [pltpu.VMEM((rows, height, n), jnp.float32)] * 2 + [
        pltpu.VMEM((count, small, 2 * n), jnp.float32), pltpu.VMEM((height, n), jnp.float32),
    ] + [pltpu.VMEM((cols, deep, n), jnp.float32)] * 4 + [
        pltpu.VMEM((n, 2 * n), jnp.float32), dma((cols,)), dma((1,)), dma((1,)),
    ] + sum_scratch(count, small, 2 * n) + PlaneSum.scratch(rows, cols, deep, n) * 2
    scratch += LineGather.scratch(rows) + Spread.scratch(rows) + RowGather.scratch(cols)
    scratch += LineGather.scratch(rows) + Spread.scratch(rows) + RowGather.scratch(cols)
    return pl.pallas_call(
        functools.partial(front_kernel, rows, cols, held),
        out_shape=outs,
        in_specs=[NEAR, NEAR, NEAR, NEAR, NEAR, ANY],
        out_specs=[NEAR] * 5 + [ANY] * 4,
        scratch_shapes=scratch,
        compiler_params=pltpu.CompilerParams(collective_id=ident, has_side_effects=True),
    )(top.reshape(count, small, 2 * n), a_panel, l_panel, a_diag, l_inverse, a_trail)


def image_kernel(rows, cols, cross_ref, a_ref, refl_ref, f_ref, y_ref, image_ref, total_ref, f_cols,
                 y_rows, f_line, tiles, high, low, mine, twin_in, hop_in, *refs):
    p = Place(rows, cols)
    tile_sem, twin_send, twin_recv, hop_send, hop_recv, *refs = refs
    s_sum, s_fline, s_fspread, s_y = take(refs, 9, 5, 3, 5)
    gather_y = RowGather(p, y_ref, y_rows, s_y)
    height, _ = image_ref.shape
    chips = p.chips
    sums = PlaneSum(p, cross_ref, total_ref, *s_sum[:3], s_sum[3:])
    f_pass = LineGather(p, f_ref, f_line, s_fline)
    f_spread = Spread(p, f_line, f_cols, s_fspread)
    masks = sorted(range(1, chips), key=lambda m: (m & -m, m)) + [0]
    other = 1 - p.core

    def piece_col(step):
        index = step // 2
        if step % 2:
            return p.relative(masks[index], p.core) * 2 + p.core
        return p.relative(masks[index], other) * 2 + other

    def load(step):
        at = pl.multiple_of(piece_col(step) * height, 8)
        return pltpu.make_async_copy(
            a_ref.at[pl.ds(at, height), :], tiles.at[step % 2], tile_sem.at[step % 2]
        )

    def to_twin(index):
        return remote(
            mine.at[2 * index], twin_in.at[index], twin_send.at[index], twin_recv.at[index],
            (p.i, p.twin),
        )

    hops = [(step, m) for step in range(p.bits) for m in range(chips) if m % (2 << step) == 0]
    number = {key: at for at, key in enumerate(hops)}

    def hop(step, mask):
        index = number[(step, mask)]
        to = p.flip(p.chip, step, p.core) * 2 + p.core
        return remote(
            mine.at[2 * masks.index(mask + (1 << step)) + 1], hop_in.at[index], hop_send.at[index],
            hop_recv.at[index], (p.i, to),
        )

    greet_near(rows, cols)
    load(0).start()
    sums.begin()
    high[...], low[...] = two(refl_ref[...])
    depth = high.shape[0]
    chunk = min(depth, 512)

    def multiply(slot, at):
        total = None
        for k in range(depth // chunk):
            a_high, a_low = two(tiles[slot, :, k * chunk:(k + 1) * chunk])
            y_high, y_low = high[k * chunk:(k + 1) * chunk, :], low[k * chunk:(k + 1) * chunk, :]
            dot = functools.partial(jnp.dot, preferred_element_type=jnp.float32)
            now = dot(a_high, y_high) + (dot(a_high, y_low) + dot(a_low, y_high))
            total = now if total is None else total + now
        mine[at] = total

    for step in range(2 * chips):
        if step + 1 < 2 * chips:
            load(step + 1).start()
        load(step).wait()
        multiply(step % 2, step)
        index = step // 2
        if step % 2 == 0:
            to_twin(index).start()
        else:
            mask = masks[index]
            low_bit = p.bits if mask == 0 else (mask & -mask).bit_length() - 1
            to_twin(index).wait_recv()
            value = mine[step] + twin_in[index]
            for t in range(low_bit):
                hop(t, mask).wait_recv()
                value = value + hop_in[number[(t, mask)]]
            if mask:
                mine[step] = value
                hop(low_bit, mask - (1 << low_bit)).start()
            else:
                image_ref[...] = value
        if step == 1:
            sums.middle()
            f_pass.begin()
        if step == 3:
            sums.late()
        if step == 2 * chips - 2:
            f_pass.own.wait()
            f_spread.begin(p.i)
            f_pass.forward(1)
            f_spread.begin_next(1)
        if step == 2 * chips - 3:
            gather_y.begin()
    for at, arrival in enumerate(gather_y.arrivals()):
        gather_y.forward(*arrival)
        if at == 0 and rows > 2:
            f_pass.forward(2)
            f_spread.begin_next(2)
    for later in range(3, rows):
        f_pass.forward(later)
        f_spread.begin_next(later)
    sums.arrive()
    sums.finish()
    gather_y.finish()
    for index in range(chips):
        to_twin(index).wait_send()
    for step, mask in hops:
        hop(step, mask).wait_send()
    f_pass.finish()
    f_spread.finish()


def image(rows, cols, cross, a_trail, refl_cols, first_y, refl, ident):
    width, n = cross.shape
    piece = width // cols
    wide = a_trail.shape[1]
    height = refl.shape[0]
    chips = cols // 2
    outs = [
        jax.ShapeDtypeStruct((height, n), jnp.float32),
        jax.ShapeDtypeStruct((cols, piece, n), jnp.float32),
        jax.ShapeDtypeStruct((rows, height, n), jnp.float32),
        jax.ShapeDtypeStruct((cols, height, n), jnp.float32),
    ]
    dma = pltpu.SemaphoreType.DMA
    scratch = [
        pltpu.VMEM((rows, height, n), jnp.float32),
        pltpu.VMEM((2, height, wide), jnp.float32), pltpu.VMEM((wide, n), jnp.bfloat16),
        pltpu.VMEM((wide, n), jnp.bfloat16), pltpu.VMEM((cols, height, n), jnp.float32),
        pltpu.VMEM((chips, height, n), jnp.float32), pltpu.VMEM((chips, height, n), jnp.float32),
        dma((2,)), dma((chips,)), dma((chips,)), dma((chips,)), dma((chips,)),
    ] + PlaneSum.scratch(rows, cols, piece, n) + LineGather.scratch(rows)
    scratch += Spread.scratch(rows) + RowGather.scratch(cols)
    result, total, f_cols, y_rows = pl.pallas_call(
        functools.partial(image_kernel, rows, cols),
        out_shape=outs,
        in_specs=[NEAR, ANY, NEAR, NEAR, NEAR],
        out_specs=[NEAR, NEAR, ANY, ANY],
        scratch_shapes=scratch,
        compiler_params=pltpu.CompilerParams(collective_id=ident, has_side_effects=True),
    )(cross.reshape(cols, piece, n), a_trail, refl_cols, first_y, refl)
    return result, total.reshape(width, n), f_cols.reshape(-1, n), y_rows.reshape(-1, n)


def update_kernel(rows, cols, core_ref, a_ref, l_cols, f_cols, f_rows, l_rows, x_ref, out_ref,
                  total_ref, x_cols, x_rows, x_line, tiles, sides, results, high, low, *refs):
    p = Place(rows, cols)
    tile_sem, side_sem, out_sem, *refs = refs
    s_sum, s_line, s_spread, s_x = take(refs, 9, 5, 3, 5)
    sums = PlaneSum(p, core_ref, total_ref, *s_sum[:3], s_sum[3:])
    line = LineGather(p, x_ref, x_line, s_line)
    spread = Spread(p, x_line, x_cols, s_spread)
    gather_x = RowGather(p, x_ref, x_rows, s_x)
    height, n = f_rows.shape[1:]

    def load(step):
        slot = lax.rem(step, 2)
        return (
            pltpu.make_async_copy(
                a_ref.at[pl.ds(pl.multiple_of(step * height, 8), height), :], tiles.at[slot],
                tile_sem.at[slot],
            ),
            pltpu.make_async_copy(f_rows.at[step], sides.at[slot, 0], side_sem.at[0, slot]),
            pltpu.make_async_copy(l_rows.at[step], sides.at[slot, 1], side_sem.at[1, slot]),
        )

    def store(step):
        slot = lax.rem(step, 2)
        return pltpu.make_async_copy(
            results.at[slot], out_ref.at[pl.ds(pl.multiple_of(step * height, 8), height), :],
            out_sem.at[slot],
        )

    greet_near(rows, cols)
    for copy in load(0):
        copy.start()
    sums.begin()
    line.begin()
    gather_x.begin()
    high[:, :n], low[:, :n] = two(l_cols[...])
    high[:, n:], low[:, n:] = two(f_cols[...])
    last = cols - 1
    chunk = min(high.shape[0], 512)

    def body(step, carry):
        @pl.when(step < last)
        def _():
            for copy in load(step + 1):
                copy.start()

        for copy in load(step):
            copy.wait()

        @pl.when(step >= 2)
        def _():
            store(step - 2).wait()

        slot = lax.rem(step, 2)
        f_high, f_low = two(sides[slot, 0])
        l_high, l_low = two(sides[slot, 1])

        def dot(left, right):
            return lax.dot_general(
                left, right, (((1,), (1,)), ((), ())), preferred_element_type=jnp.float32
            )

        for k in range(high.shape[0] // chunk):
            at = slice(k * chunk, (k + 1) * chunk)
            with_l, with_f = high[at, :n], high[at, n:]
            results[slot, :, at] = tiles[slot, :, at] - (
                (dot(f_high, with_l) + dot(l_high, with_f))
                + (dot(f_high, low[at, :n]) + dot(f_low, with_l))
                + (dot(l_high, low[at, n:]) + dot(l_low, with_f))
            )
        store(step).start()

        actions = {}

        def put(when, action):
            actions.setdefault(min(when, last), []).append(action)

        def spread_own():
            line.own.wait()
            spread.begin(p.i)

        put(0, spread_own)
        put(1, sums.middle)
        for hop in range(1, rows):
            put(2 * hop + hop // 3, lambda hop=hop: line.forward(hop))
            put(2 * hop + hop // 3, lambda hop=hop: spread.begin_next(hop))
        for index, arrival in enumerate(gather_x.arrivals()):
            put(2 + 2 * index, lambda arrival=arrival: gather_x.forward(*arrival))
        put(4, sums.late)
        for when, todo in actions.items():
            @pl.when(step == when)
            def _(todo=todo):
                for action in todo:
                    action()
        return carry

    lax.fori_loop(0, cols, body, 0)
    sums.arrive()
    sums.finish()
    gather_x.finish()
    spread.finish()
    line.finish()
    for step in range(max(cols - 2, 0), cols):
        store(step).wait()


def update(rows, cols, core, a_trail, l_cols, f_cols, f_rows, l_rows, x, ident):
    n = core.shape[0]
    piece = n // cols
    height = x.shape[0]
    wide = a_trail.shape[1]
    outs = [
        jax.ShapeDtypeStruct(a_trail.shape, jnp.float32),
        jax.ShapeDtypeStruct((cols, piece, n), jnp.float32),
        jax.ShapeDtypeStruct((rows, height, n), jnp.float32),
        jax.ShapeDtypeStruct((cols, height, n), jnp.float32),
    ]
    dma = pltpu.SemaphoreType.DMA
    scratch = [
        pltpu.VMEM((rows, height, n), jnp.float32),
        pltpu.VMEM((2, height, wide), jnp.float32), pltpu.VMEM((2, 2, height, n), jnp.float32),
        pltpu.VMEM((2, height, wide), jnp.float32), pltpu.VMEM((wide, 2 * n), jnp.bfloat16),
        pltpu.VMEM((wide, 2 * n), jnp.bfloat16), dma((2,)), dma((2, 2)), dma((2,)),
    ] + PlaneSum.scratch(rows, cols, piece, n) + LineGather.scratch(rows)
    scratch += Spread.scratch(rows) + RowGather.scratch(cols)
    updated, total, x_cols, x_rows = pl.pallas_call(
        functools.partial(update_kernel, rows, cols),
        out_shape=outs,
        in_specs=[NEAR, ANY, NEAR, NEAR, ANY, ANY, NEAR],
        out_specs=[ANY, NEAR, ANY, ANY],
        scratch_shapes=scratch,
        compiler_params=pltpu.CompilerParams(collective_id=ident, has_side_effects=True),
    )(core.reshape(cols, piece, n), a_trail, l_cols, f_cols, f_rows, l_rows, x)
    return updated, total.reshape(n, n), x_cols.reshape(-1, n), x_rows.reshape(-1, n)


def shards(rows, cols, a_trail, a_panel, l_panel, a_diag, l_inverse):
    height, block_width = a_panel.shape
    me = lax.axis_index("row") * cols + lax.axis_index("col")
    tall = min(height, block_width)
    top = jnp.concatenate((a_panel[:tall], l_panel[:tall]), axis=1)
    panel_out, first_y, next_panel, inverse, newton, panel_cols, l_rows, f_rows, l_cols = front(
        rows, cols, jnp.concatenate([top] * (block_width // tall), axis=0), tall, a_panel, l_panel,
        a_diag, l_inverse, a_trail, 0,
    )
    panel_cols, l_cols = panel_cols.reshape(-1, block_width), l_cols.reshape(-1, block_width)

    def picker(at):
        return (at[:, None] - block_width == lax.iota(jnp.int32, block_width)[None, :]).astype(
            jnp.float32
        )

    wide = a_trail.shape[1]
    refl = large_product(next_panel, inverse.T) + picker(me * height + lax.iota(jnp.int32, height))
    refl_cols = large_product(panel_cols, inverse.T) + picker(
        lax.axis_index("col") * wide + lax.iota(jnp.int32, wide)
    )
    image_shard, cross, f_cols, refl_rows = image(
        rows, cols,
        jnp.concatenate((large_product(first_y.T, refl), large_product(l_panel.T, refl)), axis=0),
        a_trail, refl_cols, first_y, refl, 2,
    )
    x_shard = product(
        image_shard - large_product(first_y, cross[block_width:])
        - large_product(l_panel, cross[:block_width]),
        newton.T,
    )
    updated, core_sum, x_cols, x_rows = update(
        rows, cols, large_product(refl.T, x_shard), a_trail, l_cols, f_cols, f_rows, l_rows, x_shard, 3
    )
    half_core = 0.5 * product(newton, core_sum)
    z_cols = x_cols - large_product(refl_cols, half_core + half_core.T)
    trail_out = updated - large_product(
        jnp.concatenate((x_rows, refl_rows), axis=1),
        jnp.concatenate((refl_cols, z_cols), axis=1).T,
    )
    return (trail_out, panel_out)


def layer(rows, cols, *args):
    return shards(rows, cols, *args)


def solution(mesh):
    rows, cols = mesh.shape["row"], mesh.shape["col"]
    return jax.shard_map(
        functools.partial(layer, rows, cols),
        mesh=mesh,
        in_specs=(P("row", "col"), P(BOTH, None), P(BOTH, None), P(), P()),
        out_specs=(P("row", "col"), P(BOTH, None)),
        check_vma=False,
    )
```

```python
import functools

import jax
import jax.numpy as jnp
from jax import lax
from jax.experimental import pallas as pl
from jax.experimental.pallas import tpu as pltpu
from jax.sharding import PartitionSpec as P

NS_STEPS = 8
BOTH = ("row", "col")
MESH_ID = pl.DeviceIdType.MESH


def product(left, right):
    return jnp.dot(left, right, precision=lax.Precision.HIGHEST, preferred_element_type=jnp.float32)


def large_product(left, right):
    return jnp.dot(left, right, precision=lax.Precision.HIGH, preferred_element_type=jnp.float32)


def exact(left, right, dims=(((1,), (0,)), ((), ()))):
    return lax.dot_general(left, right, dims, precision=lax.Precision.HIGHEST, preferred_element_type=jnp.float32)


def three(x):
    high = x.astype(jnp.bfloat16).astype(jnp.float32)
    rest = x - high
    mid = rest.astype(jnp.bfloat16).astype(jnp.float32)
    return high, mid, rest - mid


def sub_block(V, lanes_at, n, W):
    row = lax.broadcasted_iota(jnp.int32, (8, 128), 0)
    shifted = pltpu.roll(V[:, :n], n - lanes_at, 1)[:, :128]
    cols = [jnp.broadcast_to(shifted[:, j:j+1], (8, 128)) for j in range(8)]
    vs = [V[:, 128*t:128*(t+1)] for t in range(W//128)]
    for j in range(8):
        r = lax.rsqrt(cols[j][j:j+1, :])
        r = r * (1.5 - 0.5 * cols[j][j:j+1, :] * r * r)
        lj = jnp.where(row > j, cols[j] * r, 0.0)
        sc = jnp.where(row == j, jnp.broadcast_to(r, (8,128)), 1.0)
        for k in range(j+1, 8):
            cols[k] = cols[k] - lj * lj[k:k+1, :]
        for t in range(len(vs)):
            top = vs[t][j:j+1, :] * r
            vs[t] = jnp.where(row == j, jnp.broadcast_to(top, (8,128)), vs[t] - lj * top)
    return jnp.concatenate(vs, axis=1)


def eliminate(work, n, begin, end, after):
    lane = lax.broadcasted_iota(jnp.int32, (8, n), 1)

    def body(b, carry):
        k0 = pl.multiple_of(b * 8, 8)
        V = sub_block(work[pl.ds(k0, 8), :], k0, n, 2 * n)
        work[pl.ds(k0, 8), :] = V
        h, m, l = three(jnp.where(lane >= k0 + 8, V[:, :n], 0.0))
        hr, mr, lr = three(V)
        lhs = jnp.concatenate([h, h, m, h, m, l], axis=0).astype(jnp.bfloat16)
        rhs = jnp.concatenate([hr, mr, hr, lr, mr, hr], axis=0).astype(jnp.bfloat16)
        work[...] -= lax.dot_general(
            lhs, rhs, (((0,), (0,)), ((), ())), preferred_element_type=jnp.float32
        )
        after(b)
        return carry

    lax.fori_loop(begin, end, body, 0)


def unit(n):
    return (
        lax.broadcasted_iota(jnp.int32, (n, n), 0) == lax.broadcasted_iota(jnp.int32, (n, n), 1)
    ).astype(jnp.float32)


def newton_product(q_top):
    rem = -q_top
    approx = unit(q_top.shape[0]) + rem
    for _ in range(NS_STEPS - 1):
        rem = exact(rem, rem)
        approx = approx + exact(approx, rem)
    return approx


def greet_all(rows, cols):
    count = rows * cols
    me = lax.axis_index("row") * cols + lax.axis_index("col")
    barrier = pltpu.get_barrier_semaphore()

    def greet(step, carry):
        at = lax.rem(me + step, count)
        pl.semaphore_signal(
            barrier, inc=1, device_id=(at // cols, lax.rem(at, cols)), device_id_type=MESH_ID
        )
        return carry

    lax.fori_loop(1, count, greet, 0)
    pl.semaphore_wait(barrier, count - 1)


def greet_near(rows, cols):
    i, c = lax.axis_index("row"), lax.axis_index("col")
    barrier = pltpu.get_barrier_semaphore()

    def greet_plane(step, carry):
        pl.semaphore_signal(
            barrier, inc=1, device_id=(i, lax.rem(c + step, cols)), device_id_type=MESH_ID
        )
        return carry

    def greet_line(step, carry):
        pl.semaphore_signal(
            barrier, inc=1, device_id=(lax.rem(i + step, rows), c), device_id_type=MESH_ID
        )
        return carry

    lax.fori_loop(1, cols, greet_plane, 0)
    lax.fori_loop(1, rows, greet_line, 0)
    pl.semaphore_wait(barrier, rows + cols - 2)


def sum_steps(rows, cols, x_ref, o_ref, recv, red, send_a, recv_a, send_b, recv_b, held):
    count = rows * cols
    me = lax.axis_index("row") * cols + lax.axis_index("col")

    def peer(step):
        at = lax.rem(me + step, count)
        return at, (at // cols, lax.rem(at, cols))

    def owner(at):
        return (at * x_ref.shape[1]) // held

    def scatter(step):
        at, device = peer(step)
        return pltpu.make_async_remote_copy(
            src_ref=x_ref.at[at], dst_ref=recv.at[step], send_sem=send_a.at[step],
            recv_sem=recv_a.at[step], device_id=device, device_id_type=MESH_ID,
        )

    def gather(step):
        device = peer(step)[1]
        return pltpu.make_async_remote_copy(
            src_ref=red, dst_ref=o_ref.at[me], send_sem=send_b.at[step],
            recv_sem=recv_b.at[step], device_id=device, device_id_type=MESH_ID,
        )

    def loop(action):
        def body(step, carry):
            action(step)
            return carry

        lax.fori_loop(1, count, body, 0)

    def sends(step, action):
        if held is None:
            action()
        else:
            pl.when(owner(peer(step)[0]) == me)(action)

    def first():
        loop(lambda step: sends(step, lambda: scatter(step).start()))

    def second():
        if held is None:
            def add(step, total):
                scatter(step).wait_recv()
                return total + recv[step]

            total = lax.fori_loop(1, count, add, x_ref[me])
            red[...] = total
            o_ref[me] = total
        else:
            source = owner(me)

            @pl.when(source == me)
            def _():
                red[...] = x_ref[me]
                o_ref[me] = x_ref[me]

            @pl.when(source != me)
            def _():
                step = lax.rem(me + count - source, count)
                scatter(step).wait_recv()
                red[...] = recv[step]
                o_ref[me] = recv[step]
        loop(lambda step: gather(step).start())

    def third():
        def finish(step):
            gather(step).wait_recv()
            sends(step, lambda: scatter(step).wait_send())
            gather(step).wait_send()

        loop(finish)

    return first, second, third


def sum_scratch(count, piece, width):
    return [
        pltpu.VMEM((count, piece, width), jnp.float32),
        pltpu.VMEM((piece, width), jnp.float32),
        pltpu.SemaphoreType.DMA((count,)),
        pltpu.SemaphoreType.DMA((count,)),
        pltpu.SemaphoreType.DMA((count,)),
        pltpu.SemaphoreType.DMA((count,)),
    ]


def remote(src, dst, send, recv, device):
    return pltpu.make_async_remote_copy(
        src_ref=src, dst_ref=dst, send_sem=send, recv_sem=recv, device_id=device,
        device_id_type=MESH_ID,
    )


def two(x):
    high = x.astype(jnp.bfloat16)
    return high, (x - high.astype(jnp.float32)).astype(jnp.bfloat16)


class Place:
    def __init__(self, rows, cols):
        self.rows, self.cols, self.chips = rows, cols, cols // 2
        self.i, self.c = lax.axis_index("row"), lax.axis_index("col")
        self.core = lax.rem(self.c, 2)
        self.chip = self.c // 2
        self.twin = self.c + 1 - 2 * self.core
        self.bits = self.chips.bit_length() - 1

    def stride(self, step, core):
        return (1 - core) * (1 << step) + core * (1 << (self.bits - 1 - step))

    def flip(self, chip, step, core):
        size = self.stride(step, core)
        return chip + (1 - 2 * lax.rem(chip // size, 2)) * size

    def relative(self, mask, core):
        chip = self.chip
        for step in range(self.bits):
            if mask >> step & 1:
                chip = self.flip(chip, step, core)
        return chip


class PlaneSum:
    def __init__(self, place, x, out, recv, part, red, sems):
        self.p, self.x, self.out, self.recv, self.part, self.red = place, x, out, recv, part, red
        self.sems = sems

    @staticmethod
    def scratch(rows, cols, piece, width):
        return [
            pltpu.VMEM((cols, piece, width), jnp.float32),
            pltpu.VMEM((rows, piece, width), jnp.float32),
            pltpu.VMEM((piece, width), jnp.float32),
        ] + [pltpu.SemaphoreType.DMA((cols,))] * 2 + [pltpu.SemaphoreType.DMA((rows,))] * 2 + [
            pltpu.SemaphoreType.DMA((cols,))
        ] * 2

    def scatter(self, step):
        p = self.p
        to = lax.rem(p.c + step, p.cols)
        return remote(
            self.x.at[to], self.recv.at[step], self.sems[0].at[step], self.sems[1].at[step], (p.i, to)
        )

    def across(self, step):
        p = self.p
        to = lax.rem(p.i + step, p.rows)
        return remote(
            self.part.at[0], self.part.at[step], self.sems[2].at[step], self.sems[3].at[step],
            (to, p.c),
        )

    def gather(self, step):
        p = self.p
        to = lax.rem(p.c + step, p.cols)
        return remote(
            self.red, self.out.at[p.c], self.sems[4].at[step], self.sems[5].at[step], (p.i, to)
        )

    def loop(self, count, action):
        def body(step, carry):
            action(step)
            return carry

        lax.fori_loop(1, count, body, 0)

    def begin(self):
        self.loop(self.p.cols, lambda step: self.scatter(step).start())

    def middle(self):
        def add(step, total):
            self.scatter(step).wait_recv()
            return total + self.recv[step]

        self.part[0] = lax.fori_loop(1, self.p.cols, add, self.x[self.p.c])
        self.loop(self.p.rows, lambda step: self.across(step).start())

    def late(self):
        def add(step, total):
            self.across(step).wait_recv()
            return total + self.part[step]

        total = lax.fori_loop(1, self.p.rows, add, self.part[0])
        self.red[...] = total
        self.out[self.p.c] = total
        self.loop(self.p.cols, lambda step: self.gather(step).start())

    def arrive(self):
        self.loop(self.p.cols, lambda step: self.gather(step).wait_recv())

    def finish(self):
        self.loop(self.p.cols, lambda step: self.scatter(step).wait_send())
        self.loop(self.p.cols, lambda step: self.gather(step).wait_send())
        self.loop(self.p.rows, lambda step: self.across(step).wait_send())


class RowGather:
    def __init__(self, place, x, out, sems):
        self.p, self.x, self.out, self.sems = place, x, out, sems
        p = place
        self.own = pltpu.make_async_copy(x, out.at[p.c], sems[4].at[0])

    @staticmethod
    def scratch(cols):
        chips = cols // 2
        return [pltpu.SemaphoreType.DMA((chips,))] * 4 + [pltpu.SemaphoreType.DMA((1,))]

    def hop(self, step, mask):
        p = self.p
        at = p.relative(mask, p.core) * 2 + p.core
        index = (1 << step) - 1 + mask
        to = p.flip(p.chip, step, p.core) * 2 + p.core
        return remote(
            self.out.at[at] if mask else self.x, self.out.at[at], self.sems[0].at[index],
            self.sems[1].at[index], (p.i, to),
        )

    def to_twin(self, mask):
        p = self.p
        at = p.relative(mask, p.core) * 2 + p.core
        return remote(
            self.out.at[at] if mask else self.x, self.out.at[at], self.sems[2].at[mask],
            self.sems[3].at[mask], (p.i, p.twin),
        )

    def begin(self):
        for step in range(self.p.bits):
            self.hop(step, 0).start()
        self.own.start()
        self.to_twin(0).start()

    def arrivals(self):
        return [(step, mask) for step in range(self.p.bits) for mask in range(1 << step)]

    def forward(self, step, mask):
        self.hop(step, mask).wait_recv()
        here = mask + (1 << step)
        for later in range(step + 1, self.p.bits):
            self.hop(later, here).start()
        self.to_twin(here).start()

    def finish(self):
        self.own.wait()
        for mask in range(self.p.chips):
            self.to_twin(mask).wait_recv()
        for mask in range(self.p.chips):
            self.to_twin(mask).wait_send()
        for step, mask in self.arrivals():
            self.hop(step, mask).wait_send()


class LineGather:
    def __init__(self, place, x, out, sems):
        self.p, self.x, self.out, self.sems = place, x, out, sems
        self.own = pltpu.make_async_copy(x, out.at[place.i], sems[4].at[0])

    @staticmethod
    def scratch(rows):
        return [pltpu.SemaphoreType.DMA((rows,))] * 4 + [pltpu.SemaphoreType.DMA((1,))]

    def up(self, step):
        p = self.p
        at = p.i - step
        return remote(
            self.out.at[at] if step else self.x, self.out.at[at], self.sems[0].at[step],
            self.sems[1].at[step], (p.i + 1, p.c),
        )

    def up_recv(self, step):
        p = self.p
        return remote(
            self.x, self.out.at[p.i - step], self.sems[0].at[step], self.sems[1].at[step - 1],
            (p.i - 1, p.c),
        )

    def down(self, step):
        p = self.p
        at = p.i + step
        return remote(
            self.out.at[at] if step else self.x, self.out.at[at], self.sems[2].at[step],
            self.sems[3].at[step], (p.i - 1, p.c),
        )

    def down_recv(self, step):
        p = self.p
        return remote(
            self.x, self.out.at[p.i + step], self.sems[2].at[step], self.sems[3].at[step - 1],
            (p.i + 1, p.c),
        )

    def begin(self):
        p = self.p
        pl.when(p.i + 1 < p.rows)(lambda: self.up(0).start())
        pl.when(p.i >= 1)(lambda: self.down(0).start())
        self.own.start()

    def forward(self, step):
        p = self.p

        @pl.when(p.i >= step)
        def _():
            self.up_recv(step).wait_recv()
            pl.when(p.i + 1 < p.rows)(lambda: self.up(step).start())

        @pl.when(p.i + step < p.rows)
        def _():
            self.down_recv(step).wait_recv()
            pl.when(p.i >= 1)(lambda: self.down(step).start())

    def finish(self):
        p = self.p
        for step in range(p.rows):
            pl.when((p.i >= step) & (p.i + 1 < p.rows))(lambda step=step: self.up(step).wait_send())
            pl.when((p.i + step < p.rows) & (p.i >= 1))(lambda step=step: self.down(step).wait_send())


class Spread:
    def __init__(self, place, x, out, sems):
        self.p, self.x, self.out, self.sems = place, x, out, sems
        self.per = place.cols // place.rows
        self.slot = lax.rem(place.c, place.rows)

    @staticmethod
    def scratch(rows):
        return [pltpu.SemaphoreType.DMA((rows,))] * 3

    def target(self, plane):
        return plane * self.per + self.p.c // self.p.rows

    def copy(self, plane):
        return remote(
            self.x.at[plane], self.out.at[self.slot], self.sems[0].at[plane],
            self.sems[1].at[self.slot], (self.p.i, self.target(plane)),
        )

    def local(self, plane):
        return pltpu.make_async_copy(self.x.at[plane], self.out.at[self.slot], self.sems[2].at[plane])

    def begin(self, plane):
        here = self.target(plane) == self.p.c
        pl.when(here)(lambda: self.local(plane).start())
        pl.when(jnp.logical_not(here))(lambda: self.copy(plane).start())

    def begin_next(self, step):
        p = self.p
        pl.when(p.i >= step)(lambda: self.begin(p.i - step))
        pl.when(p.i + step < p.rows)(lambda: self.begin(p.i + step))

    def finish(self):
        p = self.p
        for slot in range(p.rows):
            source = lax.rem(p.c, self.per) * p.rows + slot

            @pl.when(source != p.c)
            def _(slot=slot):
                remote(
                    self.x.at[0], self.out.at[slot], self.sems[0].at[0], self.sems[1].at[slot],
                    (p.i, p.twin),
                ).wait_recv()

        for plane in range(p.rows):
            here = self.target(plane) == p.c
            pl.when(here)(lambda plane=plane: self.local(plane).wait())
            pl.when(jnp.logical_not(here))(lambda plane=plane: self.copy(plane).wait_send())


def take(refs, *counts):
    out, at = [], 0
    for count in counts:
        out.append(refs[at:at + count])
        at += count
    return out


ANY = pl.BlockSpec(memory_space=pl.ANY)
NEAR = pl.BlockSpec(memory_space=pltpu.VMEM)


def front_kernel(rows, cols, held, top_ref, panel_ref, l_ref, diag_ref, linv_ref, a_ref,
                 out_ref, f_ref, next_ref, inv_ref, newton_ref, panel_cols, l_rows, f_rows, l_cols,
                 *refs):
    p = Place(rows, cols)
    panel_line, l_line, top_all, a_first, gram_in, gram_all, pick_in, pick_all, work, *refs = refs
    send_p, recv_p, own_sem, *refs = refs
    s_top, s_gram, s_pick, s_line, s_spread, s_lrow, s_lline, s_lspread, s_frow = take(
        refs, 6, 9, 9, 5, 3, 5, 5, 3, 5
    )
    n = inv_ref.shape[0]
    height = f_ref.shape[0]
    tops = sum_steps(rows, cols, top_ref, top_all, *s_top, held)
    grams = PlaneSum(p, gram_in, gram_all, *s_gram[:3], s_gram[3:])
    picks = PlaneSum(p, pick_in, pick_all, *s_pick[:3], s_pick[3:])
    line = LineGather(p, next_ref, panel_line, s_line)
    spread = Spread(p, panel_line, panel_cols, s_spread)
    l_row = RowGather(p, l_ref, l_rows, s_lrow)
    l_pass = LineGather(p, l_ref, l_line, s_lline)
    l_spread = Spread(p, l_line, l_cols, s_lspread)
    f_row = RowGather(p, f_ref, f_rows, s_frow)

    def piece(to):
        return remote(
            a_ref.at[pl.ds(to * height, height), pl.ds(0, n)], a_first, send_p.at[to],
            recv_p.at[0], (p.i, to),
        )

    own = pltpu.make_async_copy(a_ref.at[pl.ds(0, height), pl.ds(0, n)], a_first, own_sem.at[0])
    greet_all(rows, cols)
    tops[0]()
    across = (((1,), (1,)), ((), ()))
    along = (((0,), (0,)), ((), ()))
    linv = linv_ref[...]
    a11 = exact(exact(linv, diag_ref[...]), linv, across)
    tops[1]()

    @pl.when(p.c == 0)
    def _():
        own.start()
        for to in range(1, cols):
            piece(to).start()

    l_pass.begin()
    l_row.begin()
    half = 0.5 * exact(l_ref[...], a11)
    f_ref[...] = exact(panel_ref[...], linv, across) - half
    out_ref[...] = f_ref[...] - half
    tops[2]()
    top = top_all[...].reshape(n, 2 * n)
    l_top = top[:, n:]
    f_top = exact(top[:, :n], linv, across) - 0.5 * exact(l_top, a11)
    l_pass.forward(1)
    cut = exact(f_ref[...], l_top, across) + exact(l_ref[...], f_top, across)

    @pl.when(p.c == 0)
    def _():
        own.wait()
        for to in range(1, cols):
            piece(to).wait_send()

    @pl.when(p.c != 0)
    def _():
        piece(1).wait_recv()

    if rows > 2:
        l_pass.forward(2)
    me = p.i * cols + p.c
    at = me * height + lax.broadcasted_iota(jnp.int32, (height, n), 0)
    panel = a_first[...] - cut
    panel = jnp.where(at >= n, panel, 0.0)
    next_ref[...] = panel
    gram = exact(panel, panel, along)
    deep = n // cols
    for to in range(cols):
        gram_in[to] = gram[to * deep:(to + 1) * deep]
    grams.begin()
    picker = (at - n == lax.broadcasted_iota(jnp.int32, (height, n), 1)).astype(jnp.bfloat16)
    pick = None
    for part in three(panel):
        now = lax.dot_general(
            picker, part.astype(jnp.bfloat16), along, preferred_element_type=jnp.float32
        )
        pick = now if pick is None else pick + now
    for to in range(cols):
        pick_in[to] = pick[to * deep:(to + 1) * deep]
    picks.begin()
    arrivals = l_row.arrivals()
    l_row.forward(*arrivals[0])
    grams.middle()
    picks.middle()
    line.begin()
    for step in range(3, rows):
        l_pass.forward(step)
    grams.late()
    picks.late()
    l_pass.own.wait()
    for plane in range(rows):
        l_spread.begin(plane)
    line.own.wait()
    spread.begin(p.i)
    grams.arrive()
    work[:, :n] = gram_all[...].reshape(n, n)
    work[:, n:] = unit(n)
    todo = [lambda: line.forward(1), lambda: spread.begin_next(1)]
    todo += [lambda a=a: l_row.forward(*a) for a in arrivals[1:]]
    todo += [f_row.begin]
    for step in range(2, rows):
        todo += [lambda step=step: line.forward(step), lambda step=step: spread.begin_next(step)]
    todo += [lambda: f_row.forward(*arrivals[0])]
    panels = n // 8

    def after(panel):
        for at, act in enumerate(todo):
            pl.when(panel == (at * 8 // len(todo) + 1) * panels // 8 - 1)(act)

    eliminate(work, n, 0, panels, after)
    inverse = work[:, n:]
    inv_ref[...] = inverse
    picks.arrive()
    top_panel = pick_all[...].reshape(n, n)
    newton_ref[...] = newton_product(exact(top_panel, inverse, across))
    for arrival in arrivals[1:]:
        f_row.forward(*arrival)
    l_row.finish()
    l_spread.finish()
    spread.finish()
    f_row.finish()
    line.finish()
    l_pass.finish()
    grams.finish()
    picks.finish()


def front(rows, cols, top, held, a_panel, l_panel, a_diag, l_inverse, a_trail, ident):
    height, n = a_panel.shape
    count = rows * cols
    small, deep = n // count, n // cols

    def f32(*shape):
        return jax.ShapeDtypeStruct(shape, jnp.float32)

    outs = [
        f32(height, n), f32(height, n), f32(height, n), f32(n, n), f32(n, n),
        f32(rows, height, n), f32(cols, height, n), f32(cols, height, n), f32(rows, height, n),
    ]
    dma = pltpu.SemaphoreType.DMA
    scratch = [pltpu.VMEM((rows, height, n), jnp.float32)] * 2 + [
        pltpu.VMEM((count, small, 2 * n), jnp.float32), pltpu.VMEM((height, n), jnp.float32),
    ] + [pltpu.VMEM((cols, deep, n), jnp.float32)] * 4 + [
        pltpu.VMEM((n, 2 * n), jnp.float32), dma((cols,)), dma((1,)), dma((1,)),
    ] + sum_scratch(count, small, 2 * n) + PlaneSum.scratch(rows, cols, deep, n) * 2
    scratch += LineGather.scratch(rows) + Spread.scratch(rows) + RowGather.scratch(cols)
    scratch += LineGather.scratch(rows) + Spread.scratch(rows) + RowGather.scratch(cols)
    return pl.pallas_call(
        functools.partial(front_kernel, rows, cols, held),
        out_shape=outs,
        in_specs=[NEAR, NEAR, NEAR, NEAR, NEAR, ANY],
        out_specs=[NEAR] * 5 + [ANY] * 4,
        scratch_shapes=scratch,
        compiler_params=pltpu.CompilerParams(collective_id=ident, has_side_effects=True),
    )(top.reshape(count, small, 2 * n), a_panel, l_panel, a_diag, l_inverse, a_trail)


def image_kernel(rows, cols, cross_ref, a_ref, refl_ref, f_ref, y_ref, image_ref, total_ref, f_cols,
                 y_rows, f_line, tiles, high, low, mine, twin_in, hop_in, *refs):
    p = Place(rows, cols)
    tile_sem, twin_send, twin_recv, hop_send, hop_recv, *refs = refs
    s_sum, s_fline, s_fspread, s_y = take(refs, 9, 5, 3, 5)
    gather_y = RowGather(p, y_ref, y_rows, s_y)
    height, _ = image_ref.shape
    chips = p.chips
    sums = PlaneSum(p, cross_ref, total_ref, *s_sum[:3], s_sum[3:])
    f_pass = LineGather(p, f_ref, f_line, s_fline)
    f_spread = Spread(p, f_line, f_cols, s_fspread)
    masks = sorted(range(1, chips), key=lambda m: (m & -m, m)) + [0]
    other = 1 - p.core

    def piece_col(step):
        index = step // 2
        if step % 2:
            return p.relative(masks[index], p.core) * 2 + p.core
        return p.relative(masks[index], other) * 2 + other

    def load(step):
        at = pl.multiple_of(piece_col(step) * height, 8)
        return pltpu.make_async_copy(
            a_ref.at[pl.ds(at, height), :], tiles.at[step % 2], tile_sem.at[step % 2]
        )

    def to_twin(index):
        return remote(
            mine.at[2 * index], twin_in.at[index], twin_send.at[index], twin_recv.at[index],
            (p.i, p.twin),
        )

    hops = [(step, m) for step in range(p.bits) for m in range(chips) if m % (2 << step) == 0]
    number = {key: at for at, key in enumerate(hops)}

    def hop(step, mask):
        index = number[(step, mask)]
        to = p.flip(p.chip, step, p.core) * 2 + p.core
        return remote(
            mine.at[2 * masks.index(mask + (1 << step)) + 1], hop_in.at[index], hop_send.at[index],
            hop_recv.at[index], (p.i, to),
        )

    greet_near(rows, cols)
    load(0).start()
    sums.begin()
    high[...], low[...] = two(refl_ref[...])
    depth = high.shape[0]
    chunk = min(depth, 512)

    def multiply(slot, at):
        def add(k, carry):
            part = pl.ds(pl.multiple_of(k * chunk, chunk), chunk)
            a_high, a_low = two(tiles[slot, :, part])
            y_high, y_low = high[part, :], low[part, :]
            dot = functools.partial(jnp.dot, preferred_element_type=jnp.float32)
            now = dot(a_high, y_high) + (dot(a_high, y_low) + dot(a_low, y_high))
            mine[at] = mine[at] + now
            return carry

        mine[at] = jnp.zeros(mine.shape[1:], jnp.float32)
        lax.fori_loop(0, depth // chunk, add, 0)

    for step in range(2 * chips):
        if step + 1 < 2 * chips:
            load(step + 1).start()
        load(step).wait()
        multiply(step % 2, step)
        index = step // 2
        if step % 2 == 0:
            to_twin(index).start()
        else:
            mask = masks[index]
            low_bit = p.bits if mask == 0 else (mask & -mask).bit_length() - 1
            to_twin(index).wait_recv()
            value = mine[step] + twin_in[index]
            for t in range(low_bit):
                hop(t, mask).wait_recv()
                value = value + hop_in[number[(t, mask)]]
            if mask:
                mine[step] = value
                hop(low_bit, mask - (1 << low_bit)).start()
            else:
                image_ref[...] = value
        if step == 1:
            sums.middle()
            f_pass.begin()
        if step == 3:
            sums.late()
        if step == 2 * chips - 2:
            f_pass.own.wait()
            f_spread.begin(p.i)
            f_pass.forward(1)
            f_spread.begin_next(1)
        if step == 2 * chips - 3:
            gather_y.begin()
    for at, arrival in enumerate(gather_y.arrivals()):
        gather_y.forward(*arrival)
        if at == 0 and rows > 2:
            f_pass.forward(2)
            f_spread.begin_next(2)
    for later in range(3, rows):
        f_pass.forward(later)
        f_spread.begin_next(later)
    sums.arrive()
    sums.finish()
    gather_y.finish()
    for index in range(chips):
        to_twin(index).wait_send()
    for step, mask in hops:
        hop(step, mask).wait_send()
    f_pass.finish()
    f_spread.finish()


def image(rows, cols, cross, a_trail, refl_cols, first_y, refl, ident):
    width, n = cross.shape
    piece = width // cols
    wide = a_trail.shape[1]
    height = refl.shape[0]
    chips = cols // 2
    outs = [
        jax.ShapeDtypeStruct((height, n), jnp.float32),
        jax.ShapeDtypeStruct((cols, piece, n), jnp.float32),
        jax.ShapeDtypeStruct((rows, height, n), jnp.float32),
        jax.ShapeDtypeStruct((cols, height, n), jnp.float32),
    ]
    dma = pltpu.SemaphoreType.DMA
    scratch = [
        pltpu.VMEM((rows, height, n), jnp.float32),
        pltpu.VMEM((2, height, wide), jnp.float32), pltpu.VMEM((wide, n), jnp.bfloat16),
        pltpu.VMEM((wide, n), jnp.bfloat16), pltpu.VMEM((cols, height, n), jnp.float32),
        pltpu.VMEM((chips, height, n), jnp.float32), pltpu.VMEM((chips, height, n), jnp.float32),
        dma((2,)), dma((chips,)), dma((chips,)), dma((chips,)), dma((chips,)),
    ] + PlaneSum.scratch(rows, cols, piece, n) + LineGather.scratch(rows)
    scratch += Spread.scratch(rows) + RowGather.scratch(cols)
    result, total, f_cols, y_rows = pl.pallas_call(
        functools.partial(image_kernel, rows, cols),
        out_shape=outs,
        in_specs=[NEAR, ANY, NEAR, NEAR, NEAR],
        out_specs=[NEAR, NEAR, ANY, ANY],
        scratch_shapes=scratch,
        compiler_params=pltpu.CompilerParams(collective_id=ident, has_side_effects=True),
    )(cross.reshape(cols, piece, n), a_trail, refl_cols, first_y, refl)
    return result, total.reshape(width, n), f_cols.reshape(-1, n), y_rows.reshape(-1, n)


def update_kernel(rows, cols, core_ref, a_ref, l_cols, f_cols, f_rows, l_rows, x_ref, out_ref,
                  total_ref, x_cols, x_rows, x_line, tiles, sides, results, high, low, *refs):
    p = Place(rows, cols)
    tile_sem, side_sem, out_sem, *refs = refs
    s_sum, s_line, s_spread, s_x = take(refs, 9, 5, 3, 5)
    sums = PlaneSum(p, core_ref, total_ref, *s_sum[:3], s_sum[3:])
    line = LineGather(p, x_ref, x_line, s_line)
    spread = Spread(p, x_line, x_cols, s_spread)
    gather_x = RowGather(p, x_ref, x_rows, s_x)
    height, n = f_rows.shape[1:]

    def load(step):
        slot = lax.rem(step, 2)
        return (
            pltpu.make_async_copy(
                a_ref.at[pl.ds(pl.multiple_of(step * height, 8), height), :], tiles.at[slot],
                tile_sem.at[slot],
            ),
            pltpu.make_async_copy(f_rows.at[step], sides.at[slot, 0], side_sem.at[0, slot]),
            pltpu.make_async_copy(l_rows.at[step], sides.at[slot, 1], side_sem.at[1, slot]),
        )

    def store(step):
        slot = lax.rem(step, 2)
        return pltpu.make_async_copy(
            results.at[slot], out_ref.at[pl.ds(pl.multiple_of(step * height, 8), height), :],
            out_sem.at[slot],
        )

    greet_near(rows, cols)
    for copy in load(0):
        copy.start()
    sums.begin()
    line.begin()
    gather_x.begin()
    high[:, :n], low[:, :n] = two(l_cols[...])
    high[:, n:], low[:, n:] = two(f_cols[...])
    last = cols - 1
    chunk = min(high.shape[0], 512)

    def body(step, carry):
        @pl.when(step < last)
        def _():
            for copy in load(step + 1):
                copy.start()

        for copy in load(step):
            copy.wait()

        @pl.when(step >= 2)
        def _():
            store(step - 2).wait()

        slot = lax.rem(step, 2)
        f_high, f_low = two(sides[slot, 0])
        l_high, l_low = two(sides[slot, 1])

        def dot(left, right):
            return lax.dot_general(
                left, right, (((1,), (1,)), ((), ())), preferred_element_type=jnp.float32
            )

        for k in range(high.shape[0] // chunk):
            at = slice(k * chunk, (k + 1) * chunk)
            with_l, with_f = high[at, :n], high[at, n:]
            results[slot, :, at] = tiles[slot, :, at] - (
                (dot(f_high, with_l) + dot(l_high, with_f))
                + (dot(f_high, low[at, :n]) + dot(f_low, with_l))
                + (dot(l_high, low[at, n:]) + dot(l_low, with_f))
            )
        store(step).start()

        actions = {}

        def put(when, action):
            actions.setdefault(min(when, last), []).append(action)

        def spread_own():
            line.own.wait()
            spread.begin(p.i)

        put(0, spread_own)
        put(1, sums.middle)
        for hop in range(1, rows):
            put(2 * hop + hop // 3, lambda hop=hop: line.forward(hop))
            put(2 * hop + hop // 3, lambda hop=hop: spread.begin_next(hop))
        for index, arrival in enumerate(gather_x.arrivals()):
            put(2 + 2 * index, lambda arrival=arrival: gather_x.forward(*arrival))
        put(4, sums.late)
        for when, todo in actions.items():
            @pl.when(step == when)
            def _(todo=todo):
                for action in todo:
                    action()
        return carry

    lax.fori_loop(0, cols, body, 0)
    sums.arrive()
    sums.finish()
    gather_x.finish()
    spread.finish()
    line.finish()
    for step in range(max(cols - 2, 0), cols):
        store(step).wait()


def update(rows, cols, core, a_trail, l_cols, f_cols, f_rows, l_rows, x, ident):
    n = core.shape[0]
    piece = n // cols
    height = x.shape[0]
    wide = a_trail.shape[1]
    outs = [
        jax.ShapeDtypeStruct(a_trail.shape, jnp.float32),
        jax.ShapeDtypeStruct((cols, piece, n), jnp.float32),
        jax.ShapeDtypeStruct((rows, height, n), jnp.float32),
        jax.ShapeDtypeStruct((cols, height, n), jnp.float32),
    ]
    dma = pltpu.SemaphoreType.DMA
    scratch = [
        pltpu.VMEM((rows, height, n), jnp.float32),
        pltpu.VMEM((2, height, wide), jnp.float32), pltpu.VMEM((2, 2, height, n), jnp.float32),
        pltpu.VMEM((2, height, wide), jnp.float32), pltpu.VMEM((wide, 2 * n), jnp.bfloat16),
        pltpu.VMEM((wide, 2 * n), jnp.bfloat16), dma((2,)), dma((2, 2)), dma((2,)),
    ] + PlaneSum.scratch(rows, cols, piece, n) + LineGather.scratch(rows)
    scratch += Spread.scratch(rows) + RowGather.scratch(cols)
    updated, total, x_cols, x_rows = pl.pallas_call(
        functools.partial(update_kernel, rows, cols),
        out_shape=outs,
        in_specs=[NEAR, ANY, NEAR, NEAR, ANY, ANY, NEAR],
        out_specs=[ANY, NEAR, ANY, ANY],
        scratch_shapes=scratch,
        compiler_params=pltpu.CompilerParams(collective_id=ident, has_side_effects=True),
    )(core.reshape(cols, piece, n), a_trail, l_cols, f_cols, f_rows, l_rows, x)
    return updated, total.reshape(n, n), x_cols.reshape(-1, n), x_rows.reshape(-1, n)


def shards(rows, cols, a_trail, a_panel, l_panel, a_diag, l_inverse):
    height, block_width = a_panel.shape
    me = lax.axis_index("row") * cols + lax.axis_index("col")
    tall = min(height, block_width)
    top = jnp.concatenate((a_panel[:tall], l_panel[:tall]), axis=1)
    panel_out, first_y, next_panel, inverse, newton, panel_cols, l_rows, f_rows, l_cols = front(
        rows, cols, jnp.concatenate([top] * (block_width // tall), axis=0), tall, a_panel, l_panel,
        a_diag, l_inverse, a_trail, 0,
    )
    panel_cols, l_cols = panel_cols.reshape(-1, block_width), l_cols.reshape(-1, block_width)

    def picker(at):
        return (at[:, None] - block_width == lax.iota(jnp.int32, block_width)[None, :]).astype(
            jnp.float32
        )

    wide = a_trail.shape[1]
    refl = large_product(next_panel, inverse.T) + picker(me * height + lax.iota(jnp.int32, height))
    refl_cols = large_product(panel_cols, inverse.T) + picker(
        lax.axis_index("col") * wide + lax.iota(jnp.int32, wide)
    )
    image_shard, cross, f_cols, refl_rows = image(
        rows, cols,
        jnp.concatenate((large_product(first_y.T, refl), large_product(l_panel.T, refl)), axis=0),
        a_trail, refl_cols, first_y, refl, 2,
    )
    x_shard = product(
        image_shard - large_product(first_y, cross[block_width:])
        - large_product(l_panel, cross[:block_width]),
        newton.T,
    )
    updated, core_sum, x_cols, x_rows = update(
        rows, cols, large_product(refl.T, x_shard), a_trail, l_cols, f_cols, f_rows, l_rows, x_shard, 3
    )
    half_core = 0.5 * product(newton, core_sum)
    z_cols = x_cols - large_product(refl_cols, half_core + half_core.T)
    trail_out = updated - large_product(
        jnp.concatenate((x_rows, refl_rows), axis=1),
        jnp.concatenate((refl_cols, z_cols), axis=1).T,
    )
    return (trail_out, panel_out)


def layer(rows, cols, *args):
    return shards(rows, cols, *args)


def solution(mesh):
    rows, cols = mesh.shape["row"], mesh.shape["col"]
    return jax.shard_map(
        functools.partial(layer, rows, cols),
        mesh=mesh,
        in_specs=(P("row", "col"), P(BOTH, None), P(BOTH, None), P(), P()),
        out_specs=(P("row", "col"), P(BOTH, None)),
        check_vma=False,
    )
```
